32 devices in a mesh: tile: 8 (over z, y), acq: 4 (over x, core).
Axes of the slice: x: 2, y: 2, z: 4, core: 2. Of those that a mesh axis runs over, the one named last changes fastest.
Arguments:
- phases: float32 [64, 131072], P('acq', 'tile'), may hold values from -6 to 6
- coherence: float32 [131072], P('tile'), may hold values from 0.1 to 1
- pixel_index: int32 [131072], P('tile'), may hold values from 0 to 8191
- send_list: int32 [64, 128], P('tile'), may hold values from 0 to 16383, as said below
- counts: int32 [8, 8], P('tile'), may hold values from 16 to 128, as said below
- band_width: int32 [64], replicated, may hold values from 1 to 8
Outputs:
- residual: float32 [64, 8192], P('acq', 'tile')
- screen: float32 [64, 64, 1024], P('acq', 'tile')
The draws below stay inside these ranges and needn't reach their ends.
Inputs may be any that keep to these rules, and one draw needn't show every extreme that they name: `counts`: for every device two owner tiles (the same for all devices, possibly one) receive all 128 slots; the others receive between 16 and 63. `send_list`: the live entries of one device's rows are distinct local scatterer indices; entries beyond a row's count are valid indices that carry no data.
All inputs are finite; a program needn't handle non-finite values.
Results may differ from the reference program's by a relative error of at most 0.0003.
Values sent between devices are 32-bit elements; how exact they have to be, the bound alone decides.
No kernel may reach another device: no remote copies, remote signals or barrier semaphores. Data moves between devices by JAX's collectives and lax.ppermute only.
A program may use at most 64 MiB of HBM per device.

```python
import math
import jax
import jax.numpy as jnp
from jax import lax

ACQ = 64
SCAT_DEV = 16384
CAP = 128
COLS = 1024
RADIUS = 4
SLAB_PIX = 8192
ROWS = 64
SCAT = 131072
N_TILE = 8


def shared_plan(key):
    base = jax.random.fold_in(key, 11)
    heavy = jax.random.randint(jax.random.fold_in(base, 1), (2,), 0, N_TILE)
    loads = jax.random.randint(jax.random.fold_in(base, 2), (N_TILE, N_TILE), CAP // 8, CAP // 2)
    columns = jnp.arange(N_TILE)
    full_tile = (columns[None, :] == heavy[0]) | (columns[None, :] == heavy[1])
    loads = jnp.where(full_tile, CAP, loads).astype(jnp.int32)
    keys = jax.random.split(jax.random.fold_in(base, 3), N_TILE)
    orders = jax.vmap(lambda sub: jax.random.permutation(sub, SCAT_DEV))(keys)
    offsets = jnp.cumsum(loads, axis=1) - loads
    position = (offsets[:, :, None] + jnp.arange(CAP)[None, None, :]) % SCAT_DEV
    lists = jax.vmap(lambda order, where_at: order[where_at])(orders, position)
    return (loads, lists.reshape(N_TILE * N_TILE, CAP).astype(jnp.int32))


def draw_send_list(key, part):
    return shared_plan(key)[1]


def draw_counts(key, part):
    return shared_plan(key)[0]


def set_ends(result, rng, low, largest):
    shape = result.shape
    spot = [jax.random.randint(jax.random.fold_in(rng, axis), (), 0, shape[axis]) for axis in range(len(shape))]
    result = result.at[tuple(spot)].set(low)
    longest = shape.index(max(shape))
    spot[longest] = (spot[longest] + 1) % shape[longest]
    return result.at[tuple(spot)].set(largest)


def level_of(own_key, shape, shards, least, largest):
    factor_of, own = 1.0, jax.random.fold_in(own_key, 6)
    for dim, parts in shards:
        draws = jnp.exp(jax.random.uniform(jax.random.fold_in(own, dim), (parts,), jnp.float32, least / len(shards), largest / len(shards)))
        factor_of = factor_of * jnp.repeat(draws, shape[dim] // parts).reshape([-1 if axis == dim else 1 for axis in range(len(shape))])
    return factor_of


def normal_values(key, dims, deviation, limit, pieces=(), kind=jnp.bfloat16):
    level = level_of(key, dims, pieces, -0.22, 0.18) if pieces else 1.0
    drawn = jax.random.normal(key, dims, jnp.float32) * deviation * level
    return jnp.minimum(jnp.maximum(drawn, -limit), limit).astype(kind)


def setup_inputs(seed: int = 0) -> dict:
    streams_of = jax.random.split(jax.random.key(seed), 7)
    phases = normal_values(streams_of[0], (ACQ, SCAT), 1.0, 6.0, ((0, 4), (1, 8)), jnp.float32)
    coherence = jnp.clip(jnp.exp(math.log(1.0) - 2.3025851 * jax.random.uniform(streams_of[1], (SCAT,), jnp.float32) ** level_of(streams_of[1], (SCAT,), ((0, 8),), -0.2, 0.2)), 0.1, 1.0)
    pixel_index = set_ends(jax.random.randint(streams_of[2], (SCAT,), 0, SLAB_PIX), jax.random.fold_in(streams_of[2], 1), 0, SLAB_PIX - 1).astype(jnp.int32)
    send_list = draw_send_list(jax.random.fold_in(streams_of[6], 71), 0)
    counts = draw_counts(jax.random.fold_in(streams_of[6], 71), 0)
    band_width = set_ends(jax.random.randint(streams_of[5], (ACQ,), 1, 9), jax.random.fold_in(streams_of[5], 1), 1, 8).astype(jnp.int32)
    return {"phases": phases, "coherence": coherence, "pixel_index": pixel_index, "send_list": send_list, "counts": counts, "band_width": band_width}


min_weight = 0.1


def temporal_matrix(band_width):
    positions = jnp.arange(ACQ, dtype=jnp.int32)
    lower = jnp.maximum(positions - band_width, 0)
    upper = jnp.minimum(positions + band_width, ACQ - 1)
    inside = (positions[None, :] >= lower[:, None]) & (positions[None, :] <= upper[:, None])
    window = (upper - lower + 1).astype(jnp.float32)
    return jnp.eye(ACQ, dtype=jnp.float32) - inside.astype(jnp.float32) / window[:, None]


def kernel_weights():
    return [(RADIUS + 1 - abs(offset - RADIUS)) / float((RADIUS + 1) ** 2) for offset in range(2 * RADIUS + 1)]


def smooth(padded_rows):
    weights = kernel_weights()
    row_count = padded_rows.shape[-2] - 2 * RADIUS
    vertical = weights[0] * padded_rows[..., 0:row_count, :]
    for offset in range(1, 2 * RADIUS + 1):
        vertical = vertical + weights[offset] * padded_rows[..., offset:offset + row_count, :]
    column_count = vertical.shape[-1]
    pad_width = [(0, 0)] * (vertical.ndim - 1) + [(RADIUS, RADIUS)]
    widened = jnp.pad(vertical, pad_width)
    total = weights[0] * widened[..., 0:column_count]
    for offset in range(1, 2 * RADIUS + 1):
        total = total + weights[offset] * widened[..., offset:offset + column_count]
    return total


def reference(phases, coherence, pixel_index, send_list, counts, band_width):
    highpass = temporal_matrix(band_width)
    slot_ids = jnp.arange(CAP, dtype=jnp.int32)
    tile_ids = jnp.arange(N_TILE, dtype=jnp.int32)

    def slots_of(source):
        source = source.astype(jnp.int32)
        lists = lax.dynamic_slice_in_dim(send_list, source * N_TILE, N_TILE, 0)
        loads = lax.dynamic_slice_in_dim(counts, source, 1, 0)[0]
        live_slot = slot_ids[None, :] < loads[:, None]
        global_ids = (source * SCAT_DEV + lists).reshape(-1).astype(jnp.int32)
        targets = (tile_ids[:, None] * SLAB_PIX + pixel_index[global_ids].reshape(N_TILE, CAP)).reshape(-1)
        return global_ids, targets.astype(jnp.int32), live_slot.reshape(-1)

    def accumulate(source, carry):
        phase_sum, weight_sum = carry
        global_ids, targets, live_slot = slots_of(source)
        weights = jnp.where(live_slot, coherence[global_ids], jnp.float32(0.0))
        phase_sum = phase_sum.at[:, targets].add(phases[:, global_ids] * weights[None, :])
        weight_sum = weight_sum.at[targets].add(weights)
        return phase_sum, weight_sum

    start = (jnp.zeros((ACQ, ROWS * COLS), jnp.float32), jnp.zeros((ROWS * COLS,), jnp.float32))
    phase_sum, weight_sum = lax.fori_loop(0, N_TILE, accumulate, start)
    filtered = jnp.dot(highpass, phase_sum, precision=lax.Precision.HIGHEST, preferred_element_type=jnp.float32)
    stacked = jnp.concatenate([filtered, weight_sum[None, :]], axis=0).reshape(ACQ + 1, ROWS, COLS)
    smoothed = lax.map(lambda plane: smooth(jnp.pad(plane, ((RADIUS, RADIUS), (0, 0)))), stacked)
    screen = smoothed[:ACQ] / jnp.maximum(smoothed[ACQ], min_weight)
    flattened = screen.reshape(ACQ, ROWS * COLS)

    def residual_of(source):
        global_ids, targets, live_slot = slots_of(source)
        return jnp.where(live_slot[None, :], phases[:, global_ids] - flattened[:, targets], jnp.float32(0.0))

    residual = lax.map(residual_of, tile_ids)
    residual = jnp.transpose(residual, (1, 0, 2)).reshape(ACQ, N_TILE * N_TILE * CAP)
    return residual, screen
```

```python
import functools

import jax
import jax.numpy as jnp
from jax import lax
from jax.experimental import pallas as pl
from jax.experimental.pallas import tpu as pltpu
from jax.sharding import PartitionSpec as P

ACQ = 64
ROWS_DEV = 8
COLS = 1024
RADIUS = 4
SLAB_PIX = 8192
HALF = 64
LANES = 128


min_weight = 0.1


def with_halo(cells, sides, width):
    for axis, dim in sides:
        count = lax.axis_size(axis)
        ends = count - 1
        head = lax.slice_in_dim(cells, 0, width, axis=dim)
        tail = lax.slice_in_dim(cells, cells.shape[dim] - width, cells.shape[dim], axis=dim)
        cells = jnp.concatenate(
            [
                lax.ppermute(tail, axis, [(i, (i + 1) % count) for i in range(ends)]),
                cells,
                lax.ppermute(head, axis, [((i + 1) % count, i) for i in range(ends)]),
            ],
            axis=dim,
        )
    return cells


def temporal_matrix(band_width):
    positions = jnp.arange(ACQ, dtype=jnp.int32)
    lower = jnp.maximum(positions - band_width, 0)
    upper = jnp.minimum(positions + band_width, ACQ - 1)
    inside = (positions[None, :] >= lower[:, None]) & (positions[None, :] <= upper[:, None])
    window = (upper - lower + 1).astype(jnp.float32)
    return jnp.eye(ACQ, dtype=jnp.float32) - inside.astype(jnp.float32) / window[:, None]


def kernel_weights():
    return [
        (RADIUS + 1 - abs(offset - RADIUS)) / float((RADIUS + 1) ** 2)
        for offset in range(2 * RADIUS + 1)
    ]


def smooth(padded_rows):
    weights = kernel_weights()
    row_count = padded_rows.shape[-2] - 2 * RADIUS
    vertical = weights[0] * padded_rows[..., 0:row_count, :]
    for offset in range(1, 2 * RADIUS + 1):
        vertical = vertical + weights[offset] * padded_rows[..., offset : offset + row_count, :]
    column_count = vertical.shape[-1]
    pad_width = [(0, 0)] * (vertical.ndim - 1) + [(RADIUS, RADIUS)]
    widened = jnp.pad(vertical, pad_width)
    total = weights[0] * widened[..., 0:column_count]
    for offset in range(1, 2 * RADIUS + 1):
        total = total + weights[offset] * widened[..., offset : offset + column_count]
    return total


def apply_highpass(highpass, series):
    return jnp.dot(
        highpass, series, precision=lax.Precision.HIGHEST, preferred_element_type=jnp.float32
    )


def exchange_shards(phases, coherence, pixel_index, send_list, counts, band_width):
    acq_loc = phases.shape[0]
    capacity = send_list.shape[1]
    highpass = temporal_matrix(band_width)
    live_slot = jnp.arange(capacity, dtype=jnp.int32)[None, :] < counts[0][:, None]
    slot_weight = jnp.where(live_slot, coherence[send_list], jnp.float32(0.0))
    slot_pixel = pixel_index[send_list]
    outgoing = phases[:, send_list] * slot_weight[None]
    arrived, arrived_weight, arrived_pixel = (
        lax.all_to_all(outgoing, "tile", split_axis=1, concat_axis=1, tiled=True),
        lax.all_to_all(slot_weight[None], "tile", split_axis=1, concat_axis=1, tiled=True),
        lax.all_to_all(slot_pixel[None], "tile", split_axis=1, concat_axis=1, tiled=True),
    )
    targets = arrived_pixel.reshape(-1)
    phase_image = (
        jnp.zeros((acq_loc, SLAB_PIX), jnp.float32).at[:, targets].add(arrived.reshape(acq_loc, -1))
    )
    weight_sum = jnp.zeros((SLAB_PIX,), jnp.float32).at[targets].add(arrived_weight.reshape(-1))
    series = lax.all_to_all(phase_image, "acq", split_axis=1, concat_axis=0, tiled=True)
    phase_image = lax.all_to_all(
        apply_highpass(highpass, series), "acq", split_axis=0, concat_axis=1, tiled=True
    )
    stacked = jnp.concatenate([phase_image, weight_sum[None, :]], axis=0).reshape(
        acq_loc + 1, ROWS_DEV, COLS
    )
    padded = with_halo(stacked, (("tile", 1),), RADIUS)
    smoothed = smooth(padded)
    screen = smoothed[:acq_loc] / jnp.maximum(smoothed[acq_loc], min_weight)
    flattened = screen.reshape(acq_loc, SLAB_PIX)
    sampled = flattened[:, arrived_pixel[0]]
    returned = lax.all_to_all(sampled, "tile", split_axis=1, concat_axis=1, tiled=True)
    residual = jnp.where(live_slot[None], phases[:, send_list] - returned, jnp.float32(0.0))
    return (residual.reshape(acq_loc, -1), screen)


def heavy_tiles(counts_ref, n_tile):
    first = jnp.int32(0)
    last = jnp.int32(0)
    for t in range(n_tile):
        is_heavy = counts_ref[0, t] >= HALF
        last = jnp.where(is_heavy, t, last)
        back = n_tile - 1 - t
        first = jnp.where(counts_ref[0, back] >= HALF, back, first)
    return first, last


def split_bf16(x):
    high = x.astype(jnp.bfloat16)
    return high, (x - high.astype(jnp.float32)).astype(jnp.bfloat16)


def dot_f32(a, b, dims):
    return lax.dot_general(a, b, (dims, ((), ())), preferred_element_type=jnp.float32)


NN = ((1,), (0,))
NT = ((1,), (1,))


def packed_rows(counts_ref, list_ref, n_tile):
    first, last = heavy_tiles(counts_ref, n_tile)
    lane = lax.broadcasted_iota(jnp.int32, (1, LANES), 1)
    lower = lane < HALF
    slot = lane & (HALF - 1)
    indices, tiles, lives = [], [], []
    for p in range(n_tile // 2):
        even = list_ref[pl.ds(2 * p, 1), :]
        odd = pltpu.roll(list_ref[pl.ds(2 * p + 1, 1), :], HALF, 1)
        indices.append(jnp.where(lower, even, odd))
        tiles.append(jnp.where(lower, 2 * p, 2 * p + 1))
        lives.append(
            slot < jnp.where(lower, counts_ref[0, 2 * p], counts_ref[0, 2 * p + 1])
        )
    early = pltpu.roll(list_ref[pl.ds(first, 1), :], HALF, 1)
    late = list_ref[pl.ds(last, 1), :]
    indices.append(jnp.where(lower, early, late))
    tiles.append(jnp.where(lower, first, last))
    late_count = jnp.where(first == last, 0, counts_ref[0, last])
    lives.append(slot + HALF < jnp.where(lower, counts_ref[0, first], late_count))
    return (
        jnp.concatenate(indices, 1),
        jnp.concatenate(tiles, 1),
        jnp.concatenate([x.astype(jnp.float32) for x in lives], 1),
    )


LO = 512


def gather_kernel(n_tile, counts_ref, list_ref, phases_ref, coh_ref, pix_ref, out_ref, own_ref, wg_ref):
    acq_loc, local = phases_ref.shape
    index, tile, live = packed_rows(counts_ref, list_ref, n_tile)
    packed = index.shape[1]
    low = index & (LANES - 1)
    high = index >> 7
    chosen = lax.broadcasted_iota(jnp.int32, (LANES, packed), 0) == low
    table_rows = coh_ref.shape[0]
    coh_hi, coh_lo = split_bf16(coh_ref[...])
    pix = pix_ref[...]
    table = jnp.concatenate(
        [
            coh_hi,
            coh_lo,
            (pix >> 6).astype(jnp.float32).astype(jnp.bfloat16),
            (pix & 63).astype(jnp.float32).astype(jnp.bfloat16),
        ],
        0,
    )
    columns = dot_f32(table, chosen.astype(jnp.float32).astype(jnp.bfloat16), NN)
    row_is = lax.broadcasted_iota(jnp.int32, (table_rows, packed), 0) == high

    def pick(k):
        part = columns[k * table_rows : (k + 1) * table_rows]
        return jnp.sum(jnp.where(row_is, part, 0.0), axis=0, keepdims=True)

    weight = (pick(0) + pick(1)) * live
    pixel = pick(2) * 64.0 + pick(3) + tile.astype(jnp.float32) * float(SLAB_PIX)
    sub = lax.broadcasted_iota(jnp.int32, (8, packed), 0)
    wg_ref[...] = jnp.where(sub == 0, weight, jnp.where(sub == 1, pixel, 0.0))
    low = index & (LO - 1)
    high = index >> 9
    chosen = (lax.broadcasted_iota(jnp.int32, (LO, packed), 0) == low)
    chosen = chosen.astype(jnp.float32).astype(jnp.bfloat16)
    own = jnp.zeros((acq_loc, packed), jnp.float32)
    pieces = local // LO
    step = 8
    for start in range(0, pieces, step):
        block = jnp.concatenate(
            [phases_ref[:, h * LO : (h + 1) * LO] for h in range(start, start + step)], 0
        )
        block_hi, block_lo = split_bf16(block)
        both = dot_f32(block_hi, chosen, NN) + dot_f32(block_lo, chosen, NN)
        for h in range(step):
            own = jnp.where(high == start + h, both[h * acq_loc : (h + 1) * acq_loc], own)
    own_ref[...] = own
    out_ref[...] = own * weight


def filter_kernel(h_ref, *refs):
    *parts, wg_ref, out_ref = refs
    acq_loc = parts[0].shape[0]
    series = jnp.concatenate([part[...] for part in parts], 0)
    out_ref[0:acq_loc, :] = lax.dot_general(
        h_ref[...],
        series,
        (NN, ((), ())),
        precision=lax.Precision.HIGHEST,
        preferred_element_type=jnp.float32,
    )
    out_ref[acq_loc:, :] = wg_ref[...]


def first_pair(tile, n_pair):
    return jnp.clip((tile + 1) // 2 - 1, 0, max(n_pair - 2, 0))


def hat(distance):
    return jnp.maximum(float(RADIUS + 1) - jnp.abs(distance), 0.0)


def split_pixel(pixel):
    whole = pixel.astype(jnp.int32)
    return (whole >> 10).astype(jnp.float32), (whole & (COLS - 1)).astype(jnp.float32)


def screen_kernel(
    n_tile, me_ref, counts_ref, list_ref, all_ref, mine_ref, own_ref, screen_ref, residual_ref,
    lhs_ref, col_ref, pair_ref, res_ref,
):
    n_src, rows, packed = all_ref.shape
    acq_loc = own_ref.shape[0]
    n_pair = n_tile // 2
    width = 3 * LANES
    limit = min_weight * float((RADIUS + 1) ** 4)
    me = me_ref[0]
    first, last = heavy_tiles(counts_ref, n_tile)

    def blocks(src, pair):
        start = pl.multiple_of(pair * LANES, LANES)
        return jnp.concatenate(
            [
                all_ref[src, :, pl.ds(start, LANES)],
                all_ref[src, :, pl.ds(pl.multiple_of(start + LANES, LANES), LANES)],
                all_ref[src, :, packed - LANES :],
            ],
            1,
        )

    top = (me * ROWS_DEV).astype(jnp.float32)
    row_at = lax.broadcasted_iota(jnp.int32, (ROWS_DEV, width), 0).astype(jnp.float32) + top
    col_at = lax.broadcasted_iota(jnp.int32, (COLS, width), 0).astype(jnp.float32)
    pair = first_pair(me, n_pair)
    n_lhs = (acq_loc + 1) * ROWS_DEV
    for src in range(n_src):
        data = blocks(src, pair)
        row, col = split_pixel(data[acq_loc + 1 : acq_loc + 2])
        across = hat(row_at - row)
        lanes = pl.ds(src * width, width)
        part = jnp.concatenate([across * data[a : a + 1] for a in range(acq_loc + 1)], 0)
        part_hi, part_lo = split_bf16(part)
        lhs_ref[0:n_lhs, lanes] = part_hi
        lhs_ref[n_lhs : 2 * n_lhs, lanes] = part_lo
        col_ref[:, lanes] = hat(col_at - col).astype(jnp.bfloat16)
    for c in range(0, COLS, 256):
        image = dot_f32(lhs_ref[...], col_ref[c : c + 256, :], NT)
        image = image[0:n_lhs] + image[n_lhs:]
        below = jnp.maximum(image[acq_loc * ROWS_DEV :], limit)
        for a in range(acq_loc):
            screen_ref[a, :, c : c + 256] = image[a * ROWS_DEV : (a + 1) * ROWS_DEV] / below

    mine = mine_ref[...]
    my_row, my_col = split_pixel(mine[1:2])

    def down(row, block):
        spread = jnp.broadcast_to(row[:, block * LANES : (block + 1) * LANES], (LANES, LANES))
        return jnp.transpose(spread)

    groups = []
    for t in range(n_tile):
        p = min(max((t + 1) // 2 - 1, 0), max(n_pair - 2, 0))
        if groups and groups[-1][2] == p:
            groups[-1][1] += HALF
        else:
            groups.append([t * HALF, HALF, p])
    base = n_pair * LANES
    groups.append([base, HALF, first_pair(first, n_pair)])
    groups.append([base + HALF, HALF, first_pair(last, n_pair)])
    rows_down = jnp.concatenate([down(my_row, b) for b in range(n_pair + 1)], 0)
    cols_down = jnp.concatenate([down(my_col, b) for b in range(n_pair + 1)], 0)
    samples = []
    for start, size, p in groups:
        r_i = rows_down[start : start + size]
        c_i = cols_down[start : start + size]
        values = []
        for src in range(n_src):
            data = blocks(src, p)
            row, col = split_pixel(data[acq_loc + 1 : acq_loc + 2])
            value_hi, value_lo = split_bf16(data[0 : acq_loc + 8])
            values.append(jnp.concatenate([value_hi, value_lo], 0))
            for b in range(3):
                cut = slice(b * LANES, (b + 1) * LANES)
                both = hat(r_i - row[:, cut]) * hat(c_i - col[:, cut])
                pair_ref[0:size, src * width + b * LANES : src * width + (b + 1) * LANES] = (
                    both.astype(jnp.bfloat16)
                )
        value = jnp.concatenate(values, 1)
        got = dot_f32(value, pair_ref[0:size, :], NT)
        got = got[0 : acq_loc + 8] + got[acq_loc + 8 :]
        samples.append(got[0:acq_loc] / jnp.maximum(got[acq_loc : acq_loc + 1], limit))
    res_ref[...] = own_ref[...] - jnp.concatenate(samples, 1)

    lane = lax.broadcasted_iota(jnp.int32, (1, LANES), 1)
    lower = lane < HALF
    heavy = res_ref[:, base:]
    turned = pltpu.roll(heavy, HALF, 1)
    for t in range(n_tile):
        near = res_ref[:, (t // 2) * LANES : (t // 2 + 1) * LANES]
        if t % 2:
            near = pltpu.roll(near, HALF, 1)
        far = jnp.where(first == t, turned, heavy)
        both = jnp.where(lower, near, far)
        residual_ref[:, t * LANES : (t + 1) * LANES] = jnp.where(
            lane < counts_ref[0, t], both, 0.0
        )


def xor_permute(x, axis, mask):
    count = lax.axis_size(axis)
    return lax.ppermute(x, axis, [(i, i ^ mask) for i in range(count)])


def gathered_shards(phases, coherence, pixel_index, send_list, counts, band_width):
    acq_loc, local = phases.shape
    n_tile = lax.axis_size("tile")
    n_acq = lax.axis_size("acq")
    packed = (n_tile // 2 + 1) * LANES
    smem = pl.BlockSpec(memory_space=pltpu.SMEM)
    vmem = pl.BlockSpec(memory_space=pltpu.VMEM)
    f32 = jnp.float32
    outgoing, own, wg = pl.pallas_call(
        functools.partial(gather_kernel, n_tile),
        out_shape=(
            jax.ShapeDtypeStruct((acq_loc, packed), f32),
            jax.ShapeDtypeStruct((acq_loc, packed), f32),
            jax.ShapeDtypeStruct((8, packed), f32),
        ),
        in_specs=[smem, vmem, vmem, vmem, vmem],
        out_specs=(vmem, vmem, vmem),
        name="gather_slots",
    )(
        counts,
        send_list,
        phases,
        coherence.reshape(-1, LANES),
        pixel_index.reshape(-1, LANES),
    )
    here = lax.axis_index("acq")
    parts = [outgoing] + [xor_permute(outgoing, "acq", k) for k in range(1, n_acq)]
    source = here ^ jnp.arange(n_acq, dtype=jnp.int32)
    column = (source[:, None] * acq_loc + jnp.arange(acq_loc, dtype=jnp.int32)[None]).reshape(1, -1)
    row = here * acq_loc + jnp.arange(acq_loc, dtype=jnp.int32)
    band = lax.dynamic_slice_in_dim(band_width, here * acq_loc, acq_loc)
    lower = jnp.maximum(row - band, 0)[:, None]
    upper = jnp.minimum(row + band, ACQ - 1)[:, None]
    inside = ((column >= lower) & (column <= upper)).astype(f32)
    highpass = (column == row[:, None]).astype(f32) - inside / (upper - lower + 1).astype(f32)
    filtered = pl.pallas_call(
        filter_kernel,
        out_shape=jax.ShapeDtypeStruct((acq_loc + 8, packed), f32),
        in_specs=[vmem] * (n_acq + 2),
        out_specs=vmem,
        name="filter_slots",
    )(highpass, *parts, wg)
    held = filtered[None]
    half = n_tile // 2
    if half > 1:
        held = jnp.concatenate([held, xor_permute(held, "tile", half)], 0)
        held = jnp.concatenate([held] + [xor_permute(held, "tile", k) for k in range(1, half)], 0)
    else:
        held = jnp.concatenate([held, xor_permute(held, "tile", 1)], 0)
    me = lax.axis_index("tile").astype(jnp.int32).reshape(1)
    n_src = n_tile
    n_lhs = 2 * (acq_loc + 1) * ROWS_DEV
    width = n_src * 3 * LANES
    screen, residual = pl.pallas_call(
        functools.partial(screen_kernel, n_tile),
        out_shape=(
            jax.ShapeDtypeStruct((acq_loc, ROWS_DEV, COLS), f32),
            jax.ShapeDtypeStruct((acq_loc, n_tile * LANES), f32),
        ),
        in_specs=[smem, smem, vmem, vmem, vmem, vmem],
        out_specs=(vmem, vmem),
        scratch_shapes=[
            pltpu.VMEM((n_lhs, width), jnp.bfloat16),
            pltpu.VMEM((COLS, width), jnp.bfloat16),
            pltpu.VMEM((3 * HALF, width), jnp.bfloat16),
            pltpu.VMEM((acq_loc, packed), f32),
        ],
        compiler_params=pltpu.CompilerParams(vmem_limit_bytes=48 << 20),
        name="screen_and_residual",
    )(me, counts, send_list, held, wg, own)
    return residual, screen


def solution(mesh):
    n_tile = mesh.shape["tile"]
    few = n_tile in (4, 8)
    return jax.shard_map(
        gathered_shards if few else exchange_shards,
        mesh=mesh,
        in_specs=(P("acq", "tile"), P("tile"), P("tile"), P("tile", None), P("tile", None), P()),
        out_specs=(P("acq", "tile"), P("acq", "tile", None)),
        check_vma=False,
    )
```

```python
import functools

import jax
import jax.numpy as jnp
from jax import lax
from jax.experimental import pallas as pl
from jax.experimental.pallas import tpu as pltpu
from jax.sharding import PartitionSpec as P

ACQ = 64
ROWS_DEV = 8
COLS = 1024
RADIUS = 4
SLAB_PIX = 8192
HALF = 64
LANES = 128


min_weight = 0.1


def with_halo(cells, sides, width):
    for axis, dim in sides:
        count = lax.axis_size(axis)
        ends = count - 1
        head = lax.slice_in_dim(cells, 0, width, axis=dim)
        tail = lax.slice_in_dim(cells, cells.shape[dim] - width, cells.shape[dim], axis=dim)
        cells = jnp.concatenate(
            [
                lax.ppermute(tail, axis, [(i, (i + 1) % count) for i in range(ends)]),
                cells,
                lax.ppermute(head, axis, [((i + 1) % count, i) for i in range(ends)]),
            ],
            axis=dim,
        )
    return cells


def temporal_matrix(band_width):
    positions = jnp.arange(ACQ, dtype=jnp.int32)
    lower = jnp.maximum(positions - band_width, 0)
    upper = jnp.minimum(positions + band_width, ACQ - 1)
    inside = (positions[None, :] >= lower[:, None]) & (positions[None, :] <= upper[:, None])
    window = (upper - lower + 1).astype(jnp.float32)
    return jnp.eye(ACQ, dtype=jnp.float32) - inside.astype(jnp.float32) / window[:, None]


def kernel_weights():
    return [
        (RADIUS + 1 - abs(offset - RADIUS)) / float((RADIUS + 1) ** 2)
        for offset in range(2 * RADIUS + 1)
    ]


def smooth(padded_rows):
    weights = kernel_weights()
    row_count = padded_rows.shape[-2] - 2 * RADIUS
    vertical = weights[0] * padded_rows[..., 0:row_count, :]
    for offset in range(1, 2 * RADIUS + 1):
        vertical = vertical + weights[offset] * padded_rows[..., offset : offset + row_count, :]
    column_count = vertical.shape[-1]
    pad_width = [(0, 0)] * (vertical.ndim - 1) + [(RADIUS, RADIUS)]
    widened = jnp.pad(vertical, pad_width)
    total = weights[0] * widened[..., 0:column_count]
    for offset in range(1, 2 * RADIUS + 1):
        total = total + weights[offset] * widened[..., offset : offset + column_count]
    return total


def apply_highpass(highpass, series):
    return jnp.dot(
        highpass, series, precision=lax.Precision.HIGHEST, preferred_element_type=jnp.float32
    )


def exchange_shards(phases, coherence, pixel_index, send_list, counts, band_width):
    acq_loc = phases.shape[0]
    capacity = send_list.shape[1]
    highpass = temporal_matrix(band_width)
    live_slot = jnp.arange(capacity, dtype=jnp.int32)[None, :] < counts[0][:, None]
    slot_weight = jnp.where(live_slot, coherence[send_list], jnp.float32(0.0))
    slot_pixel = pixel_index[send_list]
    outgoing = phases[:, send_list] * slot_weight[None]
    arrived, arrived_weight, arrived_pixel = (
        lax.all_to_all(outgoing, "tile", split_axis=1, concat_axis=1, tiled=True),
        lax.all_to_all(slot_weight[None], "tile", split_axis=1, concat_axis=1, tiled=True),
        lax.all_to_all(slot_pixel[None], "tile", split_axis=1, concat_axis=1, tiled=True),
    )
    targets = arrived_pixel.reshape(-1)
    phase_image = (
        jnp.zeros((acq_loc, SLAB_PIX), jnp.float32).at[:, targets].add(arrived.reshape(acq_loc, -1))
    )
    weight_sum = jnp.zeros((SLAB_PIX,), jnp.float32).at[targets].add(arrived_weight.reshape(-1))
    series = lax.all_to_all(phase_image, "acq", split_axis=1, concat_axis=0, tiled=True)
    phase_image = lax.all_to_all(
        apply_highpass(highpass, series), "acq", split_axis=0, concat_axis=1, tiled=True
    )
    stacked = jnp.concatenate([phase_image, weight_sum[None, :]], axis=0).reshape(
        acq_loc + 1, ROWS_DEV, COLS
    )
    padded = with_halo(stacked, (("tile", 1),), RADIUS)
    smoothed = smooth(padded)
    screen = smoothed[:acq_loc] / jnp.maximum(smoothed[acq_loc], min_weight)
    flattened = screen.reshape(acq_loc, SLAB_PIX)
    sampled = flattened[:, arrived_pixel[0]]
    returned = lax.all_to_all(sampled, "tile", split_axis=1, concat_axis=1, tiled=True)
    residual = jnp.where(live_slot[None], phases[:, send_list] - returned, jnp.float32(0.0))
    return (residual.reshape(acq_loc, -1), screen)


def heavy_tiles(counts_ref, n_tile):
    first = jnp.int32(0)
    last = jnp.int32(0)
    for t in range(n_tile):
        is_heavy = counts_ref[0, t] >= HALF
        last = jnp.where(is_heavy, t, last)
        back = n_tile - 1 - t
        first = jnp.where(counts_ref[0, back] >= HALF, back, first)
    return first, last


def split_bf16(x):
    high = x.astype(jnp.bfloat16)
    return high, (x - high.astype(jnp.float32)).astype(jnp.bfloat16)


def dot_f32(a, b, dims):
    return lax.dot_general(a, b, (dims, ((), ())), preferred_element_type=jnp.float32)


NN = ((1,), (0,))
NT = ((1,), (1,))


def packed_rows(counts_ref, list_ref, n_tile):
    first, last = heavy_tiles(counts_ref, n_tile)
    lane = lax.broadcasted_iota(jnp.int32, (1, LANES), 1)
    lower = lane < HALF
    slot = lane & (HALF - 1)
    indices, tiles, lives = [], [], []
    for p in range(n_tile // 2):
        even = list_ref[pl.ds(2 * p, 1), :]
        odd = pltpu.roll(list_ref[pl.ds(2 * p + 1, 1), :], HALF, 1)
        indices.append(jnp.where(lower, even, odd))
        tiles.append(jnp.where(lower, 2 * p, 2 * p + 1))
        lives.append(
            slot < jnp.where(lower, counts_ref[0, 2 * p], counts_ref[0, 2 * p + 1])
        )
    early = pltpu.roll(list_ref[pl.ds(first, 1), :], HALF, 1)
    late = list_ref[pl.ds(last, 1), :]
    indices.append(jnp.where(lower, early, late))
    tiles.append(jnp.where(lower, first, last))
    late_count = jnp.where(first == last, 0, counts_ref[0, last])
    lives.append(slot + HALF < jnp.where(lower, counts_ref[0, first], late_count))
    return (
        jnp.concatenate(indices, 1),
        jnp.concatenate(tiles, 1),
        jnp.concatenate([x.astype(jnp.float32) for x in lives], 1),
    )


MAX_BLOCKS = 8
LO = 512
STEP = 8


def gather_kernel(n_tile, counts_ref, list_ref, phases_ref, coh_ref, pix_ref, out_ref, own_ref, wg_ref):
    acq_loc, local = phases_ref.shape
    pieces = local // LO
    step = min(STEP, pieces)
    index, tile, live = packed_rows(counts_ref, list_ref, n_tile)
    packed = index.shape[1]
    low = index & (LANES - 1)
    high = index >> 7
    chosen = lax.broadcasted_iota(jnp.int32, (LANES, packed), 0) == low
    table_rows = coh_ref.shape[0]
    coh_hi, coh_lo = split_bf16(coh_ref[...])
    pix = pix_ref[...]
    table = jnp.concatenate(
        [
            coh_hi,
            coh_lo,
            (pix >> 6).astype(jnp.float32).astype(jnp.bfloat16),
            (pix & 63).astype(jnp.float32).astype(jnp.bfloat16),
        ],
        0,
    )
    columns = dot_f32(table, chosen.astype(jnp.float32).astype(jnp.bfloat16), NN)
    row_is = lax.broadcasted_iota(jnp.int32, (table_rows, packed), 0) == high

    def pick(k):
        part = columns[k * table_rows : (k + 1) * table_rows]
        return jnp.sum(jnp.where(row_is, part, 0.0), axis=0, keepdims=True)

    weight = (pick(0) + pick(1)) * live
    pixel = pick(2) * 64.0 + pick(3) + tile.astype(jnp.float32) * float(SLAB_PIX)
    for b in range(packed // LANES):
        cut = slice(b * LANES, (b + 1) * LANES)
        wg_ref[b : b + 1, :] = weight[:, cut]
        wg_ref[MAX_BLOCKS + b : MAX_BLOCKS + b + 1, :] = pixel[:, cut]
    low = index & (LO - 1)
    high = index >> 9
    chosen = (lax.broadcasted_iota(jnp.int32, (LO, packed), 0) == low)
    chosen = chosen.astype(jnp.float32).astype(jnp.bfloat16)
    own = jnp.zeros((acq_loc, packed), jnp.float32)
    for start in range(0, pieces, step):
        block = jnp.concatenate(
            [phases_ref[:, h * LO : (h + 1) * LO] for h in range(start, start + step)], 0
        )
        block_hi, block_lo = split_bf16(block)
        both = dot_f32(block_hi, chosen, NN) + dot_f32(block_lo, chosen, NN)
        for h in range(step):
            own = jnp.where(high == start + h, both[h * acq_loc : (h + 1) * acq_loc], own)
    own_ref[...] = own
    out_ref[...] = own * weight


def filter_kernel(h_ref, *refs):
    *parts, wg_ref, out_ref = refs
    packed = parts[0].shape[1]
    series = jnp.concatenate([part[...] for part in parts], 0)
    out_ref[:, 0:packed] = lax.dot_general(
        h_ref[...],
        series,
        (NN, ((), ())),
        precision=lax.Precision.HIGHEST,
        preferred_element_type=jnp.float32,
    )
    out_ref[:, packed:] = wg_ref[...]


def first_pair(tile, n_pair):
    return jnp.clip((tile + 1) // 2 - 1, 0, max(n_pair - 2, 0))


def hat(distance):
    return jnp.maximum(float(RADIUS + 1) - jnp.abs(distance), 0.0)


def hat_bf16(distance):
    return jnp.maximum(jnp.bfloat16(RADIUS + 1) - jnp.abs(distance), jnp.bfloat16(0))


def split_pixel(pixel):
    whole = pixel.astype(jnp.int32)
    return (whole >> 10).astype(jnp.float32), (whole & (COLS - 1)).astype(jnp.float32)


def rows_of_bf16(row, count):
    few = jnp.broadcast_to(row, (16, row.shape[1])).astype(jnp.bfloat16)
    return jnp.concatenate([few] * (count // 16), 0)


CHUNK = 256


def slot_groups(n_tile, counts_ref):
    n_pair = n_tile // 2
    first, last = heavy_tiles(counts_ref, n_tile)
    groups = []
    for t in range(n_tile):
        p = min(max((t + 1) // 2 - 1, 0), max(n_pair - 2, 0))
        if groups and groups[-1][2] == p:
            groups[-1][1] += HALF
        else:
            groups.append([t * HALF, HALF, p])
    base = n_pair * LANES
    groups.append([base, HALF, first_pair(first, n_pair)])
    groups.append([base + HALF, HALF, first_pair(last, n_pair)])
    return groups


def screen_kernel(n_tile, begins, ends, *refs):
    me_ref, counts_ref, all_ref, mine_ref = refs[:4]
    refs = refs[4:]
    if not begins:
        image_in, samples_in = refs[:2]
        refs = refs[2:]
    if ends:
        own_ref, screen_ref, residual_ref = refs[:3]
        refs = refs[3:]
    else:
        image_out, samples_out = refs[:2]
        refs = refs[2:]
    tag_ref, value_ref, lhs_ref, col_ref, pair_ref, res_ref = refs
    n_src, acq_loc, packed = all_ref.shape
    packed -= LANES
    n_pair = n_tile // 2
    width = 3 * LANES
    limit = min_weight * float((RADIUS + 1) ** 4)
    me = me_ref[0]
    f32, bf16 = jnp.float32, jnp.bfloat16

    def starts(pair):
        start = pl.multiple_of(pair * LANES, LANES)
        return [start, pl.multiple_of(start + LANES, LANES), n_pair * LANES]

    def tags(src, pair):
        blocks = [tag_ref[src, 0:3, pl.ds(s, LANES)] for s in starts(pair)]
        every = jnp.concatenate(blocks, 1)
        return every[0:1], every[1:2], every[2:3]

    sub = lax.broadcasted_iota(jnp.int32, (16, LANES), 0)
    for src in range(n_src):
        value_hi, value_lo = split_bf16(all_ref[src, :, 0:packed])
        value_ref[src, 0:acq_loc, :] = value_hi
        value_ref[src, acq_loc : 2 * acq_loc, :] = value_lo
        for b in range(n_pair + 1):
            lanes = slice(b * LANES, (b + 1) * LANES)
            row, col = split_pixel(all_ref[src, MAX_BLOCKS + b : MAX_BLOCKS + b + 1, packed:])
            weight = all_ref[src, b : b + 1, packed:]
            tag_ref[src, 0:1, lanes] = weight
            tag_ref[src, 1:2, lanes] = row
            tag_ref[src, 2:3, lanes] = col
            w_hi = weight.astype(bf16).astype(f32)
            both = jnp.where(sub == 0, w_hi, jnp.where(sub == 1, weight - w_hi, 0.0))
            value_ref[src, 2 * acq_loc :, lanes] = both.astype(bf16)

    top = (me * ROWS_DEV).astype(f32)
    row_at = lax.broadcasted_iota(jnp.int32, (ROWS_DEV, width), 0).astype(f32) + top
    col_at = lax.broadcasted_iota(jnp.int32, (CHUNK, width), 0) - CHUNK // 2
    col_at = col_at.astype(f32).astype(bf16)
    pair = first_pair(me, n_pair)
    n_img = acq_loc * ROWS_DEV
    for src in range(n_src):
        weight, row, col = tags(src, pair)
        across = hat(row_at - row)
        lanes = slice(src * width, (src + 1) * width)
        data = jnp.concatenate([all_ref[src, :, pl.ds(s, LANES)] for s in starts(pair)], 1)
        part = jnp.concatenate([across * data[a : a + 1] for a in range(acq_loc)], 0)
        part_hi, part_lo = split_bf16(part)
        lhs_ref[0:n_img, lanes] = part_hi
        lhs_ref[n_img : 2 * n_img, lanes] = part_lo
        w_part = across * weight
        w_hi = w_part.astype(bf16).astype(f32)
        lhs_ref[2 * n_img :, lanes] = jnp.concatenate([w_hi, w_part - w_hi], 0).astype(bf16)
        for c in range(0, COLS, CHUNK):
            near = jnp.clip(col - float(c + CHUNK // 2), -160.0, 160.0)
            col_ref[c : c + CHUNK, lanes] = hat_bf16(col_at - rows_of_bf16(near, CHUNK))

    def down_lanes(row):
        return jnp.transpose(jnp.broadcast_to(row, (LANES, LANES)))

    mine = [split_pixel(mine_ref[MAX_BLOCKS + b : MAX_BLOCKS + b + 1, :]) for b in range(n_pair + 1)]
    rows_down = jnp.concatenate([down_lanes(r) for r, _ in mine], 0).astype(bf16)
    cols_down = jnp.concatenate([down_lanes(c) for _, c in mine], 0)

    def sample(start, size, p):
        r_i = rows_down[start : start + size]
        c_i = cols_down[start : start + size]
        values = []
        for src in range(n_src):
            _, row, col = tags(src, p)
            for b, s in enumerate(starts(p)):
                cut = slice(b * LANES, (b + 1) * LANES)
                values.append(value_ref[src, :, pl.ds(s, LANES)])
                over = hat_bf16(r_i - rows_of_bf16(row[:, cut], size))
                both = over * hat_bf16((c_i - col[:, cut]).astype(bf16))
                at = src * width + b * LANES
                pair_ref[start : start + size, at : at + LANES] = both
        got = dot_f32(jnp.concatenate(values, 1), pair_ref[start : start + size, :], NT)
        total = got[0:acq_loc] + got[acq_loc : 2 * acq_loc]
        below = got[2 * acq_loc : 2 * acq_loc + 8]
        return jnp.concatenate([total, below], 0)

    def slab(c):
        got = dot_f32(lhs_ref[...], col_ref[c : c + CHUNK, :], NT)
        return jnp.concatenate(
            [
                got[0:n_img] + got[n_img : 2 * n_img],
                got[2 * n_img : 2 * n_img + ROWS_DEV] + got[2 * n_img + ROWS_DEV :],
            ],
            0,
        )

    for c in range(0, COLS, CHUNK):
        image = slab(c)
        if not begins:
            image = image + image_in[:, c : c + CHUNK]
        if not ends:
            image_out[:, c : c + CHUNK] = image
            continue
        below = jnp.maximum(image[n_img:], limit)
        for a in range(acq_loc):
            screen_ref[a, :, c : c + CHUNK] = image[a * ROWS_DEV : (a + 1) * ROWS_DEV] / below
    samples = jnp.concatenate([sample(*group) for group in slot_groups(n_tile, counts_ref)], 1)
    if not begins:
        samples = samples + samples_in[...]
    if not ends:
        samples_out[...] = samples
        return
    below = samples[acq_loc : acq_loc + 1] + samples[acq_loc + 1 : acq_loc + 2]
    res_ref[...] = own_ref[...] - samples[0:acq_loc] / jnp.maximum(below, limit)

    first, _ = heavy_tiles(counts_ref, n_tile)
    lane = lax.broadcasted_iota(jnp.int32, (1, LANES), 1)
    lower = lane < HALF
    heavy = res_ref[:, n_pair * LANES :]
    turned = pltpu.roll(heavy, HALF, 1)
    for t in range(n_tile):
        near = res_ref[:, (t // 2) * LANES : (t // 2 + 1) * LANES]
        if t % 2:
            near = pltpu.roll(near, HALF, 1)
        far = jnp.where(first == t, turned, heavy)
        both = jnp.where(lower, near, far)
        residual_ref[:, t * LANES : (t + 1) * LANES] = jnp.where(
            lane < counts_ref[0, t], both, 0.0
        )


def add_sources(n_tile, me, counts, sources, mine, sums, own):
    n_src, acq_loc, packed = sources.shape
    packed -= LANES
    width = n_src * 3 * LANES
    f32, bf16 = jnp.float32, jnp.bfloat16
    smem = pl.BlockSpec(memory_space=pltpu.SMEM)
    vmem = pl.BlockSpec(memory_space=pltpu.VMEM)
    n_lhs = 2 * (acq_loc + 1) * ROWS_DEV
    begins, ends = sums is None, own is not None
    args = [me, counts, sources, mine]
    if not begins:
        args += list(sums)
    if ends:
        args.append(own)
        shapes = ((acq_loc, ROWS_DEV, COLS), (acq_loc, n_tile * LANES))
    else:
        shapes = ((n_lhs // 2, COLS), (acq_loc + 8, packed))
    macs = width * (n_lhs * COLS + (2 * acq_loc + 16) * packed)
    return pl.pallas_call(
        functools.partial(screen_kernel, n_tile, begins, ends),
        out_shape=tuple(jax.ShapeDtypeStruct(shape, f32) for shape in shapes),
        in_specs=[smem, smem] + [vmem] * (len(args) - 2),
        out_specs=(vmem, vmem),
        scratch_shapes=[
            pltpu.VMEM((n_src, 8, packed), f32),
            pltpu.VMEM((n_src, 2 * acq_loc + 16, packed), bf16),
            pltpu.VMEM((n_lhs, width), bf16),
            pltpu.VMEM((COLS, width), bf16),
            pltpu.VMEM((packed, width), bf16),
            pltpu.VMEM((acq_loc, packed), f32),
        ],
        input_output_aliases={} if begins or ends else {4: 0, 5: 1},
        cost_estimate=pl.CostEstimate(flops=2 * macs, bytes_accessed=1 << 20, transcendentals=0),
        compiler_params=pltpu.CompilerParams(vmem_limit_bytes=SCREEN_VMEM),
        name="add_sources",
    )(*args)


SCREEN_VMEM = 24 << 20


def xor_permute(x, axis, mask):
    count = lax.axis_size(axis)
    return lax.ppermute(x, axis, [(i, i ^ mask) for i in range(count)])


def gathered_shards(phases, coherence, pixel_index, send_list, counts, band_width):
    acq_loc, local = phases.shape
    n_tile = lax.axis_size("tile")
    n_acq = lax.axis_size("acq")
    packed = (n_tile // 2 + 1) * LANES
    smem = pl.BlockSpec(memory_space=pltpu.SMEM)
    vmem = pl.BlockSpec(memory_space=pltpu.VMEM)
    f32 = jnp.float32
    outgoing, own, wg = pl.pallas_call(
        functools.partial(gather_kernel, n_tile),
        out_shape=(
            jax.ShapeDtypeStruct((acq_loc, packed), f32),
            jax.ShapeDtypeStruct((acq_loc, packed), f32),
            jax.ShapeDtypeStruct((2 * MAX_BLOCKS, LANES), f32),
        ),
        in_specs=[smem, vmem, vmem, vmem, vmem],
        out_specs=(vmem, vmem, vmem),
        compiler_params=pltpu.CompilerParams(vmem_limit_bytes=56 << 20),
        name="gather_slots",
    )(
        counts,
        send_list,
        phases,
        coherence.reshape(-1, LANES),
        pixel_index.reshape(-1, LANES),
    )
    here = lax.axis_index("acq")
    parts = [outgoing] + [xor_permute(outgoing, "acq", k) for k in range(1, n_acq)]
    source = here ^ jnp.arange(n_acq, dtype=jnp.int32)
    column = (source[:, None] * acq_loc + jnp.arange(acq_loc, dtype=jnp.int32)[None]).reshape(1, -1)
    row = here * acq_loc + jnp.arange(acq_loc, dtype=jnp.int32)
    band = lax.dynamic_slice_in_dim(band_width, here * acq_loc, acq_loc)
    lower = jnp.maximum(row - band, 0)[:, None]
    upper = jnp.minimum(row + band, ACQ - 1)[:, None]
    inside = ((column >= lower) & (column <= upper)).astype(f32)
    highpass = (column == row[:, None]).astype(f32) - inside / (upper - lower + 1).astype(f32)
    filtered = pl.pallas_call(
        filter_kernel,
        out_shape=jax.ShapeDtypeStruct((acq_loc, packed + LANES), f32),
        in_specs=[vmem] * (n_acq + 2),
        out_specs=vmem,
        compiler_params=pltpu.CompilerParams(vmem_limit_bytes=4 << 20),
        name="filter_slots",
    )(highpass, *parts, wg)
    me = lax.axis_index("tile").astype(jnp.int32).reshape(1)
    half = n_tile // 2
    held = jnp.stack([filtered, xor_permute(filtered, "tile", half)])
    others = [xor_permute(held, "tile", k) for k in range(1, half)]
    sums = None
    for sources in [held] + others[:-1]:
        sums = add_sources(n_tile, me, counts, sources, wg, sums, None)
    screen, residual = add_sources(n_tile, me, counts, others[-1], wg, sums, own)
    return residual, screen


def solution(mesh):
    n_tile = mesh.shape["tile"]
    few = n_tile in (4, 8)
    return jax.shard_map(
        gathered_shards if few else exchange_shards,
        mesh=mesh,
        in_specs=(P("acq", "tile"), P("tile"), P("tile"), P("tile", None), P("tile", None), P()),
        out_specs=(P("acq", "tile"), P("acq", "tile", None)),
        check_vma=False,
    )
```

```python
import functools

import jax
import jax.numpy as jnp
from jax import lax
from jax.experimental import pallas as pl
from jax.experimental.pallas import tpu as pltpu
from jax.sharding import PartitionSpec as P

ACQ = 64
ROWS_DEV = 8
COLS = 1024
RADIUS = 4
SLAB_PIX = 8192
HALF = 64
LANES = 128


min_weight = 0.1


def with_halo(cells, sides, width):
    for axis, dim in sides:
        count = lax.axis_size(axis)
        ends = count - 1
        head = lax.slice_in_dim(cells, 0, width, axis=dim)
        tail = lax.slice_in_dim(cells, cells.shape[dim] - width, cells.shape[dim], axis=dim)
        cells = jnp.concatenate(
            [
                lax.ppermute(tail, axis, [(i, (i + 1) % count) for i in range(ends)]),
                cells,
                lax.ppermute(head, axis, [((i + 1) % count, i) for i in range(ends)]),
            ],
            axis=dim,
        )
    return cells


def temporal_matrix(band_width):
    positions = jnp.arange(ACQ, dtype=jnp.int32)
    lower = jnp.maximum(positions - band_width, 0)
    upper = jnp.minimum(positions + band_width, ACQ - 1)
    inside = (positions[None, :] >= lower[:, None]) & (positions[None, :] <= upper[:, None])
    window = (upper - lower + 1).astype(jnp.float32)
    return jnp.eye(ACQ, dtype=jnp.float32) - inside.astype(jnp.float32) / window[:, None]


def kernel_weights():
    return [
        (RADIUS + 1 - abs(offset - RADIUS)) / float((RADIUS + 1) ** 2)
        for offset in range(2 * RADIUS + 1)
    ]


def smooth(padded_rows):
    weights = kernel_weights()
    row_count = padded_rows.shape[-2] - 2 * RADIUS
    vertical = weights[0] * padded_rows[..., 0:row_count, :]
    for offset in range(1, 2 * RADIUS + 1):
        vertical = vertical + weights[offset] * padded_rows[..., offset : offset + row_count, :]
    column_count = vertical.shape[-1]
    pad_width = [(0, 0)] * (vertical.ndim - 1) + [(RADIUS, RADIUS)]
    widened = jnp.pad(vertical, pad_width)
    total = weights[0] * widened[..., 0:column_count]
    for offset in range(1, 2 * RADIUS + 1):
        total = total + weights[offset] * widened[..., offset : offset + column_count]
    return total


def apply_highpass(highpass, series):
    return jnp.dot(
        highpass, series, precision=lax.Precision.HIGHEST, preferred_element_type=jnp.float32
    )


def exchange_shards(phases, coherence, pixel_index, send_list, counts, band_width):
    acq_loc = phases.shape[0]
    capacity = send_list.shape[1]
    highpass = temporal_matrix(band_width)
    live_slot = jnp.arange(capacity, dtype=jnp.int32)[None, :] < counts[0][:, None]
    slot_weight = jnp.where(live_slot, coherence[send_list], jnp.float32(0.0))
    slot_pixel = pixel_index[send_list]
    outgoing = phases[:, send_list] * slot_weight[None]
    arrived, arrived_weight, arrived_pixel = (
        lax.all_to_all(outgoing, "tile", split_axis=1, concat_axis=1, tiled=True),
        lax.all_to_all(slot_weight[None], "tile", split_axis=1, concat_axis=1, tiled=True),
        lax.all_to_all(slot_pixel[None], "tile", split_axis=1, concat_axis=1, tiled=True),
    )
    targets = arrived_pixel.reshape(-1)
    phase_image = (
        jnp.zeros((acq_loc, SLAB_PIX), jnp.float32).at[:, targets].add(arrived.reshape(acq_loc, -1))
    )
    weight_sum = jnp.zeros((SLAB_PIX,), jnp.float32).at[targets].add(arrived_weight.reshape(-1))
    series = lax.all_to_all(phase_image, "acq", split_axis=1, concat_axis=0, tiled=True)
    phase_image = lax.all_to_all(
        apply_highpass(highpass, series), "acq", split_axis=0, concat_axis=1, tiled=True
    )
    stacked = jnp.concatenate([phase_image, weight_sum[None, :]], axis=0).reshape(
        acq_loc + 1, ROWS_DEV, COLS
    )
    padded = with_halo(stacked, (("tile", 1),), RADIUS)
    smoothed = smooth(padded)
    screen = smoothed[:acq_loc] / jnp.maximum(smoothed[acq_loc], min_weight)
    flattened = screen.reshape(acq_loc, SLAB_PIX)
    sampled = flattened[:, arrived_pixel[0]]
    returned = lax.all_to_all(sampled, "tile", split_axis=1, concat_axis=1, tiled=True)
    residual = jnp.where(live_slot[None], phases[:, send_list] - returned, jnp.float32(0.0))
    return (residual.reshape(acq_loc, -1), screen)


def heavy_tiles(counts_ref, n_tile):
    first = jnp.int32(0)
    last = jnp.int32(0)
    for t in range(n_tile):
        is_heavy = counts_ref[0, t] >= HALF
        last = jnp.where(is_heavy, t, last)
        back = n_tile - 1 - t
        first = jnp.where(counts_ref[0, back] >= HALF, back, first)
    return first, last


def split_bf16(x):
    high = x.astype(jnp.bfloat16)
    return high, (x - high.astype(jnp.float32)).astype(jnp.bfloat16)


def dot_f32(a, b, dims):
    return lax.dot_general(a, b, (dims, ((), ())), preferred_element_type=jnp.float32)


NN = ((1,), (0,))
NT = ((1,), (1,))


def packed_rows(counts_ref, list_ref, n_tile):
    first, last = heavy_tiles(counts_ref, n_tile)
    lane = lax.broadcasted_iota(jnp.int32, (1, LANES), 1)
    lower = lane < HALF
    slot = lane & (HALF - 1)
    indices, tiles, lives = [], [], []
    for p in range(n_tile // 2):
        even = list_ref[pl.ds(2 * p, 1), :]
        odd = pltpu.roll(list_ref[pl.ds(2 * p + 1, 1), :], HALF, 1)
        indices.append(jnp.where(lower, even, odd))
        tiles.append(jnp.where(lower, 2 * p, 2 * p + 1))
        lives.append(
            slot < jnp.where(lower, counts_ref[0, 2 * p], counts_ref[0, 2 * p + 1])
        )
    early = pltpu.roll(list_ref[pl.ds(first, 1), :], HALF, 1)
    late = list_ref[pl.ds(last, 1), :]
    indices.append(jnp.where(lower, early, late))
    tiles.append(jnp.where(lower, first, last))
    late_count = jnp.where(first == last, 0, counts_ref[0, last])
    lives.append(slot + HALF < jnp.where(lower, counts_ref[0, first], late_count))
    return (
        jnp.concatenate(indices, 1),
        jnp.concatenate(tiles, 1),
        jnp.concatenate([x.astype(jnp.float32) for x in lives], 1),
    )


MAX_BLOCKS = 8
NOWHERE = -(SLAB_PIX * 8)
LO = 512
STEP = 8


def gather_kernel(n_tile, counts_ref, list_ref, phases_ref, coh_ref, pix_ref, out_ref, own_ref):
    acq_loc, local = phases_ref.shape
    pieces = local // LO
    step = min(STEP, pieces)
    index, tile, live = packed_rows(counts_ref, list_ref, n_tile)
    packed = index.shape[1]
    low = index & (LANES - 1)
    high = index >> 7
    chosen = lax.broadcasted_iota(jnp.int32, (LANES, packed), 0) == low
    table_rows = coh_ref.shape[0]
    coh_hi, coh_lo = split_bf16(coh_ref[...])
    pix = pix_ref[...]
    table = jnp.concatenate(
        [
            coh_hi,
            coh_lo,
            (pix >> 6).astype(jnp.float32).astype(jnp.bfloat16),
            (pix & 63).astype(jnp.float32).astype(jnp.bfloat16),
        ],
        0,
    )
    columns = dot_f32(table, chosen.astype(jnp.float32).astype(jnp.bfloat16), NN)
    row_is = lax.broadcasted_iota(jnp.int32, (table_rows, packed), 0) == high

    def pick(k):
        part = columns[k * table_rows : (k + 1) * table_rows]
        return jnp.sum(jnp.where(row_is, part, 0.0), axis=0, keepdims=True)

    weight = (pick(0) + pick(1)) * live
    pixel = pick(2) * 64.0 + pick(3) + tile.astype(jnp.float32) * float(SLAB_PIX)
    pixel = jnp.where(live > 0.0, pixel, float(NOWHERE))
    out_ref[:, packed:] = jnp.zeros((acq_loc, LANES), jnp.float32)
    for b in range(packed // LANES):
        cut = slice(b * LANES, (b + 1) * LANES)
        out_ref[b : b + 1, packed:] = weight[:, cut]
        out_ref[MAX_BLOCKS + b : MAX_BLOCKS + b + 1, packed:] = pixel[:, cut]
    low = index & (LO - 1)
    high = index >> 9
    chosen = (lax.broadcasted_iota(jnp.int32, (LO, packed), 0) == low)
    chosen = chosen.astype(jnp.float32).astype(jnp.bfloat16)
    own = jnp.zeros((acq_loc, packed), jnp.float32)
    for start in range(0, pieces, step):
        block = jnp.concatenate(
            [phases_ref[:, h * LO : (h + 1) * LO] for h in range(start, start + step)], 0
        )
        block_hi, block_lo = split_bf16(block)
        both = dot_f32(block_hi, chosen, NN) + dot_f32(block_lo, chosen, NN)
        for h in range(step):
            own = jnp.where(high == start + h, both[h * acq_loc : (h + 1) * acq_loc], own)
    own_ref[...] = own
    out_ref[:, 0:packed] = own * weight


def filter_dot(weights, series):
    return lax.dot_general(
        weights,
        series,
        (NN, ((), ())),
        precision=lax.Precision.HIGHEST,
        preferred_element_type=jnp.float32,
    )


def filter_own_kernel(h_ref, part_ref, out_ref):
    acq_loc, lanes = part_ref.shape
    packed = lanes - LANES
    out_ref[:, 0:packed] = filter_dot(h_ref[:, 0:acq_loc], part_ref[:, 0:packed])
    out_ref[:, packed:] = part_ref[:, packed:]


def filter_kernel(h_ref, begun_ref, *refs):
    *parts, out_ref = refs
    acq_loc, lanes = begun_ref.shape
    packed = lanes - LANES
    series = jnp.concatenate([part[:, 0:packed] for part in parts], 0)
    out_ref[:, 0:packed] = begun_ref[:, 0:packed] + filter_dot(h_ref[:, acq_loc:], series)
    out_ref[:, packed:] = begun_ref[:, packed:]


def first_pair(tile, n_pair):
    return jnp.clip((tile + 1) // 2 - 1, 0, max(n_pair - 2, 0))


def hat(distance):
    return jnp.maximum(float(RADIUS + 1) - jnp.abs(distance), 0.0)


def hat_bf16(distance):
    return jnp.maximum(jnp.bfloat16(RADIUS + 1) - jnp.abs(distance), jnp.bfloat16(0))


def split_pixel(pixel):
    whole = pixel.astype(jnp.int32)
    return (whole >> 10).astype(jnp.float32), (whole & (COLS - 1)).astype(jnp.float32)


def split_column(col):
    coarse = jnp.floor(col * 0.125) * 8.0
    return coarse, col - coarse


def rows_of_bf16(row, count):
    few = jnp.broadcast_to(row, (16, row.shape[1])).astype(jnp.bfloat16)
    return jnp.concatenate([few] * (count // 16), 0)


CHUNK = 256


def screen_kernel(n_tile, begins, ends, *refs):
    all_ref, mine_ref = refs[:2]
    refs = refs[2:]
    if not begins:
        image_in, samples_in = refs[:2]
        refs = refs[2:]
    if ends:
        own_ref, screen_ref, residual_ref = refs[:3]
        refs = refs[3:]
    else:
        image_out, samples_out = refs[:2]
        refs = refs[2:]
    tag_ref, value_ref, lhs_ref, col_ref, pair_ref, res_ref, made_ref, made_sem = refs
    n_src, acq_loc, packed = all_ref.shape
    packed -= LANES
    n_pair = n_tile // 2
    width = 3 * LANES
    limit = min_weight * float((RADIUS + 1) ** 4)
    me = lax.axis_index("tile")
    f32, bf16 = jnp.float32, jnp.bfloat16

    def starts(pair):
        start = pl.multiple_of(pair * LANES, LANES)
        return [start, pl.multiple_of(start + LANES, LANES), n_pair * LANES]

    def tags(src, pair):
        blocks = [tag_ref[src, 0:3, pl.ds(s, LANES)] for s in starts(pair)]
        every = jnp.concatenate(blocks, 1)
        return every[0:1], every[1:2], every[2:3]

    sub = lax.broadcasted_iota(jnp.int32, (16, LANES), 0)
    for src in range(n_src):
        value_hi, value_lo = split_bf16(all_ref[src, :, 0:packed])
        value_ref[src, 0:acq_loc, :] = value_hi
        value_ref[src, acq_loc : 2 * acq_loc, :] = value_lo
        for b in range(n_pair + 1):
            lanes = slice(b * LANES, (b + 1) * LANES)
            row, col = split_pixel(all_ref[src, MAX_BLOCKS + b : MAX_BLOCKS + b + 1, packed:])
            weight = all_ref[src, b : b + 1, packed:]
            tag_ref[src, 0:1, lanes] = weight
            tag_ref[src, 1:2, lanes] = row
            tag_ref[src, 2:3, lanes] = col
            tag_ref[src, 3:4, lanes], tag_ref[src, 4:5, lanes] = split_column(col)
            w_hi = weight.astype(bf16).astype(f32)
            both = jnp.where(sub == 0, w_hi, jnp.where(sub == 1, weight - w_hi, 0.0))
            value_ref[src, 2 * acq_loc :, lanes] = both.astype(bf16)

    top = (me * ROWS_DEV).astype(f32)
    row_at = lax.broadcasted_iota(jnp.int32, (ROWS_DEV, width), 0).astype(f32) + top
    col_at = lax.broadcasted_iota(jnp.int32, (CHUNK, width), 0) - CHUNK // 2
    col_at = col_at.astype(f32).astype(bf16)
    pair = first_pair(me, n_pair)
    n_img = acq_loc * ROWS_DEV
    for src in range(n_src):
        weight, row, col = tags(src, pair)
        across = hat(row_at - row)
        lanes = slice(src * width, (src + 1) * width)
        data = jnp.concatenate([all_ref[src, :, pl.ds(s, LANES)] for s in starts(pair)], 1)
        part = jnp.concatenate([across * data[a : a + 1] for a in range(acq_loc)], 0)
        part_hi, part_lo = split_bf16(part)
        lhs_ref[0:n_img, lanes] = part_hi
        lhs_ref[n_img : 2 * n_img, lanes] = part_lo
        w_part = across * weight
        w_hi = w_part.astype(bf16).astype(f32)
        lhs_ref[2 * n_img :, lanes] = jnp.concatenate([w_hi, w_part - w_hi], 0).astype(bf16)

    def down_lanes(row):
        return jnp.transpose(jnp.broadcast_to(row, (LANES, LANES)))

    mine = [mine_ref[MAX_BLOCKS + b : MAX_BLOCKS + b + 1, packed:] for b in range(n_pair + 1)]
    places = [split_pixel(pixel) for pixel in mine]
    rows_down = jnp.concatenate([down_lanes(r) for r, _ in places], 0).astype(bf16)
    coarse_down, fine_down = (
        jnp.concatenate([down_lanes(split_column(c)[k]) for _, c in places], 0).astype(bf16)
        for k in (0, 1)
    )

    def pair_hats(i):
        for src in range(n_src):
            for b in range(n_pair + 1):
                cut = slice(b * LANES, (b + 1) * LANES)
                at = src * packed + b * LANES
                low, high = i * LANES, (i + 1) * LANES
                if max(i, b) < n_pair and i != b:
                    if b == i + 1:
                        low += HALF
                    elif b == i - 1:
                        high -= HALF
                    else:
                        high = low
                for start in (i * LANES, i * LANES + HALF):
                    if low <= start < high:
                        continue
                    zero = jnp.zeros((HALF, LANES), bf16)
                    pair_ref[start : start + HALF, at : at + LANES] = zero
                if low == high:
                    continue
                size = high - low
                row, coarse, fine = (
                    rows_of_bf16(tag_ref[src, k : k + 1, cut], size) for k in (1, 3, 4)
                )
                over = hat_bf16(rows_down[low:high] - row)
                across = (coarse_down[low:high] - coarse) + (fine_down[low:high] - fine)
                pair_ref[low:high, at : at + LANES] = over * hat_bf16(across)

    def sample():
        values = jnp.concatenate([value_ref[src] for src in range(n_src)], 1)
        got = dot_f32(values, pair_ref[...], NT)
        total = got[0:acq_loc] + got[acq_loc : 2 * acq_loc]
        below = got[2 * acq_loc : 2 * acq_loc + 8]
        return jnp.concatenate([total, below], 0)

    def slab(c):
        for src in range(n_src):
            _, _, col = tags(src, pair)
            near = jnp.clip(col - float(c + CHUNK // 2), -160.0, 160.0)
            lanes = slice(src * width, (src + 1) * width)
            col_ref[c : c + CHUNK, lanes] = hat_bf16(col_at - rows_of_bf16(near, CHUNK))
        got = dot_f32(lhs_ref[...], col_ref[c : c + CHUNK, :], NT)
        return jnp.concatenate(
            [
                got[0:n_img] + got[n_img : 2 * n_img],
                got[2 * n_img : 2 * n_img + ROWS_DEV] + got[2 * n_img + ROWS_DEV :],
            ],
            0,
        )

    copies = []
    for c in range(0, COLS, CHUNK):
        image = slab(c)
        lanes = slice(c, c + CHUNK)
        if not begins:
            image = image + image_in[:, lanes]
        if not ends:
            image_out[:, lanes] = image
            continue
        below = jnp.maximum(image[n_img:], limit)
        for a in range(acq_loc):
            made_ref[a, :, lanes] = image[a * ROWS_DEV : (a + 1) * ROWS_DEV] / below
        copies.append(
            pltpu.make_async_copy(
                made_ref.at[:, :, lanes], screen_ref.at[:, :, lanes], made_sem.at[c // CHUNK]
            )
        )
        copies[-1].start()
    for i in range(n_pair + 1):
        pair_hats(i)
    samples = sample()
    if not begins:
        samples = samples + samples_in[...]
    if not ends:
        samples_out[...] = samples
        return
    below = samples[acq_loc : acq_loc + 1] + samples[acq_loc + 1 : acq_loc + 2]
    res_ref[...] = own_ref[...] - samples[0:acq_loc] / jnp.maximum(below, limit)

    lower = lax.broadcasted_iota(jnp.int32, (1, LANES), 1) < HALF
    tiles = [pixel.astype(jnp.int32) // SLAB_PIX for pixel in mine]
    heavy = res_ref[:, n_pair * LANES :]
    turned = pltpu.roll(heavy, HALF, 1)
    tile_turned = pltpu.roll(tiles[n_pair], HALF, 1)
    for t in range(n_tile):
        near = res_ref[:, (t // 2) * LANES : (t // 2 + 1) * LANES]
        tile_near = tiles[t // 2]
        if t % 2:
            near = pltpu.roll(near, HALF, 1)
            tile_near = pltpu.roll(tile_near, HALF, 1)
        far = jnp.where(tile_turned == t, turned, jnp.where(tiles[n_pair] == t, heavy, 0.0))
        residual_ref[:, t * LANES : (t + 1) * LANES] = jnp.where(
            lower, jnp.where(tile_near == t, near, 0.0), far
        )
    for copy in copies:
        copy.wait()


def add_sources(n_tile, sources, mine, sums, own):
    n_src, acq_loc, packed = sources.shape
    packed -= LANES
    width = n_src * 3 * LANES
    f32, bf16 = jnp.float32, jnp.bfloat16
    vmem = pl.BlockSpec(memory_space=pltpu.VMEM)
    n_lhs = 2 * (acq_loc + 1) * ROWS_DEV
    begins, ends = sums is None, own is not None
    args = [sources, mine]
    if not begins:
        args += list(sums)
    if ends:
        args.append(own)
        shapes = ((acq_loc, ROWS_DEV, COLS), (acq_loc, n_tile * LANES))
    else:
        shapes = ((n_lhs // 2, COLS), (acq_loc + 8, packed))
    macs = width * (n_lhs * COLS + (2 * acq_loc + 16) * packed)
    return pl.pallas_call(
        functools.partial(screen_kernel, n_tile, begins, ends),
        out_shape=tuple(jax.ShapeDtypeStruct(shape, f32) for shape in shapes),
        in_specs=[vmem] * len(args),
        out_specs=(pl.BlockSpec(memory_space=pl.ANY) if ends else vmem, vmem),
        scratch_shapes=[
            pltpu.VMEM((n_src, 8, packed), f32),
            pltpu.VMEM((n_src, 2 * acq_loc + 16, packed), bf16),
            pltpu.VMEM((n_lhs, width), bf16),
            pltpu.VMEM((COLS, width), bf16),
            pltpu.VMEM((packed, n_src * packed), bf16),
            pltpu.VMEM((acq_loc, packed), f32),
            pltpu.VMEM((acq_loc, ROWS_DEV, COLS), f32),
            pltpu.SemaphoreType.DMA((COLS // CHUNK,)),
        ],
        input_output_aliases={} if begins or ends else {2: 0, 3: 1},
        cost_estimate=pl.CostEstimate(flops=2 * macs, bytes_accessed=1 << 20, transcendentals=0),
        compiler_params=pltpu.CompilerParams(vmem_limit_bytes=SCREEN_VMEM),
        name="add_sources",
    )(*args)


SCREEN_VMEM = 24 << 20


def xor_permute(x, axis, mask):
    count = lax.axis_size(axis)
    return lax.ppermute(x, axis, [(i, i ^ mask) for i in range(count)])


def gathered_shards(phases, coherence, pixel_index, send_list, counts, band_width):
    acq_loc, local = phases.shape
    n_tile = lax.axis_size("tile")
    n_acq = lax.axis_size("acq")
    packed = (n_tile // 2 + 1) * LANES
    smem = pl.BlockSpec(memory_space=pltpu.SMEM)
    vmem = pl.BlockSpec(memory_space=pltpu.VMEM)
    f32 = jnp.float32
    packet, own = pl.pallas_call(
        functools.partial(gather_kernel, n_tile),
        out_shape=(
            jax.ShapeDtypeStruct((acq_loc, packed + LANES), f32),
            jax.ShapeDtypeStruct((acq_loc, packed), f32),
        ),
        in_specs=[smem, vmem, vmem, vmem, vmem],
        out_specs=(vmem, vmem),
        compiler_params=pltpu.CompilerParams(vmem_limit_bytes=56 << 20),
        name="gather_slots",
    )(
        counts,
        send_list,
        phases,
        coherence.reshape(-1, LANES),
        pixel_index.reshape(-1, LANES),
    )
    here = lax.axis_index("acq")
    parts = [packet] + [xor_permute(packet, "acq", k) for k in range(1, n_acq)]
    source = here ^ jnp.arange(n_acq, dtype=jnp.int32)
    column = (source[:, None] * acq_loc + jnp.arange(acq_loc, dtype=jnp.int32)[None]).reshape(1, -1)
    row = here * acq_loc + jnp.arange(acq_loc, dtype=jnp.int32)
    band = lax.dynamic_slice_in_dim(band_width, here * acq_loc, acq_loc)
    lower = jnp.maximum(row - band, 0)[:, None]
    upper = jnp.minimum(row + band, ACQ - 1)[:, None]
    inside = ((column >= lower) & (column <= upper)).astype(f32)
    highpass = (column == row[:, None]).astype(f32) - inside / (upper - lower + 1).astype(f32)
    packet_shape = jax.ShapeDtypeStruct((acq_loc, packed + LANES), f32)
    small = pltpu.CompilerParams(vmem_limit_bytes=4 << 20)
    begun = pl.pallas_call(
        filter_own_kernel,
        out_shape=packet_shape,
        in_specs=[vmem] * 2,
        out_specs=vmem,
        cost_estimate=pl.CostEstimate(flops=1 << 20, bytes_accessed=1 << 20, transcendentals=0),
        compiler_params=small,
        name="filter_own_slots",
    )(highpass, packet)
    filtered = pl.pallas_call(
        filter_kernel,
        out_shape=packet_shape,
        in_specs=[vmem] * (n_acq + 1),
        out_specs=vmem,
        compiler_params=small,
        name="filter_slots",
    )(highpass, begun, *parts[1:])
    half = n_tile // 2
    across = xor_permute(filtered, "tile", half)
    sums = add_sources(n_tile, filtered[None], filtered, None, None)
    across, sums = lax.optimization_barrier((across, sums))
    held = jnp.stack([filtered, across])
    arriving = [across[None]] + [xor_permute(held, "tile", k) for k in range(1, half)]
    for sources in arriving[:-1]:
        sums = add_sources(n_tile, sources, filtered, sums, None)
    screen, residual = add_sources(n_tile, arriving[-1], filtered, sums, own)
    return residual, screen


def solution(mesh):
    n_tile = mesh.shape["tile"]
    few = n_tile in (4, 8)
    return jax.shard_map(
        gathered_shards if few else exchange_shards,
        mesh=mesh,
        in_specs=(P("acq", "tile"), P("tile"), P("tile"), P("tile", None), P("tile", None), P()),
        out_specs=(P("acq", "tile"), P("acq", "tile", None)),
        check_vma=False,
    )
```

```python
import functools

import jax
import jax.numpy as jnp
from jax import lax
from jax.experimental import pallas as pl
from jax.experimental.pallas import tpu as pltpu
from jax.sharding import PartitionSpec as P

ACQ = 64
ROWS_DEV = 8
COLS = 1024
RADIUS = 4
SLAB_PIX = 8192
HALF = 64
LANES = 128


min_weight = 0.1


def with_halo(cells, sides, width):
    for axis, dim in sides:
        count = lax.axis_size(axis)
        ends = count - 1
        head = lax.slice_in_dim(cells, 0, width, axis=dim)
        tail = lax.slice_in_dim(cells, cells.shape[dim] - width, cells.shape[dim], axis=dim)
        cells = jnp.concatenate(
            [
                lax.ppermute(tail, axis, [(i, (i + 1) % count) for i in range(ends)]),
                cells,
                lax.ppermute(head, axis, [((i + 1) % count, i) for i in range(ends)]),
            ],
            axis=dim,
        )
    return cells


def temporal_matrix(band_width):
    positions = jnp.arange(ACQ, dtype=jnp.int32)
    lower = jnp.maximum(positions - band_width, 0)
    upper = jnp.minimum(positions + band_width, ACQ - 1)
    inside = (positions[None, :] >= lower[:, None]) & (positions[None, :] <= upper[:, None])
    window = (upper - lower + 1).astype(jnp.float32)
    return jnp.eye(ACQ, dtype=jnp.float32) - inside.astype(jnp.float32) / window[:, None]


def kernel_weights():
    return [
        (RADIUS + 1 - abs(offset - RADIUS)) / float((RADIUS + 1) ** 2)
        for offset in range(2 * RADIUS + 1)
    ]


def smooth(padded_rows):
    weights = kernel_weights()
    row_count = padded_rows.shape[-2] - 2 * RADIUS
    vertical = weights[0] * padded_rows[..., 0:row_count, :]
    for offset in range(1, 2 * RADIUS + 1):
        vertical = vertical + weights[offset] * padded_rows[..., offset : offset + row_count, :]
    column_count = vertical.shape[-1]
    pad_width = [(0, 0)] * (vertical.ndim - 1) + [(RADIUS, RADIUS)]
    widened = jnp.pad(vertical, pad_width)
    total = weights[0] * widened[..., 0:column_count]
    for offset in range(1, 2 * RADIUS + 1):
        total = total + weights[offset] * widened[..., offset : offset + column_count]
    return total


def apply_highpass(highpass, series):
    return jnp.dot(
        highpass, series, precision=lax.Precision.HIGHEST, preferred_element_type=jnp.float32
    )


def exchange_shards(phases, coherence, pixel_index, send_list, counts, band_width):
    acq_loc = phases.shape[0]
    capacity = send_list.shape[1]
    highpass = temporal_matrix(band_width)
    live_slot = jnp.arange(capacity, dtype=jnp.int32)[None, :] < counts[0][:, None]
    slot_weight = jnp.where(live_slot, coherence[send_list], jnp.float32(0.0))
    slot_pixel = pixel_index[send_list]
    outgoing = phases[:, send_list] * slot_weight[None]
    arrived, arrived_weight, arrived_pixel = (
        lax.all_to_all(outgoing, "tile", split_axis=1, concat_axis=1, tiled=True),
        lax.all_to_all(slot_weight[None], "tile", split_axis=1, concat_axis=1, tiled=True),
        lax.all_to_all(slot_pixel[None], "tile", split_axis=1, concat_axis=1, tiled=True),
    )
    targets = arrived_pixel.reshape(-1)
    phase_image = (
        jnp.zeros((acq_loc, SLAB_PIX), jnp.float32).at[:, targets].add(arrived.reshape(acq_loc, -1))
    )
    weight_sum = jnp.zeros((SLAB_PIX,), jnp.float32).at[targets].add(arrived_weight.reshape(-1))
    series = lax.all_to_all(phase_image, "acq", split_axis=1, concat_axis=0, tiled=True)
    phase_image = lax.all_to_all(
        apply_highpass(highpass, series), "acq", split_axis=0, concat_axis=1, tiled=True
    )
    stacked = jnp.concatenate([phase_image, weight_sum[None, :]], axis=0).reshape(
        acq_loc + 1, ROWS_DEV, COLS
    )
    padded = with_halo(stacked, (("tile", 1),), RADIUS)
    smoothed = smooth(padded)
    screen = smoothed[:acq_loc] / jnp.maximum(smoothed[acq_loc], min_weight)
    flattened = screen.reshape(acq_loc, SLAB_PIX)
    sampled = flattened[:, arrived_pixel[0]]
    returned = lax.all_to_all(sampled, "tile", split_axis=1, concat_axis=1, tiled=True)
    residual = jnp.where(live_slot[None], phases[:, send_list] - returned, jnp.float32(0.0))
    return (residual.reshape(acq_loc, -1), screen)


def split_bf16(x):
    high = x.astype(jnp.bfloat16)
    return high, (x - high.astype(jnp.float32)).astype(jnp.bfloat16)


def rows_of_bf16(row, count):
    few = jnp.broadcast_to(row, (16, row.shape[1])).astype(jnp.bfloat16)
    return jnp.concatenate([few] * (count // 16), 0)


def dot_f32(a, b, dims):
    return lax.dot_general(a, b, (dims, ((), ())), preferred_element_type=jnp.float32)


NN = ((1,), (0,))
NT = ((1,), (1,))


def packed_rows(counts, lists):
    n_tile = counts.shape[1]
    at = lax.broadcasted_iota(jnp.int32, counts.shape, 1).astype(jnp.float32)
    heavy = counts >= HALF
    first = jnp.min(jnp.where(heavy, at, float(n_tile - 1)), axis=1, keepdims=True)
    last = jnp.max(jnp.where(heavy, at, 0.0), axis=1, keepdims=True)
    lane = lax.broadcasted_iota(jnp.int32, (1, LANES), 1)
    lower = lane < HALF
    slot = lane & (HALF - 1)

    def halves(low, high):
        return jnp.where(lower, jnp.broadcast_to(low, lower.shape), jnp.broadcast_to(high, lower.shape))

    def count_of(t):
        return counts[:, t : t + 1]

    indices, tiles, lives = [], [], []
    for t in range(0, n_tile, 2):
        odd = pltpu.roll(lists[t + 1 : t + 2], HALF, 1)
        indices.append(jnp.where(lower, lists[t : t + 1], odd))
        tiles.append(jnp.where(lower, t, t + 1))
        lives.append(slot < halves(count_of(t), count_of(t + 1)))
    early, late = lists[0:1], lists[0:1]
    early_count, late_count = count_of(0), count_of(0)
    for t in range(1, n_tile):
        row = lists[t : t + 1]
        early = jnp.where(jnp.broadcast_to(first == t, row.shape), row, early)
        late = jnp.where(jnp.broadcast_to(last == t, row.shape), row, late)
        early_count = jnp.where(first == t, count_of(t), early_count)
        late_count = jnp.where(last == t, count_of(t), late_count)
    late_count = jnp.where(first == last, 0, late_count)
    indices.append(jnp.where(lower, pltpu.roll(early, HALF, 1), late))
    tiles.append(halves(first, last).astype(jnp.int32))
    lives.append(slot + HALF < halves(early_count, late_count))
    return (
        jnp.concatenate(indices, 1),
        jnp.concatenate(tiles, 1),
        jnp.concatenate([x.astype(jnp.float32) for x in lives], 1),
    )


MAX_BLOCKS = 8
NOWHERE = -(SLAB_PIX * 8)
LO = 512
STEP = 32


def gather_kernel(
    counts_hbm, list_hbm, coh_hbm, pix_hbm, phases_hbm, out_ref, own_ref,
    counts_ref, list_ref, coh_ref, pix_ref, phases_ref, sems,
):
    acq_loc, local = phases_ref.shape
    pieces = local // LO
    step = min(STEP, pieces)
    inputs = [
        (counts_hbm, counts_ref), (list_hbm, list_ref), (coh_hbm, coh_ref), (pix_hbm, pix_ref)
    ]
    for start in range(0, pieces, step):
        lanes = pl.ds(start * LO, step * LO)
        inputs.append((phases_hbm.at[:, lanes], phases_ref.at[:, lanes]))
    copies = [pltpu.make_async_copy(*pair, sems.at[i]) for i, pair in enumerate(inputs)]
    for copy in copies:
        copy.start()
    for copy in copies[0:2]:
        copy.wait()
    index, tile, live = packed_rows(counts_ref[...], list_ref[...])
    packed = index.shape[1]
    low = (index & (LO - 1)) - LO // 2
    high = index >> 9
    at = (lax.broadcasted_iota(jnp.int32, (LO, packed), 0) - LO // 2).astype(jnp.float32)
    off = at.astype(jnp.bfloat16) - rows_of_bf16(low.astype(jnp.float32), LO)
    chosen = jnp.maximum(jnp.bfloat16(1) - jnp.abs(off), jnp.bfloat16(0))
    twice = jnp.concatenate([chosen, chosen], 0)
    for copy in copies[2:4]:
        copy.wait()

    def pieces_of(ref):
        split = LO // LANES
        return jnp.concatenate([ref[pl.ds(k, pieces, stride=split), :] for k in range(split)], 1)

    pix = pieces_of(pix_ref)
    table = jnp.concatenate(
        [
            jnp.concatenate(split_bf16(pieces_of(coh_ref)), 1),
            jnp.concatenate(
                [
                    ((pix >> 6) << 6).astype(jnp.float32).astype(jnp.bfloat16),
                    (pix & 63).astype(jnp.float32).astype(jnp.bfloat16),
                ],
                1,
            ),
        ],
        0,
    )
    columns = dot_f32(table, twice, NN)
    row_is = lax.broadcasted_iota(jnp.int32, (pieces, packed), 0) == high

    def pick(k):
        part = columns[k * pieces : (k + 1) * pieces]
        return jnp.sum(jnp.where(row_is, part, 0.0), axis=0, keepdims=True)

    weight = pick(0) * live
    pixel = pick(1) + tile.astype(jnp.float32) * float(SLAB_PIX)
    pixel = jnp.where(live > 0.0, pixel, float(NOWHERE))
    out_ref[:, packed:] = jnp.zeros((acq_loc, LANES), jnp.float32)
    for b in range(packed // LANES):
        cut = slice(b * LANES, (b + 1) * LANES)
        out_ref[b : b + 1, packed:] = weight[:, cut]
        out_ref[MAX_BLOCKS + b : MAX_BLOCKS + b + 1, packed:] = pixel[:, cut]
    own = jnp.zeros((acq_loc, packed), jnp.float32)
    for start in range(0, pieces, step):
        copies[4 + start // step].wait()
        block = jnp.concatenate(
            [phases_ref[:, h * LO : (h + 1) * LO] for h in range(start, start + step)], 0
        )
        both = dot_f32(jnp.concatenate(split_bf16(block), 1), twice, NN)
        for h in range(step):
            own = jnp.where(high == start + h, both[h * acq_loc : (h + 1) * acq_loc], own)
    own_ref[...] = own
    out_ref[:, 0:packed] = own * weight


def gather_call(phases, coherence, pixel_index, send_list, counts):
    acq_loc, local = phases.shape
    packed = (send_list.shape[0] // 2 + 1) * LANES
    vmem = pl.BlockSpec(memory_space=pltpu.VMEM)
    f32 = jnp.float32
    inputs = (counts, send_list, coherence.reshape(-1, LANES), pixel_index.reshape(-1, LANES), phases)
    return pl.pallas_call(
        gather_kernel,
        out_shape=(
            jax.ShapeDtypeStruct((acq_loc, packed + LANES), f32),
            jax.ShapeDtypeStruct((acq_loc, packed), f32),
        ),
        in_specs=[pl.BlockSpec(memory_space=pl.ANY)] * len(inputs),
        out_specs=(vmem, vmem),
        scratch_shapes=[pltpu.VMEM(x.shape, x.dtype) for x in inputs]
        + [pltpu.SemaphoreType.DMA((4 + max(local // (LO * STEP), 1),))],
        compiler_params=pltpu.CompilerParams(vmem_limit_bytes=12 << 20),
        name="gather_slots",
    )(*[pltpu.with_memory_space_constraint(x, pltpu.HBM) for x in inputs])


def filter_dot(weights, series):
    return lax.dot_general(
        weights,
        series,
        (((0,), (0,)), ((), ())),
        precision=lax.Precision.HIGHEST,
        preferred_element_type=jnp.float32,
    )


def down_lanes(row):
    return jnp.transpose(jnp.broadcast_to(row, (LANES, LANES)))


def filter_own_kernel(n_acq, band_ref, part_ref, out_ref, h_ref, down_ref):
    acq_loc, lanes = part_ref.shape
    packed = lanes - LANES
    me = lax.axis_index("acq")
    band = band_ref[:, 0:acq_loc]
    for a in range(1, n_acq):
        band = jnp.where(me == a, band_ref[:, a * acq_loc : (a + 1) * acq_loc], band)
    mine = me * acq_loc + lax.broadcasted_iota(jnp.int32, (1, acq_loc), 1)
    lower = jnp.maximum(mine - band, 0)
    upper = jnp.minimum(mine + band, ACQ - 1)
    share = 1.0 / (upper - lower + 1).astype(jnp.float32)
    for k in range(n_acq):
        source = (me ^ k) * acq_loc + lax.broadcasted_iota(jnp.int32, (acq_loc, acq_loc), 0)
        inside = (source >= lower) & (source <= upper)
        unit = jnp.where(source == mine, 1.0, 0.0)
        h_ref[k * acq_loc : (k + 1) * acq_loc, :] = unit - jnp.where(inside, share, 0.0)
    out_ref[:, 0:packed] = filter_dot(h_ref[0:acq_loc, :], part_ref[:, 0:packed])
    out_ref[:, packed:] = part_ref[:, packed:]
    for b in range(packed // LANES):
        pixel = part_ref[MAX_BLOCKS + b : MAX_BLOCKS + b + 1, packed:]
        row, col = split_pixel(pixel)
        for k, value in enumerate((row, *split_column(col))):
            down_ref[k, b * LANES : (b + 1) * LANES, :] = down_lanes(value)


def filter_kernel(h_ref, begun_ref, *refs):
    *parts, out_ref = refs
    acq_loc, lanes = begun_ref.shape
    packed = lanes - LANES
    series = jnp.concatenate([part[:, 0:packed] for part in parts], 0)
    out_ref[:, 0:packed] = begun_ref[:, 0:packed] + filter_dot(h_ref[acq_loc:, :], series)
    out_ref[:, packed:] = begun_ref[:, packed:]


def first_pair(tile, n_pair):
    return jnp.clip((tile + 1) // 2 - 1, 0, max(n_pair - 2, 0))


def hat(distance):
    return jnp.maximum(float(RADIUS + 1) - jnp.abs(distance), 0.0)


def hat_bf16(distance):
    return jnp.maximum(jnp.bfloat16(RADIUS + 1) - jnp.abs(distance), jnp.bfloat16(0))


def split_pixel(pixel):
    whole = pixel.astype(jnp.int32)
    return (whole >> 10).astype(jnp.float32), (whole & (COLS - 1)).astype(jnp.float32)


def split_column(col):
    coarse = jnp.floor(col * 0.125) * 8.0
    return coarse, col - coarse


CHUNK = 256


def screen_kernel(n_tile, begins, ends, *refs):
    all_ref, mine_ref, down_ref = refs[:3]
    refs = refs[3:]
    if not begins:
        image_in, samples_in = refs[:2]
        refs = refs[2:]
    if ends:
        own_ref, screen_ref, residual_ref = refs[:3]
        refs = refs[3:]
    else:
        image_out, samples_out = refs[:2]
        refs = refs[2:]
    tag_ref, few_ref, value_ref, lhs_ref, res_ref, made_ref, made_sem = refs
    n_src, acq_loc, packed = all_ref.shape
    packed -= LANES
    n_pair = n_tile // 2
    width = 3 * LANES
    limit = min_weight * float((RADIUS + 1) ** 4)
    me = lax.axis_index("tile")
    f32, bf16 = jnp.float32, jnp.bfloat16

    def starts(pair):
        start = pl.multiple_of(pair * LANES, LANES)
        return [start, pl.multiple_of(start + LANES, LANES), n_pair * LANES]

    def tags(src, pair):
        blocks = [tag_ref[src, 0:3, pl.ds(s, LANES)] for s in starts(pair)]
        every = jnp.concatenate(blocks, 1)
        return every[0:1], every[1:2], every[2:3]

    sub = lax.broadcasted_iota(jnp.int32, (16, LANES), 0)
    for src in range(n_src):
        value_hi, value_lo = split_bf16(all_ref[src, :, 0:packed])
        value_ref[src, 0:acq_loc, :] = value_hi
        value_ref[src, acq_loc : 2 * acq_loc, :] = value_lo
        for b in range(n_pair + 1):
            lanes = slice(b * LANES, (b + 1) * LANES)
            row, col = split_pixel(all_ref[src, MAX_BLOCKS + b : MAX_BLOCKS + b + 1, packed:])
            weight = all_ref[src, b : b + 1, packed:]
            tag_ref[src, 0:1, lanes] = weight
            tag_ref[src, 1:2, lanes] = row
            tag_ref[src, 2:3, lanes] = col
            for k, value in enumerate((row, *split_column(col))):
                few_ref[src, k, :, lanes] = rows_of_bf16(value, 16)
            w_hi = weight.astype(bf16).astype(f32)
            both = jnp.where(sub == 0, w_hi, jnp.where(sub == 1, weight - w_hi, 0.0))
            value_ref[src, 2 * acq_loc :, lanes] = both.astype(bf16)

    top = (me * ROWS_DEV).astype(f32)
    row_at = lax.broadcasted_iota(jnp.int32, (ROWS_DEV, width), 0).astype(f32) + top
    col_at = lax.broadcasted_iota(jnp.int32, (CHUNK, width), 0) - CHUNK // 2
    col_at = col_at.astype(f32).astype(bf16)
    pair = first_pair(me, n_pair)
    n_img = acq_loc * ROWS_DEV
    for src in range(n_src):
        weight, row, col = tags(src, pair)
        across = hat(row_at - row)
        lanes = slice(src * width, (src + 1) * width)
        data = jnp.concatenate([all_ref[src, :, pl.ds(s, LANES)] for s in starts(pair)], 1)
        part = jnp.concatenate([across * data[a : a + 1] for a in range(acq_loc)], 0)
        part_hi, part_lo = split_bf16(part)
        lhs_ref[0:n_img, lanes] = part_hi
        lhs_ref[n_img : 2 * n_img, lanes] = part_lo
        w_part = across * weight
        w_hi = w_part.astype(bf16).astype(f32)
        lhs_ref[2 * n_img :, lanes] = jnp.concatenate([w_hi, w_part - w_hi], 0).astype(bf16)

    def pair_hats(start):
        slots = slice(start, start + HALF)
        near = range(n_pair + 1)
        if start < n_pair * LANES:
            tile = start // HALF
            near = {(tile - 1) // 2, tile // 2, (tile + 1) // 2, n_pair}
        blocks = []
        row_i, coarse_i, fine_i = (down_ref[k, slots, :].astype(bf16) for k in range(3))
        for src in range(n_src):
            for b in range(n_pair + 1):
                if b not in near:
                    blocks.append(jnp.zeros((HALF, LANES), bf16))
                    continue
                cut = slice(b * LANES, (b + 1) * LANES)
                row, coarse, fine = (
                    jnp.concatenate([few_ref[src, k, :, cut]] * (HALF // 16), 0) for k in range(3)
                )
                across = (coarse_i - coarse) + (fine_i - fine)
                blocks.append(hat_bf16(row_i - row) * hat_bf16(across))

        return jnp.concatenate(blocks, 1)

    def sample():
        pairs = jnp.concatenate([pair_hats(at) for at in range(0, packed, HALF)], 0)
        values = jnp.concatenate([value_ref[src] for src in range(n_src)], 1)
        got = dot_f32(values, pairs, NT)
        total = got[0:acq_loc] + got[acq_loc : 2 * acq_loc]
        below = got[2 * acq_loc : 2 * acq_loc + 8]
        return jnp.concatenate([total, below], 0)

    def slab(c):
        cols = []
        for src in range(n_src):
            _, _, col = tags(src, pair)
            near = jnp.clip(col - float(c + CHUNK // 2), -160.0, 160.0)
            cols.append(hat_bf16(col_at - rows_of_bf16(near, CHUNK)))
        got = dot_f32(lhs_ref[...], jnp.concatenate(cols, 1), NT)
        return jnp.concatenate(
            [
                got[0:n_img] + got[n_img : 2 * n_img],
                got[2 * n_img : 2 * n_img + ROWS_DEV] + got[2 * n_img + ROWS_DEV :],
            ],
            0,
        )

    copies = []
    for c in range(0, COLS, CHUNK):
        image = slab(c)
        lanes = slice(c, c + CHUNK)
        if not begins:
            image = image + image_in[:, lanes]
        if not ends:
            image_out[:, lanes] = image
            continue
        scale = 1.0 / jnp.maximum(image[n_img:], limit)
        for a in range(acq_loc):
            made_ref[a, :, lanes] = image[a * ROWS_DEV : (a + 1) * ROWS_DEV] * scale
        copies.append(
            pltpu.make_async_copy(
                made_ref.at[:, :, lanes], screen_ref.at[:, :, lanes], made_sem.at[c // CHUNK]
            )
        )
        copies[-1].start()
    samples = sample()
    if not begins:
        samples = samples + samples_in[...]
    if not ends:
        samples_out[...] = samples
        return
    below = samples[acq_loc : acq_loc + 1] + samples[acq_loc + 1 : acq_loc + 2]
    res_ref[...] = own_ref[...] - samples[0:acq_loc] * (1.0 / jnp.maximum(below, limit))

    lower = lax.broadcasted_iota(jnp.int32, (1, LANES), 1) < HALF
    tiles = [
        mine_ref[MAX_BLOCKS + b : MAX_BLOCKS + b + 1, packed:].astype(jnp.int32) // SLAB_PIX
        for b in range(n_pair + 1)
    ]
    heavy = res_ref[:, n_pair * LANES :]
    turned = pltpu.roll(heavy, HALF, 1)
    tile_turned = pltpu.roll(tiles[n_pair], HALF, 1)
    for t in range(n_tile):
        near = res_ref[:, (t // 2) * LANES : (t // 2 + 1) * LANES]
        tile_near = tiles[t // 2]
        if t % 2:
            near = pltpu.roll(near, HALF, 1)
            tile_near = pltpu.roll(tile_near, HALF, 1)
        far = jnp.where(tile_turned == t, turned, jnp.where(tiles[n_pair] == t, heavy, 0.0))
        residual_ref[:, t * LANES : (t + 1) * LANES] = jnp.where(
            lower, jnp.where(tile_near == t, near, 0.0), far
        )
    for copy in copies:
        copy.wait()


def add_sources(n_tile, sources, mine, down, sums, own):
    n_src, acq_loc, packed = sources.shape
    packed -= LANES
    width = n_src * 3 * LANES
    f32, bf16 = jnp.float32, jnp.bfloat16
    vmem = pl.BlockSpec(memory_space=pltpu.VMEM)
    n_lhs = 2 * (acq_loc + 1) * ROWS_DEV
    begins, ends = sums is None, own is not None
    args = [sources, mine, down]
    if not begins:
        args += list(sums)
    if ends:
        args.append(own)
        shapes = ((acq_loc, ROWS_DEV, COLS), (acq_loc, n_tile * LANES))
    else:
        shapes = ((n_lhs // 2, COLS), (acq_loc + 8, packed))
    macs = width * (n_lhs * COLS + (2 * acq_loc + 16) * packed)
    return pl.pallas_call(
        functools.partial(screen_kernel, n_tile, begins, ends),
        out_shape=tuple(jax.ShapeDtypeStruct(shape, f32) for shape in shapes),
        in_specs=[vmem] * len(args),
        out_specs=(pl.BlockSpec(memory_space=pl.ANY) if ends else vmem, vmem),
        scratch_shapes=[
            pltpu.VMEM((n_src, 8, packed), f32),
            pltpu.VMEM((n_src, 3, 16, packed), bf16),
            pltpu.VMEM((n_src, 2 * acq_loc + 16, packed), bf16),
            pltpu.VMEM((n_lhs, width), bf16),
            pltpu.VMEM((acq_loc, packed), f32),
            pltpu.VMEM((acq_loc, ROWS_DEV, COLS), f32),
            pltpu.SemaphoreType.DMA((COLS // CHUNK,)),
        ],
        input_output_aliases={} if begins or ends else {3: 0, 4: 1},
        cost_estimate=pl.CostEstimate(flops=2 * macs, bytes_accessed=1 << 20, transcendentals=0),
        compiler_params=pltpu.CompilerParams(vmem_limit_bytes=SCREEN_VMEM),
        name="add_sources",
    )(*args)


SCREEN_VMEM = 24 << 20


def xor_permute(x, axis, mask):
    count = lax.axis_size(axis)
    return lax.ppermute(x, axis, [(i, i ^ mask) for i in range(count)])


def gathered_shards(phases, coherence, pixel_index, send_list, counts, band_width):
    acq_loc = phases.shape[0]
    n_tile = lax.axis_size("tile")
    n_acq = lax.axis_size("acq")
    packed = (n_tile // 2 + 1) * LANES
    vmem = pl.BlockSpec(memory_space=pltpu.VMEM)
    f32 = jnp.float32
    packet, own = gather_call(phases, coherence, pixel_index, send_list, counts)
    parts = [xor_permute(packet, "acq", k) for k in range(1, n_acq)]
    packet_shape = jax.ShapeDtypeStruct((acq_loc, packed + LANES), f32)
    begun, highpass, down = pl.pallas_call(
        functools.partial(filter_own_kernel, n_acq),
        out_shape=(
            packet_shape,
            jax.ShapeDtypeStruct((n_acq * acq_loc, acq_loc), f32),
            jax.ShapeDtypeStruct((3, packed, LANES), f32),
        ),
        in_specs=[vmem] * 2,
        out_specs=(vmem,) * 3,
        cost_estimate=pl.CostEstimate(flops=1 << 20, bytes_accessed=1 << 20, transcendentals=0),
        compiler_params=pltpu.CompilerParams(vmem_limit_bytes=4 << 20),
        name="filter_own_slots",
    )(band_width.reshape(1, -1), packet)
    filtered = pl.pallas_call(
        filter_kernel,
        out_shape=packet_shape,
        in_specs=[vmem] * (n_acq + 1),
        out_specs=vmem,
        compiler_params=pltpu.CompilerParams(vmem_limit_bytes=4 << 20),
        name="filter_slots",
    )(highpass, begun, *parts)
    half = n_tile // 2
    across = xor_permute(filtered, "tile", half)
    sums = add_sources(n_tile, filtered[None], filtered, down, None, None)
    across, sums = lax.optimization_barrier((across, sums))
    held = jnp.stack([filtered, across])
    arriving = [across[None]] + [xor_permute(held, "tile", k) for k in range(1, half)]
    for sources in arriving[:-1]:
        sums = add_sources(n_tile, sources, filtered, down, sums, None)
    screen, residual = add_sources(n_tile, arriving[-1], filtered, down, sums, own)
    return residual, screen


def solution(mesh):
    n_tile = mesh.shape["tile"]
    few = n_tile in (4, 8)
    return jax.shard_map(
        gathered_shards if few else exchange_shards,
        mesh=mesh,
        in_specs=(P("acq", "tile"), P("tile"), P("tile"), P("tile", None), P("tile", None), P()),
        out_specs=(P("acq", "tile"), P("acq", "tile", None)),
        check_vma=False,
    )
```

```python
import functools

import jax
import jax.numpy as jnp
from jax import lax
from jax.experimental import pallas as pl
from jax.experimental.pallas import tpu as pltpu
from jax.sharding import PartitionSpec as P

ACQ = 64
ROWS_DEV = 8
COLS = 1024
RADIUS = 4
SLAB_PIX = 8192
SLAB_SHIFT = 13
HALF = 64
LANES = 128


min_weight = 0.1


def with_halo(cells, sides, width):
    for axis, dim in sides:
        count = lax.axis_size(axis)
        ends = count - 1
        head = lax.slice_in_dim(cells, 0, width, axis=dim)
        tail = lax.slice_in_dim(cells, cells.shape[dim] - width, cells.shape[dim], axis=dim)
        cells = jnp.concatenate(
            [
                lax.ppermute(tail, axis, [(i, (i + 1) % count) for i in range(ends)]),
                cells,
                lax.ppermute(head, axis, [((i + 1) % count, i) for i in range(ends)]),
            ],
            axis=dim,
        )
    return cells


def temporal_matrix(band_width):
    positions = jnp.arange(ACQ, dtype=jnp.int32)
    lower = jnp.maximum(positions - band_width, 0)
    upper = jnp.minimum(positions + band_width, ACQ - 1)
    inside = (positions[None, :] >= lower[:, None]) & (positions[None, :] <= upper[:, None])
    window = (upper - lower + 1).astype(jnp.float32)
    return jnp.eye(ACQ, dtype=jnp.float32) - inside.astype(jnp.float32) / window[:, None]


def kernel_weights():
    return [
        (RADIUS + 1 - abs(offset - RADIUS)) / float((RADIUS + 1) ** 2)
        for offset in range(2 * RADIUS + 1)
    ]


def smooth(padded_rows):
    weights = kernel_weights()
    row_count = padded_rows.shape[-2] - 2 * RADIUS
    vertical = weights[0] * padded_rows[..., 0:row_count, :]
    for offset in range(1, 2 * RADIUS + 1):
        vertical = vertical + weights[offset] * padded_rows[..., offset : offset + row_count, :]
    column_count = vertical.shape[-1]
    pad_width = [(0, 0)] * (vertical.ndim - 1) + [(RADIUS, RADIUS)]
    widened = jnp.pad(vertical, pad_width)
    total = weights[0] * widened[..., 0:column_count]
    for offset in range(1, 2 * RADIUS + 1):
        total = total + weights[offset] * widened[..., offset : offset + column_count]
    return total


def apply_highpass(highpass, series):
    return jnp.dot(
        highpass, series, precision=lax.Precision.HIGHEST, preferred_element_type=jnp.float32
    )


def exchange_shards(phases, coherence, pixel_index, send_list, counts, band_width):
    acq_loc = phases.shape[0]
    capacity = send_list.shape[1]
    highpass = temporal_matrix(band_width)
    live_slot = jnp.arange(capacity, dtype=jnp.int32)[None, :] < counts[0][:, None]
    slot_weight = jnp.where(live_slot, coherence[send_list], jnp.float32(0.0))
    slot_pixel = pixel_index[send_list]
    outgoing = phases[:, send_list] * slot_weight[None]
    arrived, arrived_weight, arrived_pixel = (
        lax.all_to_all(outgoing, "tile", split_axis=1, concat_axis=1, tiled=True),
        lax.all_to_all(slot_weight[None], "tile", split_axis=1, concat_axis=1, tiled=True),
        lax.all_to_all(slot_pixel[None], "tile", split_axis=1, concat_axis=1, tiled=True),
    )
    targets = arrived_pixel.reshape(-1)
    phase_image = (
        jnp.zeros((acq_loc, SLAB_PIX), jnp.float32).at[:, targets].add(arrived.reshape(acq_loc, -1))
    )
    weight_sum = jnp.zeros((SLAB_PIX,), jnp.float32).at[targets].add(arrived_weight.reshape(-1))
    series = lax.all_to_all(phase_image, "acq", split_axis=1, concat_axis=0, tiled=True)
    phase_image = lax.all_to_all(
        apply_highpass(highpass, series), "acq", split_axis=0, concat_axis=1, tiled=True
    )
    stacked = jnp.concatenate([phase_image, weight_sum[None, :]], axis=0).reshape(
        acq_loc + 1, ROWS_DEV, COLS
    )
    padded = with_halo(stacked, (("tile", 1),), RADIUS)
    smoothed = smooth(padded)
    screen = smoothed[:acq_loc] / jnp.maximum(smoothed[acq_loc], min_weight)
    flattened = screen.reshape(acq_loc, SLAB_PIX)
    sampled = flattened[:, arrived_pixel[0]]
    returned = lax.all_to_all(sampled, "tile", split_axis=1, concat_axis=1, tiled=True)
    residual = jnp.where(live_slot[None], phases[:, send_list] - returned, jnp.float32(0.0))
    return (residual.reshape(acq_loc, -1), screen)


def split_bf16(x):
    high = x.astype(jnp.bfloat16)
    return high, (x - high.astype(jnp.float32)).astype(jnp.bfloat16)


def rows_of_bf16(row, count):
    few = jnp.broadcast_to(row, (16, row.shape[1])).astype(jnp.bfloat16)
    return jnp.concatenate([few] * (count // 16), 0)


def dot_f32(a, b, dims):
    return lax.dot_general(a, b, (dims, ((), ())), preferred_element_type=jnp.float32)


NN = ((1,), (0,))
NT = ((1,), (1,))


def packed_rows(counts, lists):
    n_tile = counts.shape[1]
    at = lax.broadcasted_iota(jnp.int32, counts.shape, 1).astype(jnp.float32)
    heavy = counts >= HALF
    first = jnp.min(jnp.where(heavy, at, float(n_tile - 1)), axis=1, keepdims=True)
    last = jnp.max(jnp.where(heavy, at, 0.0), axis=1, keepdims=True)
    lane = lax.broadcasted_iota(jnp.int32, (1, LANES), 1)
    lower = lane < HALF
    slot = lane & (HALF - 1)

    def halves(low, high):
        return jnp.where(lower, jnp.broadcast_to(low, lower.shape), jnp.broadcast_to(high, lower.shape))

    def count_of(t):
        return counts[:, t : t + 1]

    indices, tiles, lives = [], [], []
    for t in range(0, n_tile, 2):
        odd = pltpu.roll(lists[t + 1 : t + 2], HALF, 1)
        indices.append(jnp.where(lower, lists[t : t + 1], odd))
        tiles.append(jnp.where(lower, t, t + 1))
        lives.append(slot < halves(count_of(t), count_of(t + 1)))
    early, late = lists[0:1], lists[0:1]
    early_count, late_count = count_of(0), count_of(0)
    for t in range(1, n_tile):
        row = lists[t : t + 1]
        early = jnp.where(jnp.broadcast_to(first == t, row.shape), row, early)
        late = jnp.where(jnp.broadcast_to(last == t, row.shape), row, late)
        early_count = jnp.where(first == t, count_of(t), early_count)
        late_count = jnp.where(last == t, count_of(t), late_count)
    late_count = jnp.where(first == last, 0, late_count)
    indices.append(jnp.where(lower, pltpu.roll(early, HALF, 1), late))
    tiles.append(halves(first, last).astype(jnp.int32))
    lives.append(slot + HALF < halves(early_count, late_count))
    return (
        jnp.concatenate(indices, 1),
        jnp.concatenate(tiles, 1),
        jnp.concatenate([x.astype(jnp.float32) for x in lives], 1),
    )


MAX_BLOCKS = 8
NOWHERE = -(SLAB_PIX * 8)
LO = 512
STEP = 32


def gather_kernel(
    counts_hbm, list_hbm, coh_hbm, pix_hbm, phases_hbm, out_ref, own_ref,
    counts_ref, list_ref, coh_ref, pix_ref, phases_ref, sems,
):
    acq_loc, local = phases_ref.shape
    pieces = local // LO
    step = min(STEP, pieces)
    inputs = [
        (counts_hbm, counts_ref), (list_hbm, list_ref), (coh_hbm, coh_ref), (pix_hbm, pix_ref)
    ]
    for start in range(0, pieces, step):
        lanes = pl.ds(start * LO, step * LO)
        inputs.append((phases_hbm.at[:, lanes], phases_ref.at[:, lanes]))
    copies = [pltpu.make_async_copy(*pair, sems.at[i]) for i, pair in enumerate(inputs)]
    for copy in copies:
        copy.start()
    for copy in copies[0:2]:
        copy.wait()
    index, tile, live = packed_rows(counts_ref[...], list_ref[...])
    packed = index.shape[1]
    low = (index & (LO - 1)) - LO // 2
    high = index >> 9
    at = (lax.broadcasted_iota(jnp.int32, (LO, packed), 0) - LO // 2).astype(jnp.float32)
    off = at.astype(jnp.bfloat16) - rows_of_bf16(low.astype(jnp.float32), LO)
    chosen = jnp.maximum(jnp.bfloat16(1) - jnp.abs(off), jnp.bfloat16(0))
    twice = jnp.concatenate([chosen, chosen], 0)
    for copy in copies[2:4]:
        copy.wait()

    def pieces_of(ref):
        split = LO // LANES
        return jnp.concatenate([ref[pl.ds(k, pieces, stride=split), :] for k in range(split)], 1)

    pix = pieces_of(pix_ref)
    table = jnp.concatenate(
        [
            jnp.concatenate(split_bf16(pieces_of(coh_ref)), 1),
            jnp.concatenate(
                [
                    ((pix >> 6) << 6).astype(jnp.float32).astype(jnp.bfloat16),
                    (pix & 63).astype(jnp.float32).astype(jnp.bfloat16),
                ],
                1,
            ),
        ],
        0,
    )
    columns = dot_f32(table, twice, NN)
    row_is = lax.broadcasted_iota(jnp.int32, (pieces, packed), 0) == high

    def pick(k):
        part = columns[k * pieces : (k + 1) * pieces]
        return jnp.sum(jnp.where(row_is, part, 0.0), axis=0, keepdims=True)

    weight = pick(0) * live
    pixel = pick(1) + tile.astype(jnp.float32) * float(SLAB_PIX)
    pixel = jnp.where(live > 0.0, pixel, float(NOWHERE))
    out_ref[:, packed:] = jnp.zeros((acq_loc, LANES), jnp.float32)
    for b in range(packed // LANES):
        cut = slice(b * LANES, (b + 1) * LANES)
        out_ref[b : b + 1, packed:] = weight[:, cut]
        out_ref[MAX_BLOCKS + b : MAX_BLOCKS + b + 1, packed:] = pixel[:, cut]
    own = jnp.zeros((acq_loc, packed), jnp.float32)
    for start in range(0, pieces, step):
        copies[4 + start // step].wait()
        block = jnp.concatenate(
            [phases_ref[:, h * LO : (h + 1) * LO] for h in range(start, start + step)], 0
        )
        both = dot_f32(jnp.concatenate(split_bf16(block), 1), twice, NN)
        for h in range(step):
            own = jnp.where(high == start + h, both[h * acq_loc : (h + 1) * acq_loc], own)
    own_ref[...] = own
    out_ref[:, 0:packed] = own * weight


def gather_call(phases, coherence, pixel_index, send_list, counts):
    acq_loc, local = phases.shape
    packed = (send_list.shape[0] // 2 + 1) * LANES
    vmem = pl.BlockSpec(memory_space=pltpu.VMEM)
    f32 = jnp.float32
    inputs = (counts, send_list, coherence.reshape(-1, LANES), pixel_index.reshape(-1, LANES), phases)
    return pl.pallas_call(
        gather_kernel,
        out_shape=(
            jax.ShapeDtypeStruct((acq_loc, packed + LANES), f32),
            jax.ShapeDtypeStruct((acq_loc, packed), f32),
        ),
        in_specs=[pl.BlockSpec(memory_space=pl.ANY)] * len(inputs),
        out_specs=(vmem, vmem),
        scratch_shapes=[pltpu.VMEM(x.shape, x.dtype) for x in inputs]
        + [pltpu.SemaphoreType.DMA((4 + max(local // (LO * STEP), 1),))],
        compiler_params=pltpu.CompilerParams(vmem_limit_bytes=12 << 20),
        name="gather_slots",
    )(*[pltpu.with_memory_space_constraint(x, pltpu.HBM) for x in inputs])


def filter_dot(weights, series):
    return lax.dot_general(
        weights,
        series,
        (((0,), (0,)), ((), ())),
        precision=lax.Precision.HIGHEST,
        preferred_element_type=jnp.float32,
    )


def down_lanes(row):
    return jnp.transpose(jnp.broadcast_to(row, (LANES, LANES)))


def filter_own_kernel(n_acq, band_ref, part_ref, out_ref, h_ref, down_ref):
    acq_loc, lanes = part_ref.shape
    packed = lanes - LANES
    me = lax.axis_index("acq")
    band = band_ref[:, 0:acq_loc]
    for a in range(1, n_acq):
        band = jnp.where(me == a, band_ref[:, a * acq_loc : (a + 1) * acq_loc], band)
    mine = me * acq_loc + lax.broadcasted_iota(jnp.int32, (1, acq_loc), 1)
    lower = jnp.maximum(mine - band, 0)
    upper = jnp.minimum(mine + band, ACQ - 1)
    share = 1.0 / (upper - lower + 1).astype(jnp.float32)
    for k in range(n_acq):
        source = (me ^ k) * acq_loc + lax.broadcasted_iota(jnp.int32, (acq_loc, acq_loc), 0)
        inside = (source >= lower) & (source <= upper)
        unit = jnp.where(source == mine, 1.0, 0.0)
        h_ref[k * acq_loc : (k + 1) * acq_loc, :] = unit - jnp.where(inside, share, 0.0)
    out_ref[:, 0:packed] = filter_dot(h_ref[0:acq_loc, :], part_ref[:, 0:packed])
    out_ref[:, packed:] = part_ref[:, packed:]
    for b in range(packed // LANES):
        pixel = part_ref[MAX_BLOCKS + b : MAX_BLOCKS + b + 1, packed:]
        row, col = split_pixel(pixel)
        for k, value in enumerate((row, *split_column(col))):
            down_ref[k, b * LANES : (b + 1) * LANES, :] = down_lanes(value)


def filter_kernel(h_ref, begun_ref, *refs):
    *parts, out_ref = refs
    acq_loc, lanes = begun_ref.shape
    packed = lanes - LANES
    series = jnp.concatenate([part[:, 0:packed] for part in parts], 0)
    out_ref[:, 0:packed] = begun_ref[:, 0:packed] + filter_dot(h_ref[acq_loc:, :], series)
    out_ref[:, packed:] = begun_ref[:, packed:]


def first_pair(tile, n_pair):
    return jnp.clip((tile + 1) // 2 - 1, 0, max(n_pair - 2, 0))


def hat(distance):
    return jnp.maximum(float(RADIUS + 1) - jnp.abs(distance), 0.0)


def hat_bf16(distance):
    return jnp.maximum(jnp.bfloat16(RADIUS + 1) - jnp.abs(distance), jnp.bfloat16(0))


def split_pixel(pixel):
    whole = pixel.astype(jnp.int32)
    return (whole >> 10).astype(jnp.float32), (whole & (COLS - 1)).astype(jnp.float32)


def split_column(col):
    coarse = jnp.floor(col * 0.125) * 8.0
    return coarse, col - coarse


CHUNK = 256


def screen_kernel(n_tile, begins, ends, *refs):
    all_ref, mine_ref, down_ref = refs[:3]
    refs = refs[3:]
    if not begins:
        image_in, samples_in = refs[:2]
        refs = refs[2:]
    if ends:
        own_ref, screen_ref, residual_ref = refs[:3]
        refs = refs[3:]
    else:
        image_out, samples_out = refs[:2]
        refs = refs[2:]
    tag_ref, few_ref, value_ref, lhs_ref, made_ref, rest_ref, made_sem = refs
    n_src, acq_loc, packed = all_ref.shape
    packed -= LANES
    n_pair = n_tile // 2
    width = 3 * LANES
    limit = min_weight * float((RADIUS + 1) ** 4)
    me = lax.axis_index("tile")
    f32, bf16 = jnp.float32, jnp.bfloat16

    def starts(pair):
        start = pl.multiple_of(pair * LANES, LANES)
        return [start, pl.multiple_of(start + LANES, LANES), n_pair * LANES]

    def tags(src, pair):
        blocks = [tag_ref[src, 0:3, pl.ds(s, LANES)] for s in starts(pair)]
        every = jnp.concatenate(blocks, 1)
        return every[0:1], every[1:2], every[2:3]

    sub = lax.broadcasted_iota(jnp.int32, (16, LANES), 0)
    for src in range(n_src):
        value_hi, value_lo = split_bf16(all_ref[src, :, 0:packed])
        value_ref[src, 0:acq_loc, :] = value_hi
        value_ref[src, acq_loc : 2 * acq_loc, :] = value_lo
        for b in range(n_pair + 1):
            lanes = slice(b * LANES, (b + 1) * LANES)
            row, col = split_pixel(all_ref[src, MAX_BLOCKS + b : MAX_BLOCKS + b + 1, packed:])
            weight = all_ref[src, b : b + 1, packed:]
            tag_ref[src, 0:1, lanes] = weight
            tag_ref[src, 1:2, lanes] = row
            tag_ref[src, 2:3, lanes] = col
            for k, value in enumerate((row, *split_column(col))):
                few_ref[src, k, :, lanes] = rows_of_bf16(value, 16)
            w_hi = weight.astype(bf16).astype(f32)
            both = jnp.where(sub == 0, w_hi, jnp.where(sub == 1, weight - w_hi, 0.0))
            value_ref[src, 2 * acq_loc :, lanes] = both.astype(bf16)

    top = (me * ROWS_DEV).astype(f32)
    row_at = lax.broadcasted_iota(jnp.int32, (ROWS_DEV, width), 0).astype(f32) + top
    col_at = lax.broadcasted_iota(jnp.int32, (CHUNK, width), 0) - CHUNK // 2
    col_at = col_at.astype(f32).astype(bf16)
    pair = first_pair(me, n_pair)
    n_img = acq_loc * ROWS_DEV
    for src in range(n_src):
        weight, row, col = tags(src, pair)
        across = hat(row_at - row)
        lanes = slice(src * width, (src + 1) * width)
        data = jnp.concatenate([all_ref[src, :, pl.ds(s, LANES)] for s in starts(pair)], 1)
        part = jnp.concatenate([across * data[a : a + 1] for a in range(acq_loc)], 0)
        part_hi, part_lo = split_bf16(part)
        lhs_ref[0:n_img, lanes] = part_hi
        lhs_ref[n_img : 2 * n_img, lanes] = part_lo
        w_part = across * weight
        w_hi = w_part.astype(bf16).astype(f32)
        lhs_ref[2 * n_img :, lanes] = jnp.concatenate([w_hi, w_part - w_hi], 0).astype(bf16)

    def pair_hats(start):
        slots = slice(start, start + HALF)
        near = range(n_pair + 1)
        if start < n_pair * LANES:
            tile = start // HALF
            near = {(tile - 1) // 2, tile // 2, (tile + 1) // 2, n_pair}
        blocks = []
        row_i, coarse_i, fine_i = (down_ref[k, slots, :].astype(bf16) for k in range(3))
        for src in range(n_src):
            for b in range(n_pair + 1):
                if b not in near:
                    blocks.append(jnp.zeros((HALF, LANES), bf16))
                    continue
                cut = slice(b * LANES, (b + 1) * LANES)
                row, coarse, fine = (
                    jnp.concatenate([few_ref[src, k, :, cut]] * (HALF // 16), 0) for k in range(3)
                )
                across = (coarse_i - coarse) + (fine_i - fine)
                blocks.append(hat_bf16(row_i - row) * hat_bf16(across))

        return jnp.concatenate(blocks, 1)

    def sample():
        pairs = jnp.concatenate([pair_hats(at) for at in range(0, packed, HALF)], 0)
        values = jnp.concatenate([value_ref[src] for src in range(n_src)], 1)
        got = dot_f32(values, pairs, NT)
        total = got[0:acq_loc] + got[acq_loc : 2 * acq_loc]
        below = got[2 * acq_loc : 2 * acq_loc + 8]
        return jnp.concatenate([total, below], 0)

    def slab(c):
        cols = []
        for src in range(n_src):
            _, _, col = tags(src, pair)
            near = jnp.clip(col - float(c + CHUNK // 2), -160.0, 160.0)
            cols.append(hat_bf16(col_at - rows_of_bf16(near, CHUNK)))
        got = dot_f32(lhs_ref[...], jnp.concatenate(cols, 1), NT)
        return jnp.concatenate(
            [
                got[0:n_img] + got[n_img : 2 * n_img],
                got[2 * n_img : 2 * n_img + ROWS_DEV] + got[2 * n_img + ROWS_DEV :],
            ],
            0,
        )

    copies = []
    for c in range(0, COLS, CHUNK):
        image = slab(c)
        lanes = slice(c, c + CHUNK)
        if not begins:
            image = image + image_in[:, lanes]
        if not ends:
            image_out[:, lanes] = image
            continue
        scale = 1.0 / jnp.maximum(image[n_img:], limit)
        for a in range(acq_loc):
            made_ref[a, :, lanes] = image[a * ROWS_DEV : (a + 1) * ROWS_DEV] * scale
        copies.append(
            pltpu.make_async_copy(
                made_ref.at[:, :, lanes], screen_ref.at[:, :, lanes], made_sem.at[c // CHUNK]
            )
        )
        copies[-1].start()
    samples = sample()
    if not begins:
        samples = samples + samples_in[...]
    if not ends:
        samples_out[...] = samples
        return
    below = samples[acq_loc : acq_loc + 1] + samples[acq_loc + 1 : acq_loc + 2]
    rest = own_ref[...] - samples[0:acq_loc] * (1.0 / jnp.maximum(below, limit))

    lower = lax.broadcasted_iota(jnp.int32, (1, LANES), 1) < HALF
    tiles = [
        mine_ref[MAX_BLOCKS + b : MAX_BLOCKS + b + 1, packed:].astype(jnp.int32) >> SLAB_SHIFT
        for b in range(n_pair + 1)
    ]
    heavy = rest[:, n_pair * LANES :]
    turned = pltpu.roll(heavy, HALF, 1)
    tile_turned = pltpu.roll(tiles[n_pair], HALF, 1)
    for t in range(n_tile):
        near = rest[:, (t // 2) * LANES : (t // 2 + 1) * LANES]
        tile_near = tiles[t // 2]
        if t % 2:
            near = pltpu.roll(near, HALF, 1)
            tile_near = pltpu.roll(tile_near, HALF, 1)
        far = jnp.where(tile_turned == t, turned, jnp.where(tiles[n_pair] == t, heavy, 0.0))
        rest_ref[:, t * LANES : (t + 1) * LANES] = jnp.where(
            lower, jnp.where(tile_near == t, near, 0.0), far
        )
    rest_copy = pltpu.make_async_copy(rest_ref, residual_ref, made_sem.at[COLS // CHUNK])
    copies.append(rest_copy)
    rest_copy.start()
    for copy in copies:
        copy.wait()


def add_sources(n_tile, sources, mine, down, sums, own):
    n_src, acq_loc, packed = sources.shape
    packed -= LANES
    width = n_src * 3 * LANES
    f32, bf16 = jnp.float32, jnp.bfloat16
    vmem = pl.BlockSpec(memory_space=pltpu.VMEM)
    n_lhs = 2 * (acq_loc + 1) * ROWS_DEV
    begins, ends = sums is None, own is not None
    args = [sources, mine, down]
    if not begins:
        args += list(sums)
    if ends:
        args.append(own)
        shapes = ((acq_loc, ROWS_DEV, COLS), (acq_loc, n_tile * LANES))
    else:
        shapes = ((n_lhs // 2, COLS), (acq_loc + 8, packed))
    macs = width * (n_lhs * COLS + (2 * acq_loc + 16) * packed)
    return pl.pallas_call(
        functools.partial(screen_kernel, n_tile, begins, ends),
        out_shape=tuple(jax.ShapeDtypeStruct(shape, f32) for shape in shapes),
        in_specs=[vmem] * len(args),
        out_specs=(pl.BlockSpec(memory_space=pl.ANY) if ends else vmem,) * 2,
        scratch_shapes=[
            pltpu.VMEM((n_src, 8, packed), f32),
            pltpu.VMEM((n_src, 3, 16, packed), bf16),
            pltpu.VMEM((n_src, 2 * acq_loc + 16, packed), bf16),
            pltpu.VMEM((n_lhs, width), bf16),
            pltpu.VMEM((acq_loc, ROWS_DEV, COLS), f32),
            pltpu.VMEM((acq_loc, n_tile * LANES), f32),
            pltpu.SemaphoreType.DMA((COLS // CHUNK + 1,)),
        ],
        input_output_aliases={} if begins or ends else {3: 0, 4: 1},
        cost_estimate=pl.CostEstimate(flops=2 * macs, bytes_accessed=1 << 20, transcendentals=0),
        compiler_params=pltpu.CompilerParams(vmem_limit_bytes=SCREEN_VMEM),
        name="add_sources",
    )(*args)


SCREEN_VMEM = 24 << 20


def xor_permute(x, axis, mask):
    count = lax.axis_size(axis)
    return lax.ppermute(x, axis, [(i, i ^ mask) for i in range(count)])


def gathered_shards(phases, coherence, pixel_index, send_list, counts, band_width):
    acq_loc = phases.shape[0]
    n_tile = lax.axis_size("tile")
    n_acq = lax.axis_size("acq")
    packed = (n_tile // 2 + 1) * LANES
    vmem = pl.BlockSpec(memory_space=pltpu.VMEM)
    f32 = jnp.float32
    packet, own = gather_call(phases, coherence, pixel_index, send_list, counts)
    parts = [xor_permute(packet, "acq", k) for k in range(1, n_acq)]
    packet_shape = jax.ShapeDtypeStruct((acq_loc, packed + LANES), f32)
    begun, highpass, down = pl.pallas_call(
        functools.partial(filter_own_kernel, n_acq),
        out_shape=(
            packet_shape,
            jax.ShapeDtypeStruct((n_acq * acq_loc, acq_loc), f32),
            jax.ShapeDtypeStruct((3, packed, LANES), f32),
        ),
        in_specs=[vmem] * 2,
        out_specs=(vmem,) * 3,
        cost_estimate=pl.CostEstimate(flops=1 << 20, bytes_accessed=1 << 20, transcendentals=0),
        compiler_params=pltpu.CompilerParams(vmem_limit_bytes=4 << 20),
        name="filter_own_slots",
    )(band_width.reshape(1, -1), packet)
    filtered = pl.pallas_call(
        filter_kernel,
        out_shape=packet_shape,
        in_specs=[vmem] * (n_acq + 1),
        out_specs=vmem,
        compiler_params=pltpu.CompilerParams(vmem_limit_bytes=4 << 20),
        name="filter_slots",
    )(highpass, begun, *parts)
    half = n_tile // 2
    across = xor_permute(filtered, "tile", half)
    sums = add_sources(n_tile, filtered[None], filtered, down, None, None)
    across, sums = lax.optimization_barrier((across, sums))
    held = jnp.stack([filtered, across])
    arriving = [across[None]] + [xor_permute(held, "tile", k) for k in range(1, half)]
    for sources in arriving[:-1]:
        sums = add_sources(n_tile, sources, filtered, down, sums, None)
    screen, residual = add_sources(n_tile, arriving[-1], filtered, down, sums, own)
    return residual, screen


def solution(mesh):
    n_tile = mesh.shape["tile"]
    few = n_tile in (4, 8)
    return jax.shard_map(
        gathered_shards if few else exchange_shards,
        mesh=mesh,
        in_specs=(P("acq", "tile"), P("tile"), P("tile"), P("tile", None), P("tile", None), P()),
        out_specs=(P("acq", "tile"), P("acq", "tile", None)),
        check_vma=False,
    )
```

```python
import functools

import jax
import jax.numpy as jnp
from jax import lax
from jax.experimental import pallas as pl
from jax.experimental.pallas import tpu as pltpu
from jax.sharding import PartitionSpec as P

ACQ = 64
ROWS_DEV = 8
COLS = 1024
RADIUS = 4
SLAB_PIX = 8192
SLAB_SHIFT = 13
HALF = 64
LANES = 128


min_weight = 0.1


def with_halo(cells, sides, width):
    for axis, dim in sides:
        count = lax.axis_size(axis)
        ends = count - 1
        head = lax.slice_in_dim(cells, 0, width, axis=dim)
        tail = lax.slice_in_dim(cells, cells.shape[dim] - width, cells.shape[dim], axis=dim)
        cells = jnp.concatenate(
            [
                lax.ppermute(tail, axis, [(i, (i + 1) % count) for i in range(ends)]),
                cells,
                lax.ppermute(head, axis, [((i + 1) % count, i) for i in range(ends)]),
            ],
            axis=dim,
        )
    return cells


def temporal_matrix(band_width):
    positions = jnp.arange(ACQ, dtype=jnp.int32)
    lower = jnp.maximum(positions - band_width, 0)
    upper = jnp.minimum(positions + band_width, ACQ - 1)
    inside = (positions[None, :] >= lower[:, None]) & (positions[None, :] <= upper[:, None])
    window = (upper - lower + 1).astype(jnp.float32)
    return jnp.eye(ACQ, dtype=jnp.float32) - inside.astype(jnp.float32) / window[:, None]


def kernel_weights():
    return [
        (RADIUS + 1 - abs(offset - RADIUS)) / float((RADIUS + 1) ** 2)
        for offset in range(2 * RADIUS + 1)
    ]


def smooth(padded_rows):
    weights = kernel_weights()
    row_count = padded_rows.shape[-2] - 2 * RADIUS
    vertical = weights[0] * padded_rows[..., 0:row_count, :]
    for offset in range(1, 2 * RADIUS + 1):
        vertical = vertical + weights[offset] * padded_rows[..., offset : offset + row_count, :]
    column_count = vertical.shape[-1]
    pad_width = [(0, 0)] * (vertical.ndim - 1) + [(RADIUS, RADIUS)]
    widened = jnp.pad(vertical, pad_width)
    total = weights[0] * widened[..., 0:column_count]
    for offset in range(1, 2 * RADIUS + 1):
        total = total + weights[offset] * widened[..., offset : offset + column_count]
    return total


def apply_highpass(highpass, series):
    return jnp.dot(
        highpass, series, precision=lax.Precision.HIGHEST, preferred_element_type=jnp.float32
    )


def exchange_shards(phases, coherence, pixel_index, send_list, counts, band_width):
    acq_loc = phases.shape[0]
    capacity = send_list.shape[1]
    highpass = temporal_matrix(band_width)
    live_slot = jnp.arange(capacity, dtype=jnp.int32)[None, :] < counts[0][:, None]
    slot_weight = jnp.where(live_slot, coherence[send_list], jnp.float32(0.0))
    slot_pixel = pixel_index[send_list]
    outgoing = phases[:, send_list] * slot_weight[None]
    arrived, arrived_weight, arrived_pixel = (
        lax.all_to_all(outgoing, "tile", split_axis=1, concat_axis=1, tiled=True),
        lax.all_to_all(slot_weight[None], "tile", split_axis=1, concat_axis=1, tiled=True),
        lax.all_to_all(slot_pixel[None], "tile", split_axis=1, concat_axis=1, tiled=True),
    )
    targets = arrived_pixel.reshape(-1)
    phase_image = (
        jnp.zeros((acq_loc, SLAB_PIX), jnp.float32).at[:, targets].add(arrived.reshape(acq_loc, -1))
    )
    weight_sum = jnp.zeros((SLAB_PIX,), jnp.float32).at[targets].add(arrived_weight.reshape(-1))
    series = lax.all_to_all(phase_image, "acq", split_axis=1, concat_axis=0, tiled=True)
    phase_image = lax.all_to_all(
        apply_highpass(highpass, series), "acq", split_axis=0, concat_axis=1, tiled=True
    )
    stacked = jnp.concatenate([phase_image, weight_sum[None, :]], axis=0).reshape(
        acq_loc + 1, ROWS_DEV, COLS
    )
    padded = with_halo(stacked, (("tile", 1),), RADIUS)
    smoothed = smooth(padded)
    screen = smoothed[:acq_loc] / jnp.maximum(smoothed[acq_loc], min_weight)
    flattened = screen.reshape(acq_loc, SLAB_PIX)
    sampled = flattened[:, arrived_pixel[0]]
    returned = lax.all_to_all(sampled, "tile", split_axis=1, concat_axis=1, tiled=True)
    residual = jnp.where(live_slot[None], phases[:, send_list] - returned, jnp.float32(0.0))
    return (residual.reshape(acq_loc, -1), screen)


def split_bf16(x):
    high = x.astype(jnp.bfloat16)
    return high, (x - high.astype(jnp.float32)).astype(jnp.bfloat16)


def rows_of_bf16(row, count):
    few = jnp.broadcast_to(row, (16, row.shape[1])).astype(jnp.bfloat16)
    return jnp.concatenate([few] * (count // 16), 0)


def dot_f32(a, b, dims):
    return lax.dot_general(a, b, (dims, ((), ())), preferred_element_type=jnp.float32)


NN = ((1,), (0,))
NT = ((1,), (1,))


def packed_rows(counts, lists):
    n_tile = counts.shape[1]
    at = lax.broadcasted_iota(jnp.int32, counts.shape, 1).astype(jnp.float32)
    heavy = counts >= HALF
    first = jnp.min(jnp.where(heavy, at, float(n_tile - 1)), axis=1, keepdims=True)
    last = jnp.max(jnp.where(heavy, at, 0.0), axis=1, keepdims=True)
    lane = lax.broadcasted_iota(jnp.int32, (1, LANES), 1)
    lower = lane < HALF
    slot = lane & (HALF - 1)

    def halves(low, high):
        return jnp.where(lower, jnp.broadcast_to(low, lower.shape), jnp.broadcast_to(high, lower.shape))

    def count_of(t):
        return counts[:, t : t + 1]

    indices, tiles, lives = [], [], []
    for t in range(0, n_tile, 2):
        odd = pltpu.roll(lists[t + 1 : t + 2], HALF, 1)
        indices.append(jnp.where(lower, lists[t : t + 1], odd))
        tiles.append(jnp.where(lower, t, t + 1))
        lives.append(slot < halves(count_of(t), count_of(t + 1)))
    early, late = lists[0:1], lists[0:1]
    early_count, late_count = count_of(0), count_of(0)
    for t in range(1, n_tile):
        row = lists[t : t + 1]
        early = jnp.where(jnp.broadcast_to(first == t, row.shape), row, early)
        late = jnp.where(jnp.broadcast_to(last == t, row.shape), row, late)
        early_count = jnp.where(first == t, count_of(t), early_count)
        late_count = jnp.where(last == t, count_of(t), late_count)
    late_count = jnp.where(first == last, 0, late_count)
    indices.append(jnp.where(lower, pltpu.roll(early, HALF, 1), late))
    tiles.append(halves(first, last).astype(jnp.int32))
    lives.append(slot + HALF < halves(early_count, late_count))
    return (
        jnp.concatenate(indices, 1),
        jnp.concatenate(tiles, 1),
        jnp.concatenate([x.astype(jnp.float32) for x in lives], 1),
    )


MAX_BLOCKS = 8
NOWHERE = -(SLAB_PIX * 8)
LO = 512
STEP = 32


def gather_kernel(
    counts_hbm, list_hbm, coh_hbm, pix_hbm, phases_hbm, out_ref, own_ref,
    counts_ref, list_ref, coh_ref, pix_ref, phases_ref, sems,
):
    acq_loc, local = phases_ref.shape
    pieces = local // LO
    step = min(STEP, pieces)
    inputs = [
        (counts_hbm, counts_ref), (list_hbm, list_ref), (coh_hbm, coh_ref), (pix_hbm, pix_ref)
    ]
    for start in range(0, pieces, step):
        lanes = pl.ds(start * LO, step * LO)
        inputs.append((phases_hbm.at[:, lanes], phases_ref.at[:, lanes]))
    copies = [pltpu.make_async_copy(*pair, sems.at[i]) for i, pair in enumerate(inputs)]
    for copy in copies:
        copy.start()
    for copy in copies[0:2]:
        copy.wait()
    index, tile, live = packed_rows(counts_ref[...], list_ref[...])
    packed = index.shape[1]
    low = (index & (LO - 1)) - LO // 2
    high = index >> 9
    at = (lax.broadcasted_iota(jnp.int32, (LO, packed), 0) - LO // 2).astype(jnp.float32)
    off = at.astype(jnp.bfloat16) - rows_of_bf16(low.astype(jnp.float32), LO)
    chosen = jnp.maximum(jnp.bfloat16(1) - jnp.abs(off), jnp.bfloat16(0))
    twice = jnp.concatenate([chosen, chosen], 0)
    for copy in copies[2:4]:
        copy.wait()

    def pieces_of(ref):
        split = LO // LANES
        return jnp.concatenate([ref[pl.ds(k, pieces, stride=split), :] for k in range(split)], 1)

    pix = pieces_of(pix_ref)
    table = jnp.concatenate(
        [
            jnp.concatenate(split_bf16(pieces_of(coh_ref)), 1),
            jnp.concatenate(
                [
                    ((pix >> 6) << 6).astype(jnp.float32).astype(jnp.bfloat16),
                    (pix & 63).astype(jnp.float32).astype(jnp.bfloat16),
                ],
                1,
            ),
        ],
        0,
    )
    columns = dot_f32(table, twice, NN)
    row_is = lax.broadcasted_iota(jnp.int32, (pieces, packed), 0) == high

    def pick(k):
        part = columns[k * pieces : (k + 1) * pieces]
        return jnp.sum(jnp.where(row_is, part, 0.0), axis=0, keepdims=True)

    weight = pick(0) * live
    pixel = pick(1) + tile.astype(jnp.float32) * float(SLAB_PIX)
    pixel = jnp.where(live > 0.0, pixel, float(NOWHERE))
    out_ref[:, packed:] = jnp.zeros((acq_loc, LANES), jnp.float32)
    for b in range(packed // LANES):
        cut = slice(b * LANES, (b + 1) * LANES)
        out_ref[b : b + 1, packed:] = weight[:, cut]
        out_ref[MAX_BLOCKS + b : MAX_BLOCKS + b + 1, packed:] = pixel[:, cut]
    own = jnp.zeros((acq_loc, packed), jnp.float32)
    for start in range(0, pieces, step):
        copies[4 + start // step].wait()
        block = jnp.concatenate(
            [phases_ref[:, h * LO : (h + 1) * LO] for h in range(start, start + step)], 0
        )
        both = dot_f32(jnp.concatenate(split_bf16(block), 1), twice, NN)
        for h in range(step):
            own = jnp.where(high == start + h, both[h * acq_loc : (h + 1) * acq_loc], own)
    own_ref[...] = own
    out_ref[:, 0:packed] = own * weight


def gather_call(phases, coherence, pixel_index, send_list, counts):
    acq_loc, local = phases.shape
    packed = (send_list.shape[0] // 2 + 1) * LANES
    vmem = pl.BlockSpec(memory_space=pltpu.VMEM)
    f32 = jnp.float32
    inputs = (counts, send_list, coherence.reshape(-1, LANES), pixel_index.reshape(-1, LANES), phases)
    return pl.pallas_call(
        gather_kernel,
        out_shape=(
            jax.ShapeDtypeStruct((acq_loc, packed + LANES), f32),
            jax.ShapeDtypeStruct((acq_loc, packed), f32),
        ),
        in_specs=[pl.BlockSpec(memory_space=pl.ANY)] * len(inputs),
        out_specs=(vmem, vmem),
        scratch_shapes=[pltpu.VMEM(x.shape, x.dtype) for x in inputs]
        + [pltpu.SemaphoreType.DMA((4 + max(local // (LO * STEP), 1),))],
        compiler_params=pltpu.CompilerParams(vmem_limit_bytes=12 << 20),
        name="gather_slots",
    )(*[pltpu.with_memory_space_constraint(x, pltpu.HBM) for x in inputs])


def filter_dot(weights, series):
    return lax.dot_general(
        weights,
        series,
        (((0,), (0,)), ((), ())),
        precision=lax.Precision.HIGHEST,
        preferred_element_type=jnp.float32,
    )


def down_lanes(row):
    return jnp.transpose(jnp.broadcast_to(row, (LANES, LANES)))


def filter_own_kernel(n_acq, band_ref, part_ref, out_ref, h_ref, down_ref):
    acq_loc, lanes = part_ref.shape
    packed = lanes - LANES
    me = lax.axis_index("acq")
    band = band_ref[:, 0:acq_loc]
    for a in range(1, n_acq):
        band = jnp.where(me == a, band_ref[:, a * acq_loc : (a + 1) * acq_loc], band)
    mine = me * acq_loc + lax.broadcasted_iota(jnp.int32, (1, acq_loc), 1)
    lower = jnp.maximum(mine - band, 0)
    upper = jnp.minimum(mine + band, ACQ - 1)
    share = 1.0 / (upper - lower + 1).astype(jnp.float32)
    for k in range(n_acq):
        source = (me ^ k) * acq_loc + lax.broadcasted_iota(jnp.int32, (acq_loc, acq_loc), 0)
        inside = (source >= lower) & (source <= upper)
        unit = jnp.where(source == mine, 1.0, 0.0)
        h_ref[k * acq_loc : (k + 1) * acq_loc, :] = unit - jnp.where(inside, share, 0.0)
    out_ref[:, 0:packed] = filter_dot(h_ref[0:acq_loc, :], part_ref[:, 0:packed])
    out_ref[:, packed:] = part_ref[:, packed:]
    for b in range(packed // LANES):
        pixel = part_ref[MAX_BLOCKS + b : MAX_BLOCKS + b + 1, packed:]
        row, col = split_pixel(pixel)
        for k, value in enumerate((row, *split_column(col))):
            down_ref[k, b * LANES : (b + 1) * LANES, :] = down_lanes(value)


def filter_kernel(h_ref, begun_ref, *refs):
    *parts, out_ref = refs
    acq_loc, lanes = begun_ref.shape
    packed = lanes - LANES
    series = jnp.concatenate([part[:, 0:packed] for part in parts], 0)
    out_ref[:, 0:packed] = begun_ref[:, 0:packed] + filter_dot(h_ref[acq_loc:, :], series)
    out_ref[:, packed:] = begun_ref[:, packed:]


def first_pair(tile, n_pair):
    return jnp.clip((tile + 1) // 2 - 1, 0, max(n_pair - 2, 0))


def hat(distance):
    return jnp.maximum(float(RADIUS + 1) - jnp.abs(distance), 0.0)


def hat_bf16(distance):
    return jnp.maximum(jnp.bfloat16(RADIUS + 1) - jnp.abs(distance), jnp.bfloat16(0))


def split_pixel(pixel):
    whole = pixel.astype(jnp.int32)
    return (whole >> 10).astype(jnp.float32), (whole & (COLS - 1)).astype(jnp.float32)


def split_column(col):
    coarse = jnp.floor(col * 0.125) * 8.0
    return coarse, col - coarse


CHUNK = 256


def screen_kernel(n_tile, begins, ends, *refs):
    all_ref, mine_ref, down_ref = refs[:3]
    refs = refs[3:]
    if not begins:
        image_in, samples_in = refs[:2]
        refs = refs[2:]
    if ends:
        own_ref, screen_ref, residual_ref = refs[:3]
        refs = refs[3:]
    else:
        image_out, samples_out = refs[:2]
        refs = refs[2:]
    tag_ref, few_ref, value_ref, lhs_ref, made_ref, rest_ref, made_sem = refs
    n_src, acq_loc, packed = all_ref.shape
    packed -= LANES
    n_pair = n_tile // 2
    width = 3 * LANES
    limit = min_weight * float((RADIUS + 1) ** 4)
    me = lax.axis_index("tile")
    f32, bf16 = jnp.float32, jnp.bfloat16

    def starts(pair):
        start = pl.multiple_of(pair * LANES, LANES)
        return [start, pl.multiple_of(start + LANES, LANES), n_pair * LANES]

    def tags(src, pair):
        blocks = [tag_ref[src, 0:3, pl.ds(s, LANES)] for s in starts(pair)]
        every = jnp.concatenate(blocks, 1)
        return every[0:1], every[1:2], every[2:3]

    sub = lax.broadcasted_iota(jnp.int32, (16, LANES), 0)
    for src in range(n_src):
        value_hi, value_lo = split_bf16(all_ref[src, :, 0:packed])
        value_ref[src, 0:acq_loc, :] = value_hi
        value_ref[src, acq_loc : 2 * acq_loc, :] = value_lo
        for b in range(n_pair + 1):
            lanes = slice(b * LANES, (b + 1) * LANES)
            row, col = split_pixel(all_ref[src, MAX_BLOCKS + b : MAX_BLOCKS + b + 1, packed:])
            weight = all_ref[src, b : b + 1, packed:]
            tag_ref[src, 0:1, lanes] = weight
            tag_ref[src, 1:2, lanes] = row
            tag_ref[src, 2:3, lanes] = col
            for k, value in enumerate((row, *split_column(col))):
                few_ref[src, k, :, lanes] = rows_of_bf16(value, 16)
            w_hi = weight.astype(bf16).astype(f32)
            both = jnp.where(sub == 0, w_hi, jnp.where(sub == 1, weight - w_hi, 0.0))
            value_ref[src, 2 * acq_loc :, lanes] = both.astype(bf16)

    top = (me * ROWS_DEV).astype(f32)
    row_at = lax.broadcasted_iota(jnp.int32, (ROWS_DEV, width), 0).astype(f32) + top
    col_at = lax.broadcasted_iota(jnp.int32, (CHUNK, width), 0) - CHUNK // 2
    col_at = col_at.astype(f32).astype(bf16)
    pair = first_pair(me, n_pair)
    n_img = acq_loc * ROWS_DEV
    for src in range(n_src):
        weight, row, col = tags(src, pair)
        across = hat(row_at - row)
        lanes = slice(src * width, (src + 1) * width)
        data = jnp.concatenate([all_ref[src, :, pl.ds(s, LANES)] for s in starts(pair)], 1)
        part = jnp.concatenate([across * data[a : a + 1] for a in range(acq_loc)], 0)
        part_hi, part_lo = split_bf16(part)
        lhs_ref[0:n_img, lanes] = part_hi
        lhs_ref[n_img : 2 * n_img, lanes] = part_lo
        w_part = across * weight
        w_hi = w_part.astype(bf16).astype(f32)
        lhs_ref[2 * n_img :, lanes] = jnp.concatenate([w_hi, w_part - w_hi], 0).astype(bf16)

    def pair_hats(start, columns):
        slots = slice(start, start + HALF)
        near = columns
        if start < n_pair * LANES:
            tile = start // HALF
            near = {(tile - 1) // 2, tile // 2, (tile + 1) // 2, n_pair}
        row_i, coarse_i, fine_i = (down_ref[k, slots, :].astype(bf16) for k in range(3))
        blocks = []
        for src in range(n_src):
            for b in columns:
                if b not in near:
                    blocks.append(jnp.zeros((HALF, LANES), bf16))
                    continue
                cut = slice(b * LANES, (b + 1) * LANES)
                row, coarse, fine = (
                    jnp.concatenate([few_ref[src, k, :, cut]] * (HALF // 16), 0) for k in range(3)
                )
                across = (coarse_i - coarse) + (fine_i - fine)
                blocks.append(hat_bf16(row_i - row) * hat_bf16(across))
        return jnp.concatenate(blocks, 1)

    def sample():
        every = list(range(n_pair + 1))
        parts = []
        for i in range(0, n_pair + 1, 2):
            if i < n_pair:
                columns = list(range(max(i - 1, 0), min(i + 3, n_pair))) + [n_pair]
                stop = min(i + 2, n_pair)
            else:
                columns, stop = every, i + 1
            starts = range(i * LANES, stop * LANES, HALF)
            pairs = jnp.concatenate([pair_hats(start, columns) for start in starts], 0)
            values = jnp.concatenate(
                [
                    value_ref[src, :, b * LANES : (b + 1) * LANES]
                    for src in range(n_src)
                    for b in columns
                ],
                1,
            )
            got = dot_f32(values, pairs, NT)
            total = got[0:acq_loc] + got[acq_loc : 2 * acq_loc]
            below = got[2 * acq_loc : 2 * acq_loc + 8]
            parts.append(jnp.concatenate([total, below], 0))
        return jnp.concatenate(parts, 1)

    def slab(c):
        cols = []
        for src in range(n_src):
            _, _, col = tags(src, pair)
            near = jnp.clip(col - float(c + CHUNK // 2), -160.0, 160.0)
            cols.append(hat_bf16(col_at - rows_of_bf16(near, CHUNK)))
        got = dot_f32(lhs_ref[...], jnp.concatenate(cols, 1), NT)
        return jnp.concatenate(
            [
                got[0:n_img] + got[n_img : 2 * n_img],
                got[2 * n_img : 2 * n_img + ROWS_DEV] + got[2 * n_img + ROWS_DEV :],
            ],
            0,
        )

    copies = []
    for c in range(0, COLS, CHUNK):
        image = slab(c)
        lanes = slice(c, c + CHUNK)
        if not begins:
            image = image + image_in[:, lanes]
        if not ends:
            image_out[:, lanes] = image
            continue
        scale = 1.0 / jnp.maximum(image[n_img:], limit)
        for a in range(acq_loc):
            made_ref[a, :, lanes] = image[a * ROWS_DEV : (a + 1) * ROWS_DEV] * scale
        copies.append(
            pltpu.make_async_copy(
                made_ref.at[:, :, lanes], screen_ref.at[:, :, lanes], made_sem.at[c // CHUNK]
            )
        )
        copies[-1].start()
    samples = sample()
    if not begins:
        samples = samples + samples_in[...]
    if not ends:
        samples_out[...] = samples
        return
    below = samples[acq_loc : acq_loc + 1] + samples[acq_loc + 1 : acq_loc + 2]
    rest = own_ref[...] - samples[0:acq_loc] * (1.0 / jnp.maximum(below, limit))

    lower = lax.broadcasted_iota(jnp.int32, (1, LANES), 1) < HALF
    tiles = [
        mine_ref[MAX_BLOCKS + b : MAX_BLOCKS + b + 1, packed:].astype(jnp.int32) >> SLAB_SHIFT
        for b in range(n_pair + 1)
    ]
    heavy = rest[:, n_pair * LANES :]
    turned = pltpu.roll(heavy, HALF, 1)
    tile_turned = pltpu.roll(tiles[n_pair], HALF, 1)
    for t in range(n_tile):
        near = rest[:, (t // 2) * LANES : (t // 2 + 1) * LANES]
        tile_near = tiles[t // 2]
        if t % 2:
            near = pltpu.roll(near, HALF, 1)
            tile_near = pltpu.roll(tile_near, HALF, 1)
        far = jnp.where(tile_turned == t, turned, jnp.where(tiles[n_pair] == t, heavy, 0.0))
        rest_ref[:, t * LANES : (t + 1) * LANES] = jnp.where(
            lower, jnp.where(tile_near == t, near, 0.0), far
        )
    rest_copy = pltpu.make_async_copy(rest_ref, residual_ref, made_sem.at[COLS // CHUNK])
    copies.append(rest_copy)
    rest_copy.start()
    for copy in copies:
        copy.wait()


def add_sources(n_tile, sources, mine, down, sums, own):
    n_src, acq_loc, packed = sources.shape
    packed -= LANES
    width = n_src * 3 * LANES
    f32, bf16 = jnp.float32, jnp.bfloat16
    vmem = pl.BlockSpec(memory_space=pltpu.VMEM)
    n_lhs = 2 * (acq_loc + 1) * ROWS_DEV
    begins, ends = sums is None, own is not None
    args = [sources, mine, down]
    if not begins:
        args += list(sums)
    if ends:
        args.append(own)
        shapes = ((acq_loc, ROWS_DEV, COLS), (acq_loc, n_tile * LANES))
    else:
        shapes = ((n_lhs // 2, COLS), (acq_loc + 8, packed))
    macs = width * (n_lhs * COLS + (2 * acq_loc + 16) * packed)
    return pl.pallas_call(
        functools.partial(screen_kernel, n_tile, begins, ends),
        out_shape=tuple(jax.ShapeDtypeStruct(shape, f32) for shape in shapes),
        in_specs=[vmem] * len(args),
        out_specs=(pl.BlockSpec(memory_space=pl.ANY) if ends else vmem,) * 2,
        scratch_shapes=[
            pltpu.VMEM((n_src, 8, packed), f32),
            pltpu.VMEM((n_src, 3, 16, packed), bf16),
            pltpu.VMEM((n_src, 2 * acq_loc + 16, packed), bf16),
            pltpu.VMEM((n_lhs, width), bf16),
            pltpu.VMEM((acq_loc, ROWS_DEV, COLS), f32),
            pltpu.VMEM((acq_loc, n_tile * LANES), f32),
            pltpu.SemaphoreType.DMA((COLS // CHUNK + 1,)),
        ],
        input_output_aliases={} if begins or ends else {3: 0, 4: 1},
        cost_estimate=pl.CostEstimate(flops=2 * macs, bytes_accessed=1 << 20, transcendentals=0),
        compiler_params=pltpu.CompilerParams(vmem_limit_bytes=SCREEN_VMEM),
        name="add_sources",
    )(*args)


SCREEN_VMEM = 24 << 20


def xor_permute(x, axis, mask):
    count = lax.axis_size(axis)
    return lax.ppermute(x, axis, [(i, i ^ mask) for i in range(count)])


def gathered_shards(phases, coherence, pixel_index, send_list, counts, band_width):
    acq_loc = phases.shape[0]
    n_tile = lax.axis_size("tile")
    n_acq = lax.axis_size("acq")
    packed = (n_tile // 2 + 1) * LANES
    vmem = pl.BlockSpec(memory_space=pltpu.VMEM)
    f32 = jnp.float32
    packet, own = gather_call(phases, coherence, pixel_index, send_list, counts)
    parts = [xor_permute(packet, "acq", k) for k in range(1, n_acq)]
    packet_shape = jax.ShapeDtypeStruct((acq_loc, packed + LANES), f32)
    begun, highpass, down = pl.pallas_call(
        functools.partial(filter_own_kernel, n_acq),
        out_shape=(
            packet_shape,
            jax.ShapeDtypeStruct((n_acq * acq_loc, acq_loc), f32),
            jax.ShapeDtypeStruct((3, packed, LANES), f32),
        ),
        in_specs=[vmem] * 2,
        out_specs=(vmem,) * 3,
        cost_estimate=pl.CostEstimate(flops=1 << 20, bytes_accessed=1 << 20, transcendentals=0),
        compiler_params=pltpu.CompilerParams(vmem_limit_bytes=4 << 20),
        name="filter_own_slots",
    )(band_width.reshape(1, -1), packet)
    filtered = pl.pallas_call(
        filter_kernel,
        out_shape=packet_shape,
        in_specs=[vmem] * (n_acq + 1),
        out_specs=vmem,
        compiler_params=pltpu.CompilerParams(vmem_limit_bytes=4 << 20),
        name="filter_slots",
    )(highpass, begun, *parts)
    half = n_tile // 2
    across = xor_permute(filtered, "tile", half)
    sums = add_sources(n_tile, filtered[None], filtered, down, None, None)
    across, sums = lax.optimization_barrier((across, sums))
    held = jnp.stack([filtered, across])
    arriving = [across[None]] + [xor_permute(held, "tile", k) for k in (2,3,1)]
    for sources in arriving[:-1]:
        sums = add_sources(n_tile, sources, filtered, down, sums, None)
    screen, residual = add_sources(n_tile, arriving[-1], filtered, down, sums, own)
    return residual, screen


def solution(mesh):
    n_tile = mesh.shape["tile"]
    few = n_tile in (4, 8)
    return jax.shard_map(
        gathered_shards if few else exchange_shards,
        mesh=mesh,
        in_specs=(P("acq", "tile"), P("tile"), P("tile"), P("tile", None), P("tile", None), P()),
        out_specs=(P("acq", "tile"), P("acq", "tile", None)),
        check_vma=False,
    )
```

```python
import functools

import jax
import jax.numpy as jnp
from jax import lax
from jax.experimental import pallas as pl
from jax.experimental.pallas import tpu as pltpu
from jax.sharding import PartitionSpec as P

ACQ = 64
ROWS_DEV = 8
COLS = 1024
RADIUS = 4
SLAB_PIX = 8192
SLAB_SHIFT = 13
HALF = 64
LANES = 128


min_weight = 0.1


def with_halo(cells, sides, width):
    for axis, dim in sides:
        count = lax.axis_size(axis)
        ends = count - 1
        head = lax.slice_in_dim(cells, 0, width, axis=dim)
        tail = lax.slice_in_dim(cells, cells.shape[dim] - width, cells.shape[dim], axis=dim)
        cells = jnp.concatenate(
            [
                lax.ppermute(tail, axis, [(i, (i + 1) % count) for i in range(ends)]),
                cells,
                lax.ppermute(head, axis, [((i + 1) % count, i) for i in range(ends)]),
            ],
            axis=dim,
        )
    return cells


def temporal_matrix(band_width):
    positions = jnp.arange(ACQ, dtype=jnp.int32)
    lower = jnp.maximum(positions - band_width, 0)
    upper = jnp.minimum(positions + band_width, ACQ - 1)
    inside = (positions[None, :] >= lower[:, None]) & (positions[None, :] <= upper[:, None])
    window = (upper - lower + 1).astype(jnp.float32)
    return jnp.eye(ACQ, dtype=jnp.float32) - inside.astype(jnp.float32) / window[:, None]


def kernel_weights():
    return [
        (RADIUS + 1 - abs(offset - RADIUS)) / float((RADIUS + 1) ** 2)
        for offset in range(2 * RADIUS + 1)
    ]


def smooth(padded_rows):
    weights = kernel_weights()
    row_count = padded_rows.shape[-2] - 2 * RADIUS
    vertical = weights[0] * padded_rows[..., 0:row_count, :]
    for offset in range(1, 2 * RADIUS + 1):
        vertical = vertical + weights[offset] * padded_rows[..., offset : offset + row_count, :]
    column_count = vertical.shape[-1]
    pad_width = [(0, 0)] * (vertical.ndim - 1) + [(RADIUS, RADIUS)]
    widened = jnp.pad(vertical, pad_width)
    total = weights[0] * widened[..., 0:column_count]
    for offset in range(1, 2 * RADIUS + 1):
        total = total + weights[offset] * widened[..., offset : offset + column_count]
    return total


def apply_highpass(highpass, series):
    return jnp.dot(
        highpass, series, precision=lax.Precision.HIGHEST, preferred_element_type=jnp.float32
    )


def exchange_shards(phases, coherence, pixel_index, send_list, counts, band_width):
    acq_loc = phases.shape[0]
    capacity = send_list.shape[1]
    highpass = temporal_matrix(band_width)
    live_slot = jnp.arange(capacity, dtype=jnp.int32)[None, :] < counts[0][:, None]
    slot_weight = jnp.where(live_slot, coherence[send_list], jnp.float32(0.0))
    slot_pixel = pixel_index[send_list]
    outgoing = phases[:, send_list] * slot_weight[None]
    arrived, arrived_weight, arrived_pixel = (
        lax.all_to_all(outgoing, "tile", split_axis=1, concat_axis=1, tiled=True),
        lax.all_to_all(slot_weight[None], "tile", split_axis=1, concat_axis=1, tiled=True),
        lax.all_to_all(slot_pixel[None], "tile", split_axis=1, concat_axis=1, tiled=True),
    )
    targets = arrived_pixel.reshape(-1)
    phase_image = (
        jnp.zeros((acq_loc, SLAB_PIX), jnp.float32).at[:, targets].add(arrived.reshape(acq_loc, -1))
    )
    weight_sum = jnp.zeros((SLAB_PIX,), jnp.float32).at[targets].add(arrived_weight.reshape(-1))
    series = lax.all_to_all(phase_image, "acq", split_axis=1, concat_axis=0, tiled=True)
    phase_image = lax.all_to_all(
        apply_highpass(highpass, series), "acq", split_axis=0, concat_axis=1, tiled=True
    )
    stacked = jnp.concatenate([phase_image, weight_sum[None, :]], axis=0).reshape(
        acq_loc + 1, ROWS_DEV, COLS
    )
    padded = with_halo(stacked, (("tile", 1),), RADIUS)
    smoothed = smooth(padded)
    screen = smoothed[:acq_loc] / jnp.maximum(smoothed[acq_loc], min_weight)
    flattened = screen.reshape(acq_loc, SLAB_PIX)
    sampled = flattened[:, arrived_pixel[0]]
    returned = lax.all_to_all(sampled, "tile", split_axis=1, concat_axis=1, tiled=True)
    residual = jnp.where(live_slot[None], phases[:, send_list] - returned, jnp.float32(0.0))
    return (residual.reshape(acq_loc, -1), screen)


def split_bf16(x):
    high = x.astype(jnp.bfloat16)
    return high, (x - high.astype(jnp.float32)).astype(jnp.bfloat16)


def rows_of_bf16(row, count):
    few = jnp.broadcast_to(row, (16, row.shape[1])).astype(jnp.bfloat16)
    return jnp.concatenate([few] * (count // 16), 0)


def dot_f32(a, b, dims):
    return lax.dot_general(a, b, (dims, ((), ())), preferred_element_type=jnp.float32)


NN = ((1,), (0,))
NT = ((1,), (1,))


def packed_rows(counts, lists):
    n_tile = counts.shape[1]
    at = lax.broadcasted_iota(jnp.int32, counts.shape, 1).astype(jnp.float32)
    heavy = counts >= HALF
    first = jnp.min(jnp.where(heavy, at, float(n_tile - 1)), axis=1, keepdims=True)
    last = jnp.max(jnp.where(heavy, at, 0.0), axis=1, keepdims=True)
    lane = lax.broadcasted_iota(jnp.int32, (1, LANES), 1)
    lower = lane < HALF
    slot = lane & (HALF - 1)

    def halves(low, high):
        return jnp.where(lower, jnp.broadcast_to(low, lower.shape), jnp.broadcast_to(high, lower.shape))

    def count_of(t):
        return counts[:, t : t + 1]

    indices, tiles, lives = [], [], []
    for t in range(0, n_tile, 2):
        odd = pltpu.roll(lists[t + 1 : t + 2], HALF, 1)
        indices.append(jnp.where(lower, lists[t : t + 1], odd))
        tiles.append(jnp.where(lower, t, t + 1))
        lives.append(slot < halves(count_of(t), count_of(t + 1)))
    early, late = lists[0:1], lists[0:1]
    early_count, late_count = count_of(0), count_of(0)
    for t in range(1, n_tile):
        row = lists[t : t + 1]
        early = jnp.where(jnp.broadcast_to(first == t, row.shape), row, early)
        late = jnp.where(jnp.broadcast_to(last == t, row.shape), row, late)
        early_count = jnp.where(first == t, count_of(t), early_count)
        late_count = jnp.where(last == t, count_of(t), late_count)
    late_count = jnp.where(first == last, 0, late_count)
    indices.append(jnp.where(lower, pltpu.roll(early, HALF, 1), late))
    tiles.append(halves(first, last).astype(jnp.int32))
    lives.append(slot + HALF < halves(early_count, late_count))
    return (
        jnp.concatenate(indices, 1),
        jnp.concatenate(tiles, 1),
        jnp.concatenate([x.astype(jnp.float32) for x in lives], 1),
    )


MAX_BLOCKS = 8
NOWHERE = -(SLAB_PIX * 8)
LO = 512
STEP = 32


def gather_kernel(
    counts_hbm, list_hbm, coh_hbm, pix_hbm, phases_hbm, out_ref, tags_ref, own_ref,
    counts_ref, list_ref, coh_ref, pix_ref, phases_ref, sems,
):
    acq_loc, local = phases_ref.shape
    pieces = local // LO
    step = min(STEP, pieces)
    inputs = [
        (counts_hbm, counts_ref), (list_hbm, list_ref), (coh_hbm, coh_ref), (pix_hbm, pix_ref)
    ]
    for start in range(0, pieces, step):
        lanes = pl.ds(start * LO, step * LO)
        inputs.append((phases_hbm.at[:, lanes], phases_ref.at[:, lanes]))
    copies = [pltpu.make_async_copy(*pair, sems.at[i]) for i, pair in enumerate(inputs)]
    for copy in copies:
        copy.start()
    for copy in copies[0:2]:
        copy.wait()
    index, tile, live = packed_rows(counts_ref[...], list_ref[...])
    packed = index.shape[1]
    low = (index & (LO - 1)) - LO // 2
    high = index >> 9
    at = (lax.broadcasted_iota(jnp.int32, (LO, packed), 0) - LO // 2).astype(jnp.float32)
    off = at.astype(jnp.bfloat16) - rows_of_bf16(low.astype(jnp.float32), LO)
    chosen = jnp.maximum(jnp.bfloat16(1) - jnp.abs(off), jnp.bfloat16(0))
    twice = jnp.concatenate([chosen, chosen], 0)
    for copy in copies[2:4]:
        copy.wait()

    def pieces_of(ref):
        split = LO // LANES
        return jnp.concatenate([ref[pl.ds(k, pieces, stride=split), :] for k in range(split)], 1)

    pix = pieces_of(pix_ref)
    table = jnp.concatenate(
        [
            jnp.concatenate(split_bf16(pieces_of(coh_ref)), 1),
            jnp.concatenate(
                [
                    ((pix >> 6) << 6).astype(jnp.float32).astype(jnp.bfloat16),
                    (pix & 63).astype(jnp.float32).astype(jnp.bfloat16),
                ],
                1,
            ),
        ],
        0,
    )
    columns = dot_f32(table, twice, NN)
    row_is = lax.broadcasted_iota(jnp.int32, (pieces, packed), 0) == high

    def pick(k):
        part = columns[k * pieces : (k + 1) * pieces]
        return jnp.sum(jnp.where(row_is, part, 0.0), axis=0, keepdims=True)

    weight = pick(0) * live
    pixel = pick(1) + tile.astype(jnp.float32) * float(SLAB_PIX)
    pixel = jnp.where(live > 0.0, pixel, float(NOWHERE))
    tags_ref[...] = jnp.zeros(tags_ref.shape, jnp.float32)
    for b in range(packed // LANES):
        cut = slice(b * LANES, (b + 1) * LANES)
        tags_ref[b : b + 1, :] = weight[:, cut]
        tags_ref[MAX_BLOCKS + b : MAX_BLOCKS + b + 1, :] = pixel[:, cut]
    own = jnp.zeros((acq_loc, packed), jnp.float32)
    for start in range(0, pieces, step):
        copies[4 + start // step].wait()
        block = jnp.concatenate(
            [phases_ref[:, h * LO : (h + 1) * LO] for h in range(start, start + step)], 0
        )
        both = dot_f32(jnp.concatenate(split_bf16(block), 1), twice, NN)
        for h in range(step):
            own = jnp.where(high == start + h, both[h * acq_loc : (h + 1) * acq_loc], own)
    own_ref[...] = own
    out_ref[...] = own * weight


def gather_call(phases, coherence, pixel_index, send_list, counts):
    acq_loc, local = phases.shape
    packed = (send_list.shape[0] // 2 + 1) * LANES
    vmem = pl.BlockSpec(memory_space=pltpu.VMEM)
    f32 = jnp.float32
    inputs = (counts, send_list, coherence.reshape(-1, LANES), pixel_index.reshape(-1, LANES), phases)
    return pl.pallas_call(
        gather_kernel,
        out_shape=(
            jax.ShapeDtypeStruct((acq_loc, packed), f32),
            jax.ShapeDtypeStruct((2 * MAX_BLOCKS, LANES), f32),
            jax.ShapeDtypeStruct((acq_loc, packed), f32),
        ),
        in_specs=[pl.BlockSpec(memory_space=pl.ANY)] * len(inputs),
        out_specs=(vmem,) * 3,
        scratch_shapes=[pltpu.VMEM(x.shape, x.dtype) for x in inputs]
        + [pltpu.SemaphoreType.DMA((4 + max(local // (LO * STEP), 1),))],
        compiler_params=pltpu.CompilerParams(vmem_limit_bytes=12 << 20),
        name="gather_slots",
    )(*[pltpu.with_memory_space_constraint(x, pltpu.HBM) for x in inputs])


def filter_dot(weights, series):
    return lax.dot_general(
        weights,
        series,
        (((0,), (0,)), ((), ())),
        precision=lax.Precision.HIGHEST,
        preferred_element_type=jnp.float32,
    )


def down_lanes(row):
    return jnp.transpose(jnp.broadcast_to(row, (LANES, LANES)))


def filter_own_kernel(n_acq, band_ref, part_ref, tags_ref, out_ref, h_ref, down_ref):
    acq_loc, packed = part_ref.shape
    me = lax.axis_index("acq")
    band = band_ref[:, 0:acq_loc]
    for a in range(1, n_acq):
        band = jnp.where(me == a, band_ref[:, a * acq_loc : (a + 1) * acq_loc], band)
    mine = me * acq_loc + lax.broadcasted_iota(jnp.int32, (1, acq_loc), 1)
    lower = jnp.maximum(mine - band, 0)
    upper = jnp.minimum(mine + band, ACQ - 1)
    share = 1.0 / (upper - lower + 1).astype(jnp.float32)
    for k in range(n_acq):
        source = (me ^ k) * acq_loc + lax.broadcasted_iota(jnp.int32, (acq_loc, acq_loc), 0)
        inside = (source >= lower) & (source <= upper)
        unit = jnp.where(source == mine, 1.0, 0.0)
        h_ref[k * acq_loc : (k + 1) * acq_loc, :] = unit - jnp.where(inside, share, 0.0)
    out_ref[:, 0:packed] = filter_dot(h_ref[0:acq_loc, :], part_ref[...])
    out_ref[:, packed:] = tags_ref[...]
    for b in range(packed // LANES):
        pixel = tags_ref[MAX_BLOCKS + b : MAX_BLOCKS + b + 1, :]
        row, col = split_pixel(pixel)
        for k, value in enumerate((row, *split_column(col))):
            down_ref[k, b * LANES : (b + 1) * LANES, :] = down_lanes(value)


def filter_kernel(h_ref, begun_ref, *refs):
    *parts, out_ref = refs
    acq_loc, lanes = begun_ref.shape
    packed = lanes - LANES
    series = jnp.concatenate([part[...] for part in parts], 0)
    out_ref[:, 0:packed] = begun_ref[:, 0:packed] + filter_dot(h_ref[acq_loc:, :], series)
    out_ref[:, packed:] = begun_ref[:, packed:]


def first_pair(tile, n_pair):
    return jnp.clip((tile + 1) // 2 - 1, 0, max(n_pair - 2, 0))


def hat(distance):
    return jnp.maximum(float(RADIUS + 1) - jnp.abs(distance), 0.0)


def hat_bf16(distance):
    return jnp.maximum(jnp.bfloat16(RADIUS + 1) - jnp.abs(distance), jnp.bfloat16(0))


def split_pixel(pixel):
    whole = pixel.astype(jnp.int32)
    return (whole >> 10).astype(jnp.float32), (whole & (COLS - 1)).astype(jnp.float32)


def split_column(col):
    coarse = jnp.floor(col * 0.125) * 8.0
    return coarse, col - coarse


CHUNK = 256


def screen_kernel(n_tile, begins, ends, *refs):
    all_ref, mine_ref, down_ref = refs[:3]
    refs = refs[3:]
    if not begins:
        image_in, samples_in = refs[:2]
        refs = refs[2:]
    if ends:
        own_ref, screen_ref, residual_ref = refs[:3]
        refs = refs[3:]
    else:
        image_out, samples_out = refs[:2]
        refs = refs[2:]
    tag_ref, few_ref, value_ref, lhs_ref, made_ref, rest_ref, made_sem = refs
    n_src, acq_loc, packed = all_ref.shape
    packed -= LANES
    n_pair = n_tile // 2
    width = 3 * LANES
    limit = min_weight * float((RADIUS + 1) ** 4)
    me = lax.axis_index("tile")
    f32, bf16 = jnp.float32, jnp.bfloat16

    def starts(pair):
        start = pl.multiple_of(pair * LANES, LANES)
        return [start, pl.multiple_of(start + LANES, LANES), n_pair * LANES]

    def tags(src, pair):
        blocks = [tag_ref[src, 0:3, pl.ds(s, LANES)] for s in starts(pair)]
        every = jnp.concatenate(blocks, 1)
        return every[0:1], every[1:2], every[2:3]

    sub = lax.broadcasted_iota(jnp.int32, (16, LANES), 0)
    for src in range(n_src):
        value_hi, value_lo = split_bf16(all_ref[src, :, 0:packed])
        value_ref[src, 0:acq_loc, :] = value_hi
        value_ref[src, acq_loc : 2 * acq_loc, :] = value_lo
        for b in range(n_pair + 1):
            lanes = slice(b * LANES, (b + 1) * LANES)
            row, col = split_pixel(all_ref[src, MAX_BLOCKS + b : MAX_BLOCKS + b + 1, packed:])
            weight = all_ref[src, b : b + 1, packed:]
            tag_ref[src, 0:1, lanes] = weight
            tag_ref[src, 1:2, lanes] = row
            tag_ref[src, 2:3, lanes] = col
            for k, value in enumerate((row, *split_column(col))):
                few_ref[src, k, :, lanes] = rows_of_bf16(value, 16)
            w_hi = weight.astype(bf16).astype(f32)
            both = jnp.where(sub == 0, w_hi, jnp.where(sub == 1, weight - w_hi, 0.0))
            value_ref[src, 2 * acq_loc :, lanes] = both.astype(bf16)

    top = (me * ROWS_DEV).astype(f32)
    row_at = lax.broadcasted_iota(jnp.int32, (ROWS_DEV, width), 0).astype(f32) + top
    col_at = lax.broadcasted_iota(jnp.int32, (CHUNK, width), 0) - CHUNK // 2
    col_at = col_at.astype(f32).astype(bf16)
    pair = first_pair(me, n_pair)
    n_img = acq_loc * ROWS_DEV
    for src in range(n_src):
        weight, row, col = tags(src, pair)
        across = hat(row_at - row)
        lanes = slice(src * width, (src + 1) * width)
        data = jnp.concatenate([all_ref[src, :, pl.ds(s, LANES)] for s in starts(pair)], 1)
        part = jnp.concatenate([across * data[a : a + 1] for a in range(acq_loc)], 0)
        part_hi, part_lo = split_bf16(part)
        lhs_ref[0:n_img, lanes] = part_hi
        lhs_ref[n_img : 2 * n_img, lanes] = part_lo
        w_part = across * weight
        w_hi = w_part.astype(bf16).astype(f32)
        lhs_ref[2 * n_img :, lanes] = jnp.concatenate([w_hi, w_part - w_hi], 0).astype(bf16)

    def pair_hats(start, columns):
        slots = slice(start, start + HALF)
        near = columns
        if start < n_pair * LANES:
            tile = start // HALF
            near = {(tile - 1) // 2, tile // 2, (tile + 1) // 2, n_pair}
        row_i, coarse_i, fine_i = (down_ref[k, slots, :].astype(bf16) for k in range(3))
        blocks = []
        for src in range(n_src):
            for b in columns:
                if b not in near:
                    blocks.append(jnp.zeros((HALF, LANES), bf16))
                    continue
                cut = slice(b * LANES, (b + 1) * LANES)
                row, coarse, fine = (
                    jnp.concatenate([few_ref[src, k, :, cut]] * (HALF // 16), 0) for k in range(3)
                )
                across = (coarse_i - coarse) + (fine_i - fine)
                blocks.append(hat_bf16(row_i - row) * hat_bf16(across))
        return jnp.concatenate(blocks, 1)

    def sample():
        every = list(range(n_pair + 1))
        parts = []
        for i in range(0, n_pair + 1, 2):
            if i < n_pair:
                columns = list(range(max(i - 1, 0), min(i + 3, n_pair))) + [n_pair]
                stop = min(i + 2, n_pair)
            else:
                columns, stop = every, i + 1
            starts = range(i * LANES, stop * LANES, HALF)
            pairs = jnp.concatenate([pair_hats(start, columns) for start in starts], 0)
            values = jnp.concatenate(
                [
                    value_ref[src, :, b * LANES : (b + 1) * LANES]
                    for src in range(n_src)
                    for b in columns
                ],
                1,
            )
            got = dot_f32(values, pairs, NT)
            total = got[0:acq_loc] + got[acq_loc : 2 * acq_loc]
            below = got[2 * acq_loc : 2 * acq_loc + 8]
            parts.append(jnp.concatenate([total, below], 0))
        return jnp.concatenate(parts, 1)

    def slab(c):
        cols = []
        for src in range(n_src):
            _, _, col = tags(src, pair)
            near = jnp.clip(col - float(c + CHUNK // 2), -160.0, 160.0)
            cols.append(hat_bf16(col_at - rows_of_bf16(near, CHUNK)))
        got = dot_f32(lhs_ref[...], jnp.concatenate(cols, 1), NT)
        return jnp.concatenate(
            [
                got[0:n_img] + got[n_img : 2 * n_img],
                got[2 * n_img : 2 * n_img + ROWS_DEV] + got[2 * n_img + ROWS_DEV :],
            ],
            0,
        )

    copies = []
    for c in range(0, COLS, CHUNK):
        image = slab(c)
        lanes = slice(c, c + CHUNK)
        if not begins:
            image = image + image_in[:, lanes]
        if not ends:
            image_out[:, lanes] = image
            continue
        scale = 1.0 / jnp.maximum(image[n_img:], limit)
        for a in range(acq_loc):
            made_ref[a, :, lanes] = image[a * ROWS_DEV : (a + 1) * ROWS_DEV] * scale
        copies.append(
            pltpu.make_async_copy(
                made_ref.at[:, :, lanes], screen_ref.at[:, :, lanes], made_sem.at[c // CHUNK]
            )
        )
        copies[-1].start()
    samples = sample()
    if not begins:
        samples = samples + samples_in[...]
    if not ends:
        samples_out[...] = samples
        return
    below = samples[acq_loc : acq_loc + 1] + samples[acq_loc + 1 : acq_loc + 2]
    rest = own_ref[...] - samples[0:acq_loc] * (1.0 / jnp.maximum(below, limit))

    lower = lax.broadcasted_iota(jnp.int32, (1, LANES), 1) < HALF
    tiles = [
        mine_ref[MAX_BLOCKS + b : MAX_BLOCKS + b + 1, packed:].astype(jnp.int32) >> SLAB_SHIFT
        for b in range(n_pair + 1)
    ]
    heavy = rest[:, n_pair * LANES :]
    turned = pltpu.roll(heavy, HALF, 1)
    tile_turned = pltpu.roll(tiles[n_pair], HALF, 1)
    for t in range(n_tile):
        near = rest[:, (t // 2) * LANES : (t // 2 + 1) * LANES]
        tile_near = tiles[t // 2]
        if t % 2:
            near = pltpu.roll(near, HALF, 1)
            tile_near = pltpu.roll(tile_near, HALF, 1)
        far = jnp.where(tile_turned == t, turned, jnp.where(tiles[n_pair] == t, heavy, 0.0))
        rest_ref[:, t * LANES : (t + 1) * LANES] = jnp.where(
            lower, jnp.where(tile_near == t, near, 0.0), far
        )
    rest_copy = pltpu.make_async_copy(rest_ref, residual_ref, made_sem.at[COLS // CHUNK])
    copies.append(rest_copy)
    rest_copy.start()
    for copy in copies:
        copy.wait()


def add_sources(n_tile, sources, mine, down, sums, own):
    n_src, acq_loc, packed = sources.shape
    packed -= LANES
    width = n_src * 3 * LANES
    f32, bf16 = jnp.float32, jnp.bfloat16
    vmem = pl.BlockSpec(memory_space=pltpu.VMEM)
    n_lhs = 2 * (acq_loc + 1) * ROWS_DEV
    begins, ends = sums is None, own is not None
    args = [sources, mine, down]
    if not begins:
        args += list(sums)
    if ends:
        args.append(own)
        shapes = ((acq_loc, ROWS_DEV, COLS), (acq_loc, n_tile * LANES))
    else:
        shapes = ((n_lhs // 2, COLS), (acq_loc + 8, packed))
    macs = width * (n_lhs * COLS + (2 * acq_loc + 16) * packed)
    return pl.pallas_call(
        functools.partial(screen_kernel, n_tile, begins, ends),
        out_shape=tuple(jax.ShapeDtypeStruct(shape, f32) for shape in shapes),
        in_specs=[vmem] * len(args),
        out_specs=(pl.BlockSpec(memory_space=pl.ANY) if ends else vmem,) * 2,
        scratch_shapes=[
            pltpu.VMEM((n_src, 8, packed), f32),
            pltpu.VMEM((n_src, 3, 16, packed), bf16),
            pltpu.VMEM((n_src, 2 * acq_loc + 16, packed), bf16),
            pltpu.VMEM((n_lhs, width), bf16),
            pltpu.VMEM((acq_loc, ROWS_DEV, COLS), f32),
            pltpu.VMEM((acq_loc, n_tile * LANES), f32),
            pltpu.SemaphoreType.DMA((COLS // CHUNK + 1,)),
        ],
        input_output_aliases={} if begins or ends else {3: 0, 4: 1},
        cost_estimate=pl.CostEstimate(flops=2 * macs, bytes_accessed=1 << 20, transcendentals=0),
        compiler_params=pltpu.CompilerParams(vmem_limit_bytes=SCREEN_VMEM),
        name="add_sources",
    )(*args)


SCREEN_VMEM = 24 << 20


def xor_permute(x, axis, mask):
    count = lax.axis_size(axis)
    return lax.ppermute(x, axis, [(i, i ^ mask) for i in range(count)])


def gathered_shards(phases, coherence, pixel_index, send_list, counts, band_width):
    acq_loc = phases.shape[0]
    n_tile = lax.axis_size("tile")
    n_acq = lax.axis_size("acq")
    packed = (n_tile // 2 + 1) * LANES
    vmem = pl.BlockSpec(memory_space=pltpu.VMEM)
    f32 = jnp.float32
    outgoing, tags, own = gather_call(phases, coherence, pixel_index, send_list, counts)
    parts = [xor_permute(outgoing, "acq", k) for k in range(1, n_acq)]
    packet_shape = jax.ShapeDtypeStruct((acq_loc, packed + LANES), f32)
    begun, highpass, down = pl.pallas_call(
        functools.partial(filter_own_kernel, n_acq),
        out_shape=(
            packet_shape,
            jax.ShapeDtypeStruct((n_acq * acq_loc, acq_loc), f32),
            jax.ShapeDtypeStruct((3, packed, LANES), f32),
        ),
        in_specs=[vmem] * 3,
        out_specs=(vmem,) * 3,
        cost_estimate=pl.CostEstimate(flops=1 << 20, bytes_accessed=1 << 20, transcendentals=0),
        compiler_params=pltpu.CompilerParams(vmem_limit_bytes=4 << 20),
        name="filter_own_slots",
    )(band_width.reshape(1, -1), outgoing, tags)
    filtered = pl.pallas_call(
        filter_kernel,
        out_shape=packet_shape,
        in_specs=[vmem] * (n_acq + 1),
        out_specs=vmem,
        compiler_params=pltpu.CompilerParams(vmem_limit_bytes=4 << 20),
        name="filter_slots",
    )(highpass, begun, *parts)
    half = n_tile // 2
    across = xor_permute(filtered, "tile", half)
    sums = add_sources(n_tile, filtered[None], filtered, down, None, None)
    across, sums = lax.optimization_barrier((across, sums))
    held = jnp.stack([filtered, across])
    order = sorted(range(1, half), key=lambda k: (k < half // 2, k))
    arriving = [across[None]] + [xor_permute(held, "tile", k) for k in order]
    for sources in arriving[:-1]:
        sums = add_sources(n_tile, sources, filtered, down, sums, None)
    screen, residual = add_sources(n_tile, arriving[-1], filtered, down, sums, own)
    return residual, screen


def solution(mesh):
    n_tile = mesh.shape["tile"]
    few = n_tile in (4, 8)
    return jax.shard_map(
        gathered_shards if few else exchange_shards,
        mesh=mesh,
        in_specs=(P("acq", "tile"), P("tile"), P("tile"), P("tile", None), P("tile", None), P()),
        out_specs=(P("acq", "tile"), P("acq", "tile", None)),
        check_vma=False,
    )
```

```python
import functools

import jax
import jax.numpy as jnp
from jax import lax
from jax.experimental import pallas as pl
from jax.experimental.pallas import tpu as pltpu
from jax.sharding import PartitionSpec as P

ACQ = 64
ROWS_DEV = 8
COLS = 1024
RADIUS = 4
SLAB_PIX = 8192
SLAB_SHIFT = 13
HALF = 64
LANES = 128


min_weight = 0.1


def with_halo(cells, sides, width):
    for axis, dim in sides:
        count = lax.axis_size(axis)
        ends = count - 1
        head = lax.slice_in_dim(cells, 0, width, axis=dim)
        tail = lax.slice_in_dim(cells, cells.shape[dim] - width, cells.shape[dim], axis=dim)
        cells = jnp.concatenate(
            [
                lax.ppermute(tail, axis, [(i, (i + 1) % count) for i in range(ends)]),
                cells,
                lax.ppermute(head, axis, [((i + 1) % count, i) for i in range(ends)]),
            ],
            axis=dim,
        )
    return cells


def temporal_matrix(band_width):
    positions = jnp.arange(ACQ, dtype=jnp.int32)
    lower = jnp.maximum(positions - band_width, 0)
    upper = jnp.minimum(positions + band_width, ACQ - 1)
    inside = (positions[None, :] >= lower[:, None]) & (positions[None, :] <= upper[:, None])
    window = (upper - lower + 1).astype(jnp.float32)
    return jnp.eye(ACQ, dtype=jnp.float32) - inside.astype(jnp.float32) / window[:, None]


def kernel_weights():
    return [
        (RADIUS + 1 - abs(offset - RADIUS)) / float((RADIUS + 1) ** 2)
        for offset in range(2 * RADIUS + 1)
    ]


def smooth(padded_rows):
    weights = kernel_weights()
    row_count = padded_rows.shape[-2] - 2 * RADIUS
    vertical = weights[0] * padded_rows[..., 0:row_count, :]
    for offset in range(1, 2 * RADIUS + 1):
        vertical = vertical + weights[offset] * padded_rows[..., offset : offset + row_count, :]
    column_count = vertical.shape[-1]
    pad_width = [(0, 0)] * (vertical.ndim - 1) + [(RADIUS, RADIUS)]
    widened = jnp.pad(vertical, pad_width)
    total = weights[0] * widened[..., 0:column_count]
    for offset in range(1, 2 * RADIUS + 1):
        total = total + weights[offset] * widened[..., offset : offset + column_count]
    return total


def apply_highpass(highpass, series):
    return jnp.dot(
        highpass, series, precision=lax.Precision.HIGHEST, preferred_element_type=jnp.float32
    )


def exchange_shards(phases, coherence, pixel_index, send_list, counts, band_width):
    acq_loc = phases.shape[0]
    capacity = send_list.shape[1]
    highpass = temporal_matrix(band_width)
    live_slot = jnp.arange(capacity, dtype=jnp.int32)[None, :] < counts[0][:, None]
    slot_weight = jnp.where(live_slot, coherence[send_list], jnp.float32(0.0))
    slot_pixel = pixel_index[send_list]
    outgoing = phases[:, send_list] * slot_weight[None]
    arrived, arrived_weight, arrived_pixel = (
        lax.all_to_all(outgoing, "tile", split_axis=1, concat_axis=1, tiled=True),
        lax.all_to_all(slot_weight[None], "tile", split_axis=1, concat_axis=1, tiled=True),
        lax.all_to_all(slot_pixel[None], "tile", split_axis=1, concat_axis=1, tiled=True),
    )
    targets = arrived_pixel.reshape(-1)
    phase_image = (
        jnp.zeros((acq_loc, SLAB_PIX), jnp.float32).at[:, targets].add(arrived.reshape(acq_loc, -1))
    )
    weight_sum = jnp.zeros((SLAB_PIX,), jnp.float32).at[targets].add(arrived_weight.reshape(-1))
    series = lax.all_to_all(phase_image, "acq", split_axis=1, concat_axis=0, tiled=True)
    phase_image = lax.all_to_all(
        apply_highpass(highpass, series), "acq", split_axis=0, concat_axis=1, tiled=True
    )
    stacked = jnp.concatenate([phase_image, weight_sum[None, :]], axis=0).reshape(
        acq_loc + 1, ROWS_DEV, COLS
    )
    padded = with_halo(stacked, (("tile", 1),), RADIUS)
    smoothed = smooth(padded)
    screen = smoothed[:acq_loc] / jnp.maximum(smoothed[acq_loc], min_weight)
    flattened = screen.reshape(acq_loc, SLAB_PIX)
    sampled = flattened[:, arrived_pixel[0]]
    returned = lax.all_to_all(sampled, "tile", split_axis=1, concat_axis=1, tiled=True)
    residual = jnp.where(live_slot[None], phases[:, send_list] - returned, jnp.float32(0.0))
    return (residual.reshape(acq_loc, -1), screen)


def split_bf16(x):
    high = x.astype(jnp.bfloat16)
    return high, (x - high.astype(jnp.float32)).astype(jnp.bfloat16)


def rows_of_bf16(row, count):
    few = jnp.broadcast_to(row, (16, row.shape[1])).astype(jnp.bfloat16)
    return jnp.concatenate([few] * (count // 16), 0)


def dot_f32(a, b, dims):
    return lax.dot_general(a, b, (dims, ((), ())), preferred_element_type=jnp.float32)


NN = ((1,), (0,))
NT = ((1,), (1,))


def packed_rows(counts, lists):
    n_tile = counts.shape[1]
    at = lax.broadcasted_iota(jnp.int32, counts.shape, 1).astype(jnp.float32)
    heavy = counts >= HALF
    first = jnp.min(jnp.where(heavy, at, float(n_tile - 1)), axis=1, keepdims=True)
    last = jnp.max(jnp.where(heavy, at, 0.0), axis=1, keepdims=True)
    lane = lax.broadcasted_iota(jnp.int32, (1, LANES), 1)
    lower = lane < HALF
    slot = lane & (HALF - 1)

    def halves(low, high):
        return jnp.where(lower, jnp.broadcast_to(low, lower.shape), jnp.broadcast_to(high, lower.shape))

    def count_of(t):
        return counts[:, t : t + 1]

    indices, tiles, lives = [], [], []
    for t in range(0, n_tile, 2):
        odd = pltpu.roll(lists[t + 1 : t + 2], HALF, 1)
        indices.append(jnp.where(lower, lists[t : t + 1], odd))
        tiles.append(jnp.where(lower, t, t + 1))
        lives.append(slot < halves(count_of(t), count_of(t + 1)))
    early, late = lists[0:1], lists[0:1]
    early_count, late_count = count_of(0), count_of(0)
    for t in range(1, n_tile):
        row = lists[t : t + 1]
        early = jnp.where(jnp.broadcast_to(first == t, row.shape), row, early)
        late = jnp.where(jnp.broadcast_to(last == t, row.shape), row, late)
        early_count = jnp.where(first == t, count_of(t), early_count)
        late_count = jnp.where(last == t, count_of(t), late_count)
    late_count = jnp.where(first == last, 0, late_count)
    indices.append(jnp.where(lower, pltpu.roll(early, HALF, 1), late))
    tiles.append(halves(first, last).astype(jnp.int32))
    lives.append(slot + HALF < halves(early_count, late_count))
    return (
        jnp.concatenate(indices, 1),
        jnp.concatenate(tiles, 1),
        jnp.concatenate([x.astype(jnp.float32) for x in lives], 1),
    )


MAX_BLOCKS = 8
NOWHERE = -(SLAB_PIX * 8)
LO = 512
STEP = 32


def gather_kernel(
    counts_hbm, list_hbm, coh_hbm, pix_hbm, phases_hbm, out_ref, tags_ref, own_ref,
    counts_ref, list_ref, coh_ref, pix_ref, phases_ref, sems,
):
    acq_loc, local = phases_ref.shape
    pieces = local // LO
    step = min(STEP, pieces)
    inputs = [
        (counts_hbm, counts_ref), (list_hbm, list_ref), (coh_hbm, coh_ref), (pix_hbm, pix_ref)
    ]
    for start in range(0, pieces, step):
        lanes = pl.ds(start * LO, step * LO)
        inputs.append((phases_hbm.at[:, lanes], phases_ref.at[:, lanes]))
    copies = [pltpu.make_async_copy(*pair, sems.at[i]) for i, pair in enumerate(inputs)]
    for copy in copies:
        copy.start()
    for copy in copies[0:2]:
        copy.wait()
    index, tile, live = packed_rows(counts_ref[...], list_ref[...])
    packed = index.shape[1]
    low = (index & (LO - 1)) - LO // 2
    high = index >> 9
    at = (lax.broadcasted_iota(jnp.int32, (LO, packed), 0) - LO // 2).astype(jnp.float32)
    off = at.astype(jnp.bfloat16) - rows_of_bf16(low.astype(jnp.float32), LO)
    chosen = jnp.maximum(jnp.bfloat16(1) - jnp.abs(off), jnp.bfloat16(0))
    twice = jnp.concatenate([chosen, chosen], 0)
    for copy in copies[2:4]:
        copy.wait()

    def pieces_of(ref):
        split = LO // LANES
        return jnp.concatenate([ref[pl.ds(k, pieces, stride=split), :] for k in range(split)], 1)

    pix = pieces_of(pix_ref)
    table = jnp.concatenate(
        [
            jnp.concatenate(split_bf16(pieces_of(coh_ref)), 1),
            jnp.concatenate(
                [
                    ((pix >> 6) << 6).astype(jnp.float32).astype(jnp.bfloat16),
                    (pix & 63).astype(jnp.float32).astype(jnp.bfloat16),
                ],
                1,
            ),
        ],
        0,
    )
    columns = dot_f32(table, twice, NN)
    row_is = lax.broadcasted_iota(jnp.int32, (pieces, packed), 0) == high

    def pick(k):
        part = columns[k * pieces : (k + 1) * pieces]
        return jnp.sum(jnp.where(row_is, part, 0.0), axis=0, keepdims=True)

    weight = pick(0) * live
    pixel = pick(1) + tile.astype(jnp.float32) * float(SLAB_PIX)
    pixel = jnp.where(live > 0.0, pixel, float(NOWHERE))
    tags_ref[...] = jnp.zeros(tags_ref.shape, jnp.float32)
    for b in range(packed // LANES):
        cut = slice(b * LANES, (b + 1) * LANES)
        tags_ref[b : b + 1, :] = weight[:, cut]
        tags_ref[MAX_BLOCKS + b : MAX_BLOCKS + b + 1, :] = pixel[:, cut]
    own = jnp.zeros((acq_loc, packed), jnp.float32)
    for start in range(0, pieces, step):
        copies[4 + start // step].wait()
        block = jnp.concatenate(
            [phases_ref[:, h * LO : (h + 1) * LO] for h in range(start, start + step)], 0
        )
        both = dot_f32(jnp.concatenate(split_bf16(block), 1), twice, NN)
        for h in range(step):
            own = jnp.where(high == start + h, both[h * acq_loc : (h + 1) * acq_loc], own)
    own_ref[...] = own
    out_ref[...] = own * weight


def gather_call(phases, coherence, pixel_index, send_list, counts):
    acq_loc, local = phases.shape
    packed = (send_list.shape[0] // 2 + 1) * LANES
    vmem = pl.BlockSpec(memory_space=pltpu.VMEM)
    f32 = jnp.float32
    inputs = (counts, send_list, coherence.reshape(-1, LANES), pixel_index.reshape(-1, LANES), phases)
    return pl.pallas_call(
        gather_kernel,
        out_shape=(
            jax.ShapeDtypeStruct((acq_loc, packed), f32),
            jax.ShapeDtypeStruct((2 * MAX_BLOCKS, LANES), f32),
            jax.ShapeDtypeStruct((acq_loc, packed), f32),
        ),
        in_specs=[pl.BlockSpec(memory_space=pl.ANY)] * len(inputs),
        out_specs=(vmem,) * 3,
        scratch_shapes=[pltpu.VMEM(x.shape, x.dtype) for x in inputs]
        + [pltpu.SemaphoreType.DMA((4 + max(local // (LO * STEP), 1),))],
        compiler_params=pltpu.CompilerParams(vmem_limit_bytes=12 << 20),
        name="gather_slots",
    )(*[pltpu.with_memory_space_constraint(x, pltpu.HBM) for x in inputs])


def filter_dot(weights, series):
    return lax.dot_general(
        weights,
        series,
        (((0,), (0,)), ((), ())),
        precision=lax.Precision.HIGHEST,
        preferred_element_type=jnp.float32,
    )


def down_lanes(row):
    return jnp.transpose(jnp.broadcast_to(row, (LANES, LANES)))


def filter_own_kernel(n_acq, band_ref, part_ref, tags_ref, out_ref, h_ref, down_ref):
    acq_loc, packed = part_ref.shape
    me = lax.axis_index("acq")
    band = band_ref[:, 0:acq_loc]
    for a in range(1, n_acq):
        band = jnp.where(me == a, band_ref[:, a * acq_loc : (a + 1) * acq_loc], band)
    mine = me * acq_loc + lax.broadcasted_iota(jnp.int32, (1, acq_loc), 1)
    lower = jnp.maximum(mine - band, 0)
    upper = jnp.minimum(mine + band, ACQ - 1)
    share = 1.0 / (upper - lower + 1).astype(jnp.float32)
    for k, part in enumerate((0, 1, 3, 2)):
        source = (me ^ part) * acq_loc + lax.broadcasted_iota(jnp.int32, (acq_loc, acq_loc), 0)
        inside = (source >= lower) & (source <= upper)
        unit = jnp.where(source == mine, 1.0, 0.0)
        h_ref[k * acq_loc : (k + 1) * acq_loc, :] = unit - jnp.where(inside, share, 0.0)
    out_ref[:, 0:packed] = filter_dot(h_ref[0:acq_loc, :], part_ref[...])
    out_ref[:, packed:] = tags_ref[...]
    for b in range(packed // LANES):
        pixel = tags_ref[MAX_BLOCKS + b : MAX_BLOCKS + b + 1, :]
        row, col = split_pixel(pixel)
        for k, value in enumerate((row, *split_column(col))):
            down_ref[k, b * LANES : (b + 1) * LANES, :] = down_lanes(value)


def filter_kernel(h_ref, begun_ref, *refs):
    *parts, out_ref = refs
    acq_loc, lanes = begun_ref.shape
    packed = lanes - LANES
    series = jnp.concatenate([part[...] for part in parts], 0)
    out_ref[:, 0:packed] = begun_ref[:, 0:packed] + filter_dot(h_ref[acq_loc:, :], series)
    out_ref[:, packed:] = begun_ref[:, packed:]


def first_pair(tile, n_pair):
    return jnp.clip((tile + 1) // 2 - 1, 0, max(n_pair - 2, 0))


def hat(distance):
    return jnp.maximum(float(RADIUS + 1) - jnp.abs(distance), 0.0)


def hat_bf16(distance):
    return jnp.maximum(jnp.bfloat16(RADIUS + 1) - jnp.abs(distance), jnp.bfloat16(0))


def split_pixel(pixel):
    whole = pixel.astype(jnp.int32)
    return (whole >> 10).astype(jnp.float32), (whole & (COLS - 1)).astype(jnp.float32)


def split_column(col):
    coarse = jnp.floor(col * 0.125) * 8.0
    return coarse, col - coarse


CHUNK = 256


def screen_kernel(n_tile, begins, ends, *refs):
    all_ref, mine_ref, down_ref = refs[:3]
    refs = refs[3:]
    if not begins:
        image_in, samples_in = refs[:2]
        refs = refs[2:]
    if ends:
        own_ref, screen_ref, residual_ref = refs[:3]
        refs = refs[3:]
    else:
        image_out, samples_out = refs[:2]
        refs = refs[2:]
    tag_ref, few_ref, value_ref, lhs_ref, made_ref, rest_ref, made_sem = refs
    n_src, acq_loc, packed = all_ref.shape
    packed -= LANES
    n_pair = n_tile // 2
    width = 3 * LANES
    limit = min_weight * float((RADIUS + 1) ** 4)
    me = lax.axis_index("tile")
    f32, bf16 = jnp.float32, jnp.bfloat16

    def starts(pair):
        start = pl.multiple_of(pair * LANES, LANES)
        return [start, pl.multiple_of(start + LANES, LANES), n_pair * LANES]

    def tags(src, pair):
        blocks = [tag_ref[src, 0:3, pl.ds(s, LANES)] for s in starts(pair)]
        every = jnp.concatenate(blocks, 1)
        return every[0:1], every[1:2], every[2:3]

    sub = lax.broadcasted_iota(jnp.int32, (16, LANES), 0)
    for src in range(n_src):
        value_hi, value_lo = split_bf16(all_ref[src, :, 0:packed])
        value_ref[src, 0:acq_loc, :] = value_hi
        value_ref[src, acq_loc : 2 * acq_loc, :] = value_lo
        for b in range(n_pair + 1):
            lanes = slice(b * LANES, (b + 1) * LANES)
            row, col = split_pixel(all_ref[src, MAX_BLOCKS + b : MAX_BLOCKS + b + 1, packed:])
            weight = all_ref[src, b : b + 1, packed:]
            tag_ref[src, 0:1, lanes] = weight
            tag_ref[src, 1:2, lanes] = row
            tag_ref[src, 2:3, lanes] = col
            for k, value in enumerate((row, *split_column(col))):
                few_ref[src, k, :, lanes] = rows_of_bf16(value, 16)
            w_hi = weight.astype(bf16).astype(f32)
            both = jnp.where(sub == 0, w_hi, jnp.where(sub == 1, weight - w_hi, 0.0))
            value_ref[src, 2 * acq_loc :, lanes] = both.astype(bf16)

    top = (me * ROWS_DEV).astype(f32)
    row_at = lax.broadcasted_iota(jnp.int32, (ROWS_DEV, width), 0).astype(f32) + top
    col_at = lax.broadcasted_iota(jnp.int32, (CHUNK, width), 0) - CHUNK // 2
    col_at = col_at.astype(f32).astype(bf16)
    pair = first_pair(me, n_pair)
    n_img = acq_loc * ROWS_DEV
    for src in range(n_src):
        weight, row, col = tags(src, pair)
        across = hat(row_at - row)
        lanes = slice(src * width, (src + 1) * width)
        data = jnp.concatenate([all_ref[src, :, pl.ds(s, LANES)] for s in starts(pair)], 1)
        part = jnp.concatenate([across * data[a : a + 1] for a in range(acq_loc)], 0)
        part_hi, part_lo = split_bf16(part)
        lhs_ref[0:n_img, lanes] = part_hi
        lhs_ref[n_img : 2 * n_img, lanes] = part_lo
        w_part = across * weight
        w_hi = w_part.astype(bf16).astype(f32)
        lhs_ref[2 * n_img :, lanes] = jnp.concatenate([w_hi, w_part - w_hi], 0).astype(bf16)

    def pair_hats(start, columns):
        slots = slice(start, start + HALF)
        near = columns
        if start < n_pair * LANES:
            tile = start // HALF
            near = {(tile - 1) // 2, tile // 2, (tile + 1) // 2, n_pair}
        row_i, coarse_i, fine_i = (down_ref[k, slots, :].astype(bf16) for k in range(3))
        blocks = []
        for src in range(n_src):
            for b in columns:
                if b not in near:
                    blocks.append(jnp.zeros((HALF, LANES), bf16))
                    continue
                cut = slice(b * LANES, (b + 1) * LANES)
                row, coarse, fine = (
                    jnp.concatenate([few_ref[src, k, :, cut]] * (HALF // 16), 0) for k in range(3)
                )
                across = (coarse_i - coarse) + (fine_i - fine)
                blocks.append(hat_bf16(row_i - row) * hat_bf16(across))
        return jnp.concatenate(blocks, 1)

    def sample():
        every = list(range(n_pair + 1))
        parts = []
        for i in range(0, n_pair + 1, 2):
            if i < n_pair:
                columns = list(range(max(i - 1, 0), min(i + 3, n_pair))) + [n_pair]
                stop = min(i + 2, n_pair)
            else:
                columns, stop = every, i + 1
            starts = range(i * LANES, stop * LANES, HALF)
            pairs = jnp.concatenate([pair_hats(start, columns) for start in starts], 0)
            values = jnp.concatenate(
                [
                    value_ref[src, :, b * LANES : (b + 1) * LANES]
                    for src in range(n_src)
                    for b in columns
                ],
                1,
            )
            got = dot_f32(values, pairs, NT)
            total = got[0:acq_loc] + got[acq_loc : 2 * acq_loc]
            below = got[2 * acq_loc : 2 * acq_loc + 8]
            parts.append(jnp.concatenate([total, below], 0))
        return jnp.concatenate(parts, 1)

    def slab(c):
        cols = []
        for src in range(n_src):
            _, _, col = tags(src, pair)
            near = jnp.clip(col - float(c + CHUNK // 2), -160.0, 160.0)
            cols.append(hat_bf16(col_at - rows_of_bf16(near, CHUNK)))
        got = dot_f32(lhs_ref[...], jnp.concatenate(cols, 1), NT)
        return jnp.concatenate(
            [
                got[0:n_img] + got[n_img : 2 * n_img],
                got[2 * n_img : 2 * n_img + ROWS_DEV] + got[2 * n_img + ROWS_DEV :],
            ],
            0,
        )

    copies = []
    for c in range(0, COLS, CHUNK):
        image = slab(c)
        lanes = slice(c, c + CHUNK)
        if not begins:
            image = image + image_in[:, lanes]
        if not ends:
            image_out[:, lanes] = image
            continue
        scale = 1.0 / jnp.maximum(image[n_img:], limit)
        for a in range(acq_loc):
            made_ref[a, :, lanes] = image[a * ROWS_DEV : (a + 1) * ROWS_DEV] * scale
        copies.append(
            pltpu.make_async_copy(
                made_ref.at[:, :, lanes], screen_ref.at[:, :, lanes], made_sem.at[c // CHUNK]
            )
        )
        copies[-1].start()
    samples = sample()
    if not begins:
        samples = samples + samples_in[...]
    if not ends:
        samples_out[...] = samples
        return
    below = samples[acq_loc : acq_loc + 1] + samples[acq_loc + 1 : acq_loc + 2]
    rest = own_ref[...] - samples[0:acq_loc] * (1.0 / jnp.maximum(below, limit))

    lower = lax.broadcasted_iota(jnp.int32, (1, LANES), 1) < HALF
    tiles = [
        mine_ref[MAX_BLOCKS + b : MAX_BLOCKS + b + 1, packed:].astype(jnp.int32) >> SLAB_SHIFT
        for b in range(n_pair + 1)
    ]
    heavy = rest[:, n_pair * LANES :]
    turned = pltpu.roll(heavy, HALF, 1)
    tile_turned = pltpu.roll(tiles[n_pair], HALF, 1)
    for t in range(n_tile):
        near = rest[:, (t // 2) * LANES : (t // 2 + 1) * LANES]
        tile_near = tiles[t // 2]
        if t % 2:
            near = pltpu.roll(near, HALF, 1)
            tile_near = pltpu.roll(tile_near, HALF, 1)
        far = jnp.where(tile_turned == t, turned, jnp.where(tiles[n_pair] == t, heavy, 0.0))
        rest_ref[:, t * LANES : (t + 1) * LANES] = jnp.where(
            lower, jnp.where(tile_near == t, near, 0.0), far
        )
    rest_copy = pltpu.make_async_copy(rest_ref, residual_ref, made_sem.at[COLS // CHUNK])
    copies.append(rest_copy)
    rest_copy.start()
    for copy in copies:
        copy.wait()


def add_sources(n_tile, sources, mine, down, sums, own):
    n_src, acq_loc, packed = sources.shape
    packed -= LANES
    width = n_src * 3 * LANES
    f32, bf16 = jnp.float32, jnp.bfloat16
    vmem = pl.BlockSpec(memory_space=pltpu.VMEM)
    n_lhs = 2 * (acq_loc + 1) * ROWS_DEV
    begins, ends = sums is None, own is not None
    args = [sources, mine, down]
    if not begins:
        args += list(sums)
    if ends:
        args.append(own)
        shapes = ((acq_loc, ROWS_DEV, COLS), (acq_loc, n_tile * LANES))
    else:
        shapes = ((n_lhs // 2, COLS), (acq_loc + 8, packed))
    macs = width * (n_lhs * COLS + (2 * acq_loc + 16) * packed)
    return pl.pallas_call(
        functools.partial(screen_kernel, n_tile, begins, ends),
        out_shape=tuple(jax.ShapeDtypeStruct(shape, f32) for shape in shapes),
        in_specs=[vmem] * len(args),
        out_specs=(pl.BlockSpec(memory_space=pl.ANY) if ends else vmem,) * 2,
        scratch_shapes=[
            pltpu.VMEM((n_src, 8, packed), f32),
            pltpu.VMEM((n_src, 3, 16, packed), bf16),
            pltpu.VMEM((n_src, 2 * acq_loc + 16, packed), bf16),
            pltpu.VMEM((n_lhs, width), bf16),
            pltpu.VMEM((acq_loc, ROWS_DEV, COLS), f32),
            pltpu.VMEM((acq_loc, n_tile * LANES), f32),
            pltpu.SemaphoreType.DMA((COLS // CHUNK + 1,)),
        ],
        input_output_aliases={} if begins or ends else {3: 0, 4: 1},
        cost_estimate=pl.CostEstimate(flops=2 * macs, bytes_accessed=1 << 20, transcendentals=0),
        compiler_params=pltpu.CompilerParams(vmem_limit_bytes=SCREEN_VMEM),
        name="add_sources",
    )(*args)


SCREEN_VMEM = 24 << 20


def xor_permute(x, axis, mask):
    count = lax.axis_size(axis)
    return lax.ppermute(x, axis, [(i, i ^ mask) for i in range(count)])


def gathered_shards(phases, coherence, pixel_index, send_list, counts, band_width):
    acq_loc = phases.shape[0]
    n_tile = lax.axis_size("tile")
    n_acq = lax.axis_size("acq")
    packed = (n_tile // 2 + 1) * LANES
    vmem = pl.BlockSpec(memory_space=pltpu.VMEM)
    f32 = jnp.float32
    outgoing, tags, own = gather_call(phases, coherence, pixel_index, send_list, counts)
    parts = [xor_permute(outgoing, "acq", k) for k in (1, 3, 2)]
    packet_shape = jax.ShapeDtypeStruct((acq_loc, packed + LANES), f32)
    begun, highpass, down = pl.pallas_call(
        functools.partial(filter_own_kernel, n_acq),
        out_shape=(
            packet_shape,
            jax.ShapeDtypeStruct((n_acq * acq_loc, acq_loc), f32),
            jax.ShapeDtypeStruct((3, packed, LANES), f32),
        ),
        in_specs=[vmem] * 3,
        out_specs=(vmem,) * 3,
        cost_estimate=pl.CostEstimate(flops=1 << 20, bytes_accessed=1 << 20, transcendentals=0),
        compiler_params=pltpu.CompilerParams(vmem_limit_bytes=4 << 20),
        name="filter_own_slots",
    )(band_width.reshape(1, -1), outgoing, tags)
    filtered = pl.pallas_call(
        filter_kernel,
        out_shape=packet_shape,
        in_specs=[vmem] * (n_acq + 1),
        out_specs=vmem,
        compiler_params=pltpu.CompilerParams(vmem_limit_bytes=4 << 20),
        name="filter_slots",
    )(highpass, begun, *parts)
    half = n_tile // 2
    across = xor_permute(filtered, "tile", half)
    sums = add_sources(n_tile, filtered[None], filtered, down, None, None)
    across, sums = lax.optimization_barrier((across, sums))
    held = jnp.stack([filtered, across])
    order = sorted(range(1, half), key=lambda k: (k < half // 2, k))
    arriving = [across[None]] + [xor_permute(held, "tile", k) for k in order]
    for sources in arriving[:-1]:
        sums = add_sources(n_tile, sources, filtered, down, sums, None)
    screen, residual = add_sources(n_tile, arriving[-1], filtered, down, sums, own)
    return residual, screen


def solution(mesh):
    n_tile = mesh.shape["tile"]
    few = n_tile in (4, 8)
    return jax.shard_map(
        gathered_shards if few else exchange_shards,
        mesh=mesh,
        in_specs=(P("acq", "tile"), P("tile"), P("tile"), P("tile", None), P("tile", None), P()),
        out_specs=(P("acq", "tile"), P("acq", "tile", None)),
        check_vma=False,
    )
```
